32 devices in a mesh: section: 2 (over core), dp: 16 (over z, y, x).
Axes of the slice: x: 2, y: 2, z: 4, core: 2. Of those that a mesh axis runs over, the one named last changes fastest.
Arguments:
- entry_pair: bfloat16 [2, 32, 256, 1024], P('section', 'dp'), may hold values from -6 to 6
- paragraph_labels: int32 [32, 256], P('dp'), may hold values from 0 to 1, never falling along the last dimension, each value on 1 to 192 neighbouring positions
- initial_norm_scaling: bfloat16 [2, 1024], P('section'), may hold values from 0.5 to 1.5
- initial_norm_offset: bfloat16 [2, 1024], P('section'), may hold values from -2 to 2
- log_fading_rates: bfloat16 [2, 1024], P('section'), may hold values from -8 to -2
- present_position_reward: bfloat16 [2, 1024], P('section'), may hold values from -1 to 1
- shift_ratio_lookup: bfloat16 [2, 1024], P('section'), may hold values from 0 to 1
- shift_ratio_content: bfloat16 [2, 1024], P('section'), may hold values from 0 to 1
- shift_ratio_accept: bfloat16 [2, 1024], P('section'), may hold values from 0 to 1
- attention_lookup_matrix: bfloat16 [2, 1024, 1024], P('section'), may hold values from -0.1875 to 0.1875
- attention_content_matrix: bfloat16 [2, 1024, 1024], P('section'), may hold values from -0.1875 to 0.1875
- attention_accept_matrix: bfloat16 [2, 1024, 1024], P('section'), may hold values from -0.1875 to 0.1875
- attention_exit_matrix: bfloat16 [2, 1024, 1024], P('section'), may hold values from -0.75 to 0.75
- latter_norm_scaling: bfloat16 [2, 1024], P('section'), may hold values from 0.5 to 1.5
- latter_norm_offset: bfloat16 [2, 1024], P('section'), may hold values from -2 to 2
- feedforward_lookup_ratio: bfloat16 [2, 1024], P('section'), may hold values from 0 to 1
- feedforward_accept_ratio: bfloat16 [2, 1024], P('section'), may hold values from 0 to 1
- feedforward_lookup_matrix: bfloat16 [2, 1024, 4096], P('section'), may hold values from -0.1875 to 0.1875
- feedforward_accept_matrix: bfloat16 [2, 1024, 1024], P('section'), may hold values from -0.1875 to 0.1875
- feedforward_content_matrix: bfloat16 [2, 4096, 1024], P('section'), may hold values from -0.09375 to 0.09375
Outputs:
- block_ends: float32 [2, 32, 256, 1024], P('section', 'dp')
- first_gain_gradient: float32 [2, 1024], P('section', 'dp')
- first_bias_gradient: float32 [2, 1024], P('section', 'dp')
- time_decay_gradient: float32 [2, 1024], P('section', 'dp')
- time_first_gradient: float32 [2, 1024], P('section', 'dp')
- blend_key_gradient: float32 [2, 1024], P('section', 'dp')
- blend_value_gradient: float32 [2, 1024], P('section', 'dp')
- blend_recept_gradient: float32 [2, 1024], P('section', 'dp')
- weight_key_gradient: float32 [2, 1024, 1024], P('section', 'dp')
- weight_value_gradient: float32 [2, 1024, 1024], P('section', 'dp')
- weight_recept_gradient: float32 [2, 1024, 1024], P('section', 'dp')
- weight_output_gradient: float32 [2, 1024, 1024], P('section', 'dp')
- second_gain_gradient: float32 [2, 1024], P('section', 'dp')
- second_bias_gradient: float32 [2, 1024], P('section', 'dp')
- channel_key_gradient: float32 [2, 1024], P('section', 'dp')
- channel_recept_gradient: float32 [2, 1024], P('section', 'dp')
- hidden_key_gradient: float32 [2, 1024, 4096], P('section', 'dp')
- hidden_recept_gradient: float32 [2, 1024, 1024], P('section', 'dp')
- hidden_value_gradient: float32 [2, 4096, 1024], P('section', 'dp')
The draws below stay inside these ranges and needn't reach their ends.
Inputs may be any that keep to these rules, and one draw needn't show every extreme that they name: `paragraph_labels`: in every row the document number is 0 up to some token and 1 from there on, so a row holds two documents, each of 64 to 192 tokens.
All inputs are finite; a program needn't handle non-finite values.
Results may differ from the reference program's by a relative error of at most 0.015.
Values may be sent and summed in bfloat16 or wider, within the bound.
No kernel may reach another device: no remote copies, remote signals or barrier semaphores. Data moves between devices by JAX's collectives and lax.ppermute only.
A program may use at most 256 MiB of HBM per device.

```python
import math
import jax
import jax.numpy as jnp
import numpy as np
from jax import lax

EMBED_WIDTH = 1024
FF = 4096
MB_TOK = 256
BLOCK = 16
DEPTH_COUNT = 2
ROWS = 32
MOST = 192


def steps_of(stream_key, dims, shards, smallest, top_value):
    factor_of = 1.0
    for dim, parts in shards:
        heights = jax.random.uniform(jax.random.fold_in(jax.random.fold_in(stream_key, 6), dim), (parts,), jnp.float32, smallest / len(shards), top_value / len(shards))
        factor_of = factor_of * jnp.repeat(jnp.exp(heights), dims[dim] // parts).reshape((-1,) + (1,) * (len(dims) - 1 - dim))
    return factor_of


def length_profile(amount, total, reach, skew):
    portions = [(1 << 20) // math.isqrt(grade ** skew) + 1 for grade in range(2, amount + 1)]
    rest, given = total - reach - (amount - 1), [1] * (amount - 1)
    while rest > 0:
        free = [i for i in range(amount - 1) if given[i] < reach]
        whole, remaining = sum([portions[i] for i in free]), rest
        for i in free:
            more = min(reach - given[i], max(1, remaining * portions[i] // whole), rest)
            given[i] = given[i] + more
            rest = rest - more
    return np.array([reach] + given)


def uneven_parts(own_key, number_of, total, reach, slope):
    if number_of == 2:
        one = jax.random.randint(own_key, (), max(1, total - reach), min(reach, total - 1) + 1)
        return jnp.stack([one, total - one])
    sizes = jnp.asarray(length_profile(number_of, total, reach, slope), jnp.int32)
    couples = (number_of - 1) // 2
    giver, receiver = sizes[1:1 + 2 * couples:2], sizes[2:2 + 2 * couples:2]
    margin = jnp.minimum(giver - 1, reach - receiver)
    moved = jax.random.randint(jax.random.fold_in(own_key, 1), (couples,), 0, 1 << 20) % (margin + 1)
    sizes = sizes.at[1:1 + 2 * couples:2].set(giver - moved).at[2:2 + 2 * couples:2].set(receiver + moved)
    return sizes[jax.random.permutation(jax.random.fold_in(own_key, 2), number_of)]


def centred(stream_key, dims, scale, reach, cuts=(), kind=jnp.bfloat16):
    gain = steps_of(stream_key, dims, cuts, -0.22, 0.18) if cuts else 1.0
    drawn = jax.random.normal(stream_key, dims, jnp.float32) * scale * gain
    return jnp.minimum(jnp.maximum(drawn, -reach), reach).astype(kind)


def setup_inputs(seed: int = 0) -> dict:
    key_of = jax.random.split(jax.random.key(seed), 21)
    entry_pair = centred(key_of[0], (2, ROWS, MB_TOK, EMBED_WIDTH), 1.0, 6.0, ((0, 2), (1, 16)))
    paragraph_labels = jax.vmap(lambda own: jnp.searchsorted(jnp.cumsum(uneven_parts(own, 2, MB_TOK, MOST, 0)), jnp.arange(MB_TOK), side="right"))(jax.random.split(key_of[1], ROWS)).reshape((ROWS, MB_TOK)).astype(jnp.int32)
    initial_norm_scaling = jnp.clip(1.0 + 0.1 * jax.random.normal(key_of[2], (DEPTH_COUNT, EMBED_WIDTH), jnp.float32), 0.5, 1.5).astype(jnp.bfloat16)
    initial_norm_offset = centred(key_of[3], (DEPTH_COUNT, EMBED_WIDTH), 0.3, 2.0, ((0, 2),))
    log_fading_rates = jnp.clip(-8.0 + 6.0 * jax.random.uniform(key_of[4], (DEPTH_COUNT, EMBED_WIDTH), jnp.float32) ** steps_of(key_of[4], (DEPTH_COUNT, EMBED_WIDTH), ((0, 2),), -0.2, 0.2), -8.0, -2.0).astype(jnp.bfloat16)
    present_position_reward = jnp.clip(jax.random.uniform(key_of[5], (DEPTH_COUNT, EMBED_WIDTH), jnp.float32, -1.0, 1.0) * steps_of(key_of[5], (DEPTH_COUNT, EMBED_WIDTH), ((0, 2),), -0.4, 0.0), -1.0, 1.0).astype(jnp.bfloat16)
    shift_ratio_lookup = jnp.clip(1.0 * jax.random.uniform(key_of[6], (DEPTH_COUNT, EMBED_WIDTH), jnp.float32) ** steps_of(key_of[6], (DEPTH_COUNT, EMBED_WIDTH), ((0, 2),), -0.2, 0.2), 0.0, 1.0).astype(jnp.bfloat16)
    shift_ratio_content = jnp.clip(1.0 * jax.random.uniform(key_of[7], (DEPTH_COUNT, EMBED_WIDTH), jnp.float32) ** steps_of(key_of[7], (DEPTH_COUNT, EMBED_WIDTH), ((0, 2),), -0.2, 0.2), 0.0, 1.0).astype(jnp.bfloat16)
    shift_ratio_accept = jnp.clip(1.0 * jax.random.uniform(key_of[8], (DEPTH_COUNT, EMBED_WIDTH), jnp.float32) ** steps_of(key_of[8], (DEPTH_COUNT, EMBED_WIDTH), ((0, 2),), -0.2, 0.2), 0.0, 1.0).astype(jnp.bfloat16)
    attention_lookup_matrix = centred(key_of[9], (DEPTH_COUNT, EMBED_WIDTH, EMBED_WIDTH), EMBED_WIDTH ** -0.5, 0.1875, ((0, 2),))
    attention_content_matrix = centred(key_of[10], (DEPTH_COUNT, EMBED_WIDTH, EMBED_WIDTH), EMBED_WIDTH ** -0.5, 0.1875, ((0, 2),))
    attention_accept_matrix = centred(key_of[11], (DEPTH_COUNT, EMBED_WIDTH, EMBED_WIDTH), EMBED_WIDTH ** -0.5, 0.1875, ((0, 2),))
    attention_exit_matrix = centred(key_of[12], (DEPTH_COUNT, EMBED_WIDTH, EMBED_WIDTH), (EMBED_WIDTH // 16) ** -0.5, 0.75, ((0, 2),))
    latter_norm_scaling = jnp.clip(1.0 + 0.1 * jax.random.normal(key_of[13], (DEPTH_COUNT, EMBED_WIDTH), jnp.float32), 0.5, 1.5).astype(jnp.bfloat16)
    latter_norm_offset = centred(key_of[14], (DEPTH_COUNT, EMBED_WIDTH), 0.3, 2.0, ((0, 2),))
    feedforward_lookup_ratio = jnp.clip(1.0 * jax.random.uniform(key_of[15], (DEPTH_COUNT, EMBED_WIDTH), jnp.float32) ** steps_of(key_of[15], (DEPTH_COUNT, EMBED_WIDTH), ((0, 2),), -0.2, 0.2), 0.0, 1.0).astype(jnp.bfloat16)
    feedforward_accept_ratio = jnp.clip(1.0 * jax.random.uniform(key_of[16], (DEPTH_COUNT, EMBED_WIDTH), jnp.float32) ** steps_of(key_of[16], (DEPTH_COUNT, EMBED_WIDTH), ((0, 2),), -0.2, 0.2), 0.0, 1.0).astype(jnp.bfloat16)
    feedforward_lookup_matrix = centred(key_of[17], (DEPTH_COUNT, EMBED_WIDTH, FF), EMBED_WIDTH ** -0.5, 0.1875, ((0, 2),))
    feedforward_accept_matrix = centred(key_of[18], (DEPTH_COUNT, EMBED_WIDTH, EMBED_WIDTH), EMBED_WIDTH ** -0.5, 0.1875, ((0, 2),))
    feedforward_content_matrix = centred(key_of[19], (DEPTH_COUNT, FF, EMBED_WIDTH), FF ** -0.5, 0.09375, ((0, 2),))
    return dict(entry_pair=entry_pair, paragraph_labels=paragraph_labels, initial_norm_scaling=initial_norm_scaling, initial_norm_offset=initial_norm_offset, log_fading_rates=log_fading_rates, present_position_reward=present_position_reward, shift_ratio_lookup=shift_ratio_lookup, shift_ratio_content=shift_ratio_content, shift_ratio_accept=shift_ratio_accept, attention_lookup_matrix=attention_lookup_matrix, attention_content_matrix=attention_content_matrix, attention_accept_matrix=attention_accept_matrix, attention_exit_matrix=attention_exit_matrix, latter_norm_scaling=latter_norm_scaling, latter_norm_offset=latter_norm_offset, feedforward_lookup_ratio=feedforward_lookup_ratio, feedforward_accept_ratio=feedforward_accept_ratio, feedforward_lookup_matrix=feedforward_lookup_matrix, feedforward_accept_matrix=feedforward_accept_matrix, feedforward_content_matrix=feedforward_content_matrix)


@jax.custom_vjp
def lesser_precision(v):
    return lax.optimization_barrier(v.astype(jnp.bfloat16)).astype(jnp.float32)

@jax.custom_vjp
def low_back(v):
    return v

def low_keep(v):
    return (lesser_precision(v), None)

def low_pass(kept, grad):
    return (grad,)

def back_keep(v):
    return (v, None)

def back_low(kept, grad):
    return (lesser_precision(grad),)
lesser_precision.defvjp(low_keep, low_pass)
low_back.defvjp(back_keep, back_low)

def matmul_high(left, right):
    return jnp.dot(left, right, precision=lax.Precision.HIGHEST, preferred_element_type=jnp.float32)

def norm_rows(values, norm_gain, norm_bias):
    average = lax.optimization_barrier(jnp.mean(values, axis=-1, keepdims=True))
    centered = values - average
    variance = lax.optimization_barrier(jnp.mean(centered * centered, axis=-1, keepdims=True))
    return centered * lax.rsqrt(variance + 1e-05) * norm_gain + norm_bias

def previous(values, concatenated_texts):
    before = jnp.concatenate([jnp.zeros_like(values[:1]), values[:-1]], axis=0)
    joined = jnp.concatenate([jnp.zeros((1,), jnp.bool_), concatenated_texts[1:] == concatenated_texts[:-1]])
    return jnp.where(joined[:, None], before, jnp.zeros_like(before))

def blend(normed, shifted_in, factor):
    return normed * factor + shifted_in * (1.0 - factor)

def scaled_lookups(lookup_projected, content_projected, log_fading_rates, present_position_reward, concatenated_texts):
    decay_rate = jnp.exp(log_fading_rates)
    offsets = jnp.arange(BLOCK, dtype=jnp.float32)
    distance = offsets[:, None] - offsets[None, :] - 1.0
    causal = distance >= 0

    def mix_block(carry, piece):
        dividend_memory, divisor_memory, last_doc = carry
        lookup_block_piece, content_block_piece, doc_block = piece
        visible = (doc_block[:, None] == doc_block[None, :]) & causal
        exponent = -distance[:, :, None] * decay_rate + lookup_block_piece[None, :, :]
        linear_attention_routine = jnp.where(visible[:, :, None], jnp.exp(exponent), 0.0)
        running_memory = jnp.where((doc_block == last_doc)[:, None], jnp.exp(-offsets[:, None] * decay_rate), 0.0)
        extra_reward_increment = jnp.exp(present_position_reward + lookup_block_piece)
        dividend_total = running_memory * dividend_memory + lax.optimization_barrier(jnp.sum(linear_attention_routine * content_block_piece[None, :, :], axis=1)) + extra_reward_increment * content_block_piece
        divisor_total = running_memory * divisor_memory + lax.optimization_barrier(jnp.sum(linear_attention_routine, axis=1)) + extra_reward_increment
        tail_doc = doc_block[BLOCK - 1]
        tail_kernel = jnp.where((doc_block == tail_doc)[:, None], jnp.exp(-(BLOCK - 1.0 - offsets)[:, None] * decay_rate + lookup_block_piece), 0.0)
        keep_old = jnp.where(tail_doc == last_doc, jnp.exp(-BLOCK * decay_rate), 0.0)
        top_next = keep_old * dividend_memory + lax.optimization_barrier(jnp.sum(tail_kernel * content_block_piece, axis=0))
        bottom_next = keep_old * divisor_memory + lax.optimization_barrier(jnp.sum(tail_kernel, axis=0))
        return ((top_next, bottom_next, tail_doc), dividend_total / divisor_total)
    width = lookup_projected.shape[1]
    blocks = lookup_projected.shape[0] // BLOCK
    start = (jnp.zeros((width,), lookup_projected.dtype), jnp.zeros((width,), lookup_projected.dtype), jnp.array(-1, jnp.int32))
    pieces = (lookup_projected.reshape(blocks, BLOCK, width), content_projected.reshape(blocks, BLOCK, width), concatenated_texts.reshape(blocks, BLOCK).astype(jnp.int32))
    _, outputs = lax.scan(jax.checkpoint(mix_block), start, pieces)
    return outputs.reshape(lookup_projected.shape)

def layer_forward(state, concatenated_texts, learned_parameters):
    initial_norm_scaling, initial_norm_offset, log_fading_rates, present_position_reward, shift_ratio_lookup, shift_ratio_content, shift_ratio_accept, attention_lookup_matrix, attention_content_matrix, attention_accept_matrix, attention_exit_matrix, latter_norm_scaling, latter_norm_offset, feedforward_lookup_ratio, feedforward_accept_ratio, feedforward_lookup_matrix, feedforward_accept_matrix, feedforward_content_matrix = learned_parameters
    normed = norm_rows(state, initial_norm_scaling, initial_norm_offset)
    shifted_in = previous(normed, concatenated_texts)
    key_in = lesser_precision(blend(normed, shifted_in, shift_ratio_lookup))
    value_in = lesser_precision(blend(normed, shifted_in, shift_ratio_content))
    recept_in = lesser_precision(blend(normed, shifted_in, shift_ratio_accept))
    lookup_projected = low_back(matmul_high(key_in, attention_lookup_matrix))
    content_projected = low_back(matmul_high(value_in, attention_content_matrix))
    accept_logits = low_back(matmul_high(recept_in, attention_accept_matrix))
    combined_input = lesser_precision(jax.nn.sigmoid(accept_logits) * scaled_lookups(lookup_projected, content_projected, log_fading_rates, present_position_reward, concatenated_texts))
    middle = state + low_back(matmul_high(combined_input, attention_exit_matrix))
    second_normed = norm_rows(middle, latter_norm_scaling, latter_norm_offset)
    second_shifted = previous(second_normed, concatenated_texts)
    hidden_in = lesser_precision(blend(second_normed, second_shifted, feedforward_lookup_ratio))
    gate_in = lesser_precision(blend(second_normed, second_shifted, feedforward_accept_ratio))
    hidden_pre = low_back(matmul_high(hidden_in, feedforward_lookup_matrix))
    hidden_act = lesser_precision(jnp.square(jax.nn.relu(hidden_pre)))
    hidden_out = low_back(matmul_high(hidden_act, feedforward_content_matrix))
    gate_pre = low_back(matmul_high(gate_in, feedforward_accept_matrix))
    return middle + jax.nn.sigmoid(gate_pre) * hidden_out

def reference(entry_pair, paragraph_labels, initial_norm_scaling, initial_norm_offset, log_fading_rates, present_position_reward, shift_ratio_lookup, shift_ratio_content, shift_ratio_accept, attention_lookup_matrix, attention_content_matrix, attention_accept_matrix, attention_exit_matrix, latter_norm_scaling, latter_norm_offset, feedforward_lookup_ratio, feedforward_accept_ratio, feedforward_lookup_matrix, feedforward_accept_matrix, feedforward_content_matrix):
    learned_parameters = tuple((element_entry.astype(jnp.float32) for element_entry in (initial_norm_scaling, initial_norm_offset, log_fading_rates, present_position_reward, shift_ratio_lookup, shift_ratio_content, shift_ratio_accept, attention_lookup_matrix, attention_content_matrix, attention_accept_matrix, attention_exit_matrix, latter_norm_scaling, latter_norm_offset, feedforward_lookup_ratio, feedforward_accept_ratio, feedforward_lookup_matrix, feedforward_accept_matrix, feedforward_content_matrix)))

    def stacked(block_input, weights_all, concatenated_texts):
        state = block_input
        for layer_index in range(DEPTH_COUNT):
            layer_params = tuple((element_entry[layer_index] for element_entry in weights_all))
            state = layer_forward(state, concatenated_texts, layer_params)
            if layer_index + 1 < DEPTH_COUNT:
                state = low_back(lesser_precision(state))
        return lesser_precision(state)

    def row_gradients(totals, row):
        block_input, cotangent, concatenated_texts = row
        result, pullback = jax.vjp(lambda inputs, weights_all: stacked(inputs, weights_all, concatenated_texts), block_input.astype(jnp.float32), learned_parameters)
        input_gradient, weight_gradients = pullback(cotangent.astype(jnp.float32))
        totals = jax.tree.map(lambda left, right: left + right, totals, weight_gradients)
        return (totals, (input_gradient, result))
    zeros = jax.tree.map(jnp.zeros_like, learned_parameters)
    totals, (input_gradients, results) = lax.scan(row_gradients, zeros, (entry_pair[0], entry_pair[1], paragraph_labels))
    block_ends = jnp.stack([input_gradients, results], axis=0)
    return (block_ends,) + tuple(totals)
```

```python
import functools

import jax
import jax.numpy as jnp
from jax import lax
from jax.experimental import pallas as pl
from jax.experimental.pallas import tpu as pltpu
from jax.sharding import PartitionSpec as P

BF = jnp.bfloat16
F32 = jnp.float32
LANES = 128


def to_steps(scratch, row, values):
    tokens, width = values.shape
    parts = width // LANES
    for c in range(parts):
        scratch[row, pl.ds(c, tokens, stride=parts), :] = values[:, c * LANES:(c + 1) * LANES]


def column(scratch, row, c, tokens, parts):
    return scratch[row, pl.ds(c, tokens, stride=parts), :]


def recur_forward_kernel(same, fade, bonus, key, value, accept, out, ks, vs):
    rows, tokens, width = key.shape
    parts = width // LANES
    for row in range(rows):
        to_steps(ks, row, key[row])
        to_steps(vs, row, value[row])
    decay = jnp.exp(-jnp.exp(fade[...]))
    extra = bonus[...]

    def step(t, carry):
        at = pl.multiple_of(t * parts, parts)
        following = []
        for row in range(rows):
            top, bottom = carry[2 * row], carry[2 * row + 1]
            m = same[row, t]
            top, bottom = top * m, bottom * m
            k = ks[row, pl.ds(at, parts), :]
            v = vs[row, pl.ds(at, parts), :]
            ek = jnp.exp(k)
            now = jnp.exp(extra + k)
            vs[row, pl.ds(at, parts), :] = (top + now * v) / (bottom + now)
            following += [decay * top + ek * v, decay * bottom + ek]
        return tuple(following)

    zero = jnp.zeros(decay.shape, F32)
    lax.fori_loop(0, tokens, step, (zero,) * (2 * rows), unroll=4)
    for row in range(rows):
        for c in range(parts):
            cols = slice(c * LANES, (c + 1) * LANES)
            y = column(vs, row, c, tokens, parts)
            out[row, :, cols] = (jax.nn.sigmoid(accept[row, :, cols]) * y).astype(BF)


def recur_backward_kernel(same, fade, bonus, key, value, accept, delta, dkey, dvalue, daccept, dfade, dbonus, ks, vs, gs, ys, tops, bottoms):
    rows, tokens, width = key.shape
    parts = width // LANES
    for row in range(rows):
        to_steps(ks, row, key[row])
        to_steps(vs, row, value[row])
        to_steps(gs, row, delta[row] * jax.nn.sigmoid(accept[row]))
    rate = jnp.exp(fade[...])
    decay = jnp.exp(-rate)
    extra = bonus[...]

    def step(t, carry):
        at = pl.multiple_of(t * parts, parts)
        here = pl.ds(at, parts)
        following = []
        for row in range(rows):
            top, bottom = carry[2 * row], carry[2 * row + 1]
            m = same[row, t]
            top, bottom = top * m, bottom * m
            tops[row, here, :] = top
            bottoms[row, here, :] = bottom
            k = ks[row, here, :]
            v = vs[row, here, :]
            ek = jnp.exp(k)
            now = jnp.exp(extra + k)
            inverse = 1.0 / (bottom + now)
            ys[row, here, :] = (top + now * v) * inverse
            gs[row, here, :] = gs[row, here, :] * inverse
            following += [decay * top + ek * v, decay * bottom + ek]
        return tuple(following)

    zero = jnp.zeros(decay.shape, F32)
    lax.fori_loop(0, tokens, step, (zero,) * (2 * rows), unroll=4)

    def back(i, carry):
        t = tokens - 1 - i
        at = pl.multiple_of(t * parts, parts)
        here = pl.ds(at, parts)
        dw, du = carry[:2]
        following = []
        for row in range(rows):
            a, b = carry[2 + 2 * row], carry[3 + 2 * row]
            k = ks[row, here, :]
            v = vs[row, here, :]
            ek = jnp.exp(k)
            now = jnp.exp(extra + k)
            ga = gs[row, here, :]
            gb = -ga * ys[row, here, :]
            q = now * (v * ga + gb)
            ks[row, here, :] = ek * (v * a + b) + q
            vs[row, here, :] = ek * a + now * ga
            du = du + q
            dw = dw + (a * tops[row, here, :] + b * bottoms[row, here, :])
            m = same[row, t]
            following += [(ga + decay * a) * m, (gb + decay * b) * m]
        return (dw, du, *following)

    done = lax.fori_loop(0, tokens, back, (zero,) * (2 + 2 * rows), unroll=4)
    dfade[...] = -done[0] * decay * rate
    dbonus[...] = done[1]
    for row in range(rows):
        for c in range(parts):
            cols = slice(c * LANES, (c + 1) * LANES)
            dkey[row, :, cols] = column(ks, row, c, tokens, parts).astype(BF)
            dvalue[row, :, cols] = column(vs, row, c, tokens, parts).astype(BF)
            gate = jax.nn.sigmoid(accept[row, :, cols])
            y = column(ys, row, c, tokens, parts)
            daccept[row, :, cols] = (delta[row, :, cols] * y * gate * (1.0 - gate)).astype(BF)


def slabs(vector):
    return vector.reshape(vector.shape[0] // LANES, LANES)


def recur_forward(same, fade, bonus, key, value, accept):
    rows, tokens, width = key.shape
    vm = pl.BlockSpec(memory_space=pltpu.VMEM)
    scratch = pltpu.VMEM((rows, tokens * width // LANES, LANES), F32)
    return pl.pallas_call(
        recur_forward_kernel,
        out_shape=jax.ShapeDtypeStruct(key.shape, BF),
        in_specs=[pl.BlockSpec(memory_space=pltpu.SMEM)] + [vm] * 5,
        out_specs=vm,
        scratch_shapes=[scratch] * 2,
        compiler_params=pltpu.CompilerParams(vmem_limit_bytes=40 << 20),
        name="recur_forward",
    )(same, slabs(fade), slabs(bonus), key, value, accept)


def recur_backward(same, fade, bonus, key, value, accept, delta):
    rows, tokens, width = key.shape
    vm = pl.BlockSpec(memory_space=pltpu.VMEM)
    scratch = pltpu.VMEM((rows, tokens * width // LANES, LANES), F32)
    wide = jax.ShapeDtypeStruct(key.shape, BF)
    thin = jax.ShapeDtypeStruct((width // LANES, LANES), F32)
    dkey, dvalue, daccept, dfade, dbonus = pl.pallas_call(
        recur_backward_kernel,
        out_shape=(wide, wide, wide, thin, thin),
        in_specs=[pl.BlockSpec(memory_space=pltpu.SMEM)] + [vm] * 6,
        out_specs=(vm,) * 5,
        scratch_shapes=[scratch] * 6,
        compiler_params=pltpu.CompilerParams(vmem_limit_bytes=48 << 20),
        name="recur_backward",
    )(same, slabs(fade), slabs(bonus), key, value, accept, delta)
    return dkey, dvalue, daccept, dfade.reshape(width), dbonus.reshape(width)


def norm_rows(values, gain, bias):
    centered = values - jnp.mean(values, axis=-1, keepdims=True)
    variance = jnp.mean(centered * centered, axis=-1, keepdims=True)
    return centered * lax.rsqrt(variance + 1e-05) * gain + bias


def previous(values, same):
    before = jnp.concatenate([jnp.zeros_like(values[:, :1]), values[:, :-1]], axis=1)
    return before * same[:, :, None]


def blend(normed, shifted, factor):
    return normed * factor + shifted * (1.0 - factor)


def mixes(values, gain, bias, factors, same):
    normed = norm_rows(values, gain, bias)
    shifted = previous(normed, same)
    return tuple(blend(normed, shifted, f) for f in factors)


def product(left, right):
    return lax.dot_general(left, right, (((2,), (0,)), ((), ())), preferred_element_type=F32)


def back_product(deltas, right):
    return lax.dot_general(deltas, right, (((2,), (1,)), ((), ())), preferred_element_type=F32)


def outer_product(left, right):
    return lax.dot_general(left, right, (((0, 1), (0, 1)), ((), ())), preferred_element_type=F32).astype(BF)


def forward_layer(block_in, same, p):
    (g1, b1, fade, bonus, mk, mv, mr, wk, wv, wr, wo, g2, b2, ck, cr, fk, fr, fv) = p
    state = block_in.astype(F32)
    key_in, value_in, recept_in = (z.astype(BF) for z in mixes(state, g1, b1, (mk, mv, mr), same))
    key = product(key_in, wk)
    value = product(value_in, wv)
    accept = product(recept_in, wr)
    mixed = recur_forward(same, fade, bonus, key, value, accept)
    middle = state + product(mixed, wo)
    hidden_in, gate_in = (z.astype(BF) for z in mixes(middle, g2, b2, (ck, cr), same))
    hidden_pre = product(hidden_in, fk)
    hidden_act = jnp.square(jnp.maximum(hidden_pre, 0.0)).astype(BF)
    hidden_out = product(hidden_act, fv)
    gate_pre = product(gate_in, fr)
    result = (middle + jax.nn.sigmoid(gate_pre) * hidden_out).astype(BF)
    kept = (block_in, key_in, value_in, recept_in, key, value, accept, mixed, middle, hidden_in, gate_in, hidden_pre, hidden_out, gate_pre)
    return result, kept


def backward_layer(incoming, same, p, kept):
    (g1, b1, fade, bonus, mk, mv, mr, wk, wv, wr, wo, g2, b2, ck, cr, fk, fr, fv) = p
    (block_in, key_in, value_in, recept_in, key, value, accept, mixed, middle, hidden_in, gate_in, hidden_pre, hidden_out, gate_pre) = kept
    g = incoming.astype(F32)
    gate = jax.nn.sigmoid(gate_pre)
    delta_out = (g * gate).astype(BF)
    delta_gate = (g * hidden_out * gate * (1.0 - gate)).astype(BF)
    rectified = jnp.maximum(hidden_pre, 0.0)
    hidden_act = jnp.square(rectified).astype(BF)
    delta_pre = (back_product(delta_out, fv) * 2.0 * rectified).astype(BF)
    _, pull = jax.vjp(lambda z, a, b, c, d: mixes(z, a, b, (c, d), same), middle, g2, b2, ck, cr)
    middle_back, dg2, db2, dck, dcr = pull((back_product(delta_pre, fk), back_product(delta_gate, fr)))
    middle_delta = g + middle_back
    delta_branch = middle_delta.astype(BF)
    delta_mixed = back_product(delta_branch, wo)
    delta_key, delta_value, delta_accept, dfade, dbonus = recur_backward(same, fade, bonus, key, value, accept, delta_mixed)
    _, pull = jax.vjp(lambda z, a, b, c, d, e: mixes(z, a, b, (c, d, e), same), block_in.astype(F32), g1, b1, mk, mv, mr)
    state_back, dg1, db1, dmk, dmv, dmr = pull(
        (back_product(delta_key, wk), back_product(delta_value, wv), back_product(delta_accept, wr))
    )
    state_delta = middle_delta + state_back
    vectors = jnp.stack([dg1, db1, dfade, dbonus, dmk, dmv, dmr, dg2, db2, dck, dcr])

    def halves(left, right):
        cut = right.shape[-1] // 2
        return outer_product(left, right[..., :cut]), outer_product(left, right[..., cut:])

    grads = (
        halves(key_in, delta_key),
        halves(value_in, delta_value),
        halves(recept_in, delta_accept),
        halves(mixed, delta_branch),
        halves(hidden_in, delta_pre),
        halves(gate_in, delta_gate),
        halves(hidden_act, delta_out),
    )
    return state_delta, vectors, grads


def halving(blocks, order):
    count = lax.axis_size("dp")
    me = lax.axis_index("dp")
    bits = count.bit_length() - 1
    dims = list(range(bits - 1, -1, -1))
    current = blocks.reshape((2,) * bits + blocks.shape[1:])
    for at, bit in enumerate(order):
        axis = dims.index(bit)
        dims.pop(axis)
        mine = (me >> bit) & 1
        send = lax.dynamic_index_in_dim(current, 1 - mine, axis, keepdims=False)
        keep = lax.dynamic_index_in_dim(current, mine, axis, keepdims=False)
        got = lax.ppermute(send, "dp", [(i, i ^ (1 << bit)) for i in range(count)])
        current = keep.astype(F32) + got.astype(F32)
        if at + 1 < bits:
            current = current.astype(blocks.dtype)
    return current


def local(entry_pair, labels, *params):
    count = lax.axis_size("dp")
    section = lax.axis_index("section")
    own = entry_pair[0]
    p = tuple(e[0].astype(F32) if e.ndim == 2 else e[0] for e in params)
    first = jnp.zeros((labels.shape[0], 1), F32)
    same = jnp.concatenate([first, (labels[:, 1:] == labels[:, :-1]).astype(F32)], axis=1)

    shapes = jax.eval_shape(lambda x: forward_layer(x, same, p), own)
    empty = lambda: jax.tree.map(lambda s: jnp.zeros(s.shape, s.dtype), shapes)
    result, kept = lax.cond(section == 0, lambda: forward_layer(own, same, p), empty)
    received = lax.ppermute(result, "section", [(0, 1)])
    result, kept = lax.cond(section == 1, lambda: forward_layer(received, same, p), lambda: (result, kept))

    back_shapes = jax.eval_shape(lambda g: backward_layer(g, same, p, kept), own)
    empty_back = lambda: jax.tree.map(lambda s: jnp.zeros(s.shape, s.dtype), back_shapes)
    back = lax.cond(section == 1, lambda: backward_layer(own, same, p, kept), empty_back)
    received = lax.ppermute(back[0].astype(BF), "section", [(1, 0)])
    state_delta, vectors, grads = lax.cond(section == 0, lambda: backward_layer(received, same, p, kept), lambda: back)
    block_ends = jnp.where(section == 0, state_delta, result.astype(F32))

    bits = count.bit_length() - 1
    plain = tuple(range(bits))
    turned = (1, 0) + tuple(range(2, bits)) if bits > 1 else plain
    width = vectors.shape[1]
    blocks = vectors.reshape(vectors.shape[0], count, width // count).transpose(1, 0, 2)
    sums = halving(blocks, plain)
    outs = []
    for low, high in grads:
        halves = []
        for piece, order in ((low, plain), (high, turned)):
            halves.append(halving(piece.reshape(count, piece.shape[0] // count, piece.shape[1]), order))
        outs.append(jnp.concatenate(halves, axis=-1))
    gk, gv, gr, go, gfk, gfr, gfv = outs
    v = [sums[i] for i in range(sums.shape[0])]
    everything = (block_ends, *v[:7], gk, gv, gr, go, *v[7:], gfk, gfr, gfv)
    return tuple(e[None] for e in everything)


def solution(mesh):
    vec, mat = P("section", None), P("section", None, None)
    in_specs = (P("section", "dp", None, None), P("dp", None)) + (vec,) * 7 + (mat,) * 4 + (vec,) * 4 + (mat,) * 3
    vec, mat = P("section", "dp"), P("section", "dp", None)
    out_specs = (P("section", "dp", None, None),) + (vec,) * 7 + (mat,) * 4 + (vec,) * 4 + (mat,) * 3
    return jax.shard_map(local, mesh=mesh, in_specs=in_specs, out_specs=out_specs, check_vma=False)
```

```python
import functools

import jax
import jax.numpy as jnp
from jax import lax
from jax.experimental import pallas as pl
from jax.experimental.pallas import tpu as pltpu
from jax.sharding import PartitionSpec as P

BF = jnp.bfloat16
F32 = jnp.float32
LANES = 128
VM = pl.BlockSpec(memory_space=pltpu.VMEM)
HBM = pl.BlockSpec(memory_space=pl.ANY)
SM = pl.BlockSpec(memory_space=pltpu.SMEM)

def dot(left, right):
    return jnp.dot(left, right, preferred_element_type=F32)

def dot_nt(left, right):
    return lax.dot_general(left, right, (((1,), (1,)), ((), ())), preferred_element_type=F32)

def lanes(c):
    return pl.ds(pl.multiple_of(c * LANES, LANES), LANES)

def statistics(source, mean, scale, tokens, width, chunk=64):
    def step(i, _):
        at = pl.ds(pl.multiple_of(i * chunk, chunk), chunk)
        x = source[at, :].astype(F32)
        m = jnp.sum(x, axis=1, keepdims=True) * (1.0 / width)
        x = x - m
        v = jnp.sum(x * x, axis=1, keepdims=True) * (1.0 / width)
        mean[at, :] = jnp.broadcast_to(m, (chunk, LANES))
        scale[at, :] = jnp.broadcast_to(lax.rsqrt(v + 1e-05), (chunk, LANES))
        return 0
    lax.fori_loop(0, tokens // chunk, step, 0)

def mix_into(source, mean, scale, same, gain, bias, factors, targets, width):
    def step(c, _):
        cols = lanes(c)
        z = (source[:, cols].astype(F32) - mean[...]) * scale[...] * gain[:, cols].astype(F32) + bias[:, cols].astype(F32)
        before = pltpu.roll(z, 1, 0) * same[...]
        step_up = z - before
        for factor, target in zip(factors, targets):
            target[:, cols] = (before + step_up * factor[:, cols].astype(F32)).astype(BF)
        return 0
    lax.fori_loop(0, width // LANES, step, 0)

def fetch(pairs, sems):
    copies = [pltpu.make_async_copy(s, d, sems.at[i]) for i, (s, d) in enumerate(pairs)]
    for c in copies:
        c.start()
    return copies

def forward_kernel(rows, with_delta, *refs):
    (same_s, same, h, g1, b1, fade, bonus, mk, mv, mr, g2, b2, ck, cr, cot) = refs[:15]
    weights = refs[15:22]
    n_out = 15
    outs = refs[22:22 + n_out]
    (wk, wv, wr, wo, fk, fr, fv, mean, scale, key_in, value_in, recept_in, ks, vs, ys, gate, mixed, middle,
     hidden_in, gate_in, rect, act, delta_out, delta_gate, result, in_sems, out_sems) = refs[22 + n_out:]
    tokens, width = h.shape
    each = tokens // rows
    parts = width // LANES
    tile = 512
    ff = rect.shape[1]
    loads = fetch(list(zip(weights, (wk, wv, wr, wo, fk, fr, fv))), in_sems)
    saves = []

    def save(source):
        i = len(saves)
        saves.append(pltpu.make_async_copy(source, outs[i], out_sems.at[i]))
        saves[-1].start()

    statistics(h, mean, scale, tokens, width)
    mix_into(h, mean, scale, same, g1, b1, (mk, mv, mr), (key_in, value_in, recept_in), width)
    for z in (key_in, value_in, recept_in):
        save(z)

    def cols_of(j):
        return pl.ds(pl.multiple_of(j * tile, tile), tile)

    def steps_tile(values, target, j):
        for row in range(rows):
            for c in range(tile // LANES):
                target[pl.ds(row * each * parts + j * (tile // LANES) + c, each, stride=parts), :] = values[row * each:(row + 1) * each, c * LANES:(c + 1) * LANES]

    loads[0].wait()
    def key_tile(j, _):
        steps_tile(dot(key_in[...], wk[:, cols_of(j)]), ks, j)
        return 0
    lax.fori_loop(0, width // tile, key_tile, 0)
    loads[1].wait()
    def value_tile(j, _):
        steps_tile(dot(value_in[...], wv[:, cols_of(j)]), vs, j)
        return 0
    lax.fori_loop(0, width // tile, value_tile, 0)
    save(ks)
    save(vs)
    loads[2].wait()
    def accept_tile(j, _):
        gate[:, cols_of(j)] = jax.nn.sigmoid(dot(recept_in[...], wr[:, cols_of(j)]))
        return 0
    lax.fori_loop(0, width // tile, accept_tile, 0)
    save(gate)

    decay = jnp.exp(-jnp.exp(fade[...]))
    extra = bonus[...]
    def step(t, carry):
        following = []
        for row in range(rows):
            here = pl.ds(pl.multiple_of((row * each + t) * parts, parts), parts)
            m = same_s[row, t]
            top, bottom = carry[2 * row] * m, carry[2 * row + 1] * m
            k, v = ks[here, :], vs[here, :]
            ek, now = jnp.exp(k), jnp.exp(extra + k)
            ys[here, :] = (top + now * v) / (bottom + now)
            following += [decay * top + ek * v, decay * bottom + ek]
        return tuple(following)
    zero = jnp.zeros(decay.shape, F32)
    lax.fori_loop(0, each, step, (zero,) * (2 * rows), unroll=4)

    for row in range(rows):
        def mixed_step(c, _, row=row):
            y = ys[pl.ds(row * each * parts + c, each, stride=parts), :]
            mixed[row * each:(row + 1) * each, lanes(c)] = (gate[row * each:(row + 1) * each, lanes(c)] * y).astype(BF)
            return 0
        lax.fori_loop(0, parts, mixed_step, 0)
    save(mixed)
    loads[3].wait()
    def middle_tile(j, _):
        middle[:, cols_of(j)] = h[:, cols_of(j)].astype(F32) + dot(mixed[...], wo[:, cols_of(j)])
        return 0
    lax.fori_loop(0, width // tile, middle_tile, 0)
    save(middle)

    statistics(middle, mean, scale, tokens, width)
    mix_into(middle, mean, scale, same, g2, b2, (ck, cr), (hidden_in, gate_in), width)
    save(hidden_in)
    save(gate_in)
    loads[4].wait()
    def hidden_tile(j, _):
        r = jnp.maximum(dot(hidden_in[...], fk[:, cols_of(j)]), 0.0)
        rect[:, cols_of(j)] = r.astype(BF)
        act[:, cols_of(j)] = (r * r).astype(BF)
        return 0
    lax.fori_loop(0, ff // tile, hidden_tile, 0)
    save(rect)
    save(act)
    saves[5].wait()
    loads[5].wait()
    def gate_tile(j, _):
        gate[:, cols_of(j)] = jax.nn.sigmoid(dot(gate_in[...], fr[:, cols_of(j)]))
        return 0
    lax.fori_loop(0, width // tile, gate_tile, 0)
    loads[6].wait()
    def out_tile(j, _):
        cols = cols_of(j)
        o = dot(act[...], fv[:, cols])
        s = gate[:, cols]
        result[:, cols] = (middle[:, cols] + s * o).astype(BF)
        g = cot[:, cols].astype(F32)
        if with_delta:
            delta_out[:, cols] = (g * s).astype(BF)
            delta_gate[:, cols] = (g * o * s * (1.0 - s)).astype(BF)
        else:
            delta_out[:, cols] = s.astype(BF)
            delta_gate[:, cols] = (o * s * (1.0 - s)).astype(BF)
        return 0
    lax.fori_loop(0, width // tile, out_tile, 0)
    save(result)
    save(delta_out)
    save(delta_gate)
    for i, c in enumerate(saves):
        if i != 5:
            c.wait()

def forward(rows, with_delta, same_s, same, h, p, cot):
    (g1, b1, fade, bonus, mk, mv, mr, wk, wv, wr, wo, g2, b2, ck, cr, fk, fr, fv) = p
    tokens, width = h.shape
    ff = fk.shape[1]
    vm = pl.BlockSpec(memory_space=pltpu.VMEM)
    hbm = pl.BlockSpec(memory_space=pl.ANY)
    slabs = tokens * width // LANES
    outs = [((tokens, width), BF)] * 3 + [((slabs, LANES), F32)] * 2 + [((tokens, width), F32), ((tokens, width), BF), ((tokens, width), F32)]
    outs += [((tokens, width), BF)] * 2 + [((tokens, ff), BF)] * 2 + [((tokens, width), BF)] * 3
    outs = outs[:14] if False else outs
    wide, wide32, step32 = pltpu.VMEM((tokens, width), BF), pltpu.VMEM((tokens, width), F32), pltpu.VMEM((slabs, LANES), F32)
    stat = pltpu.VMEM((tokens, LANES), F32)
    square = pltpu.VMEM((width, width), BF)
    big = pltpu.VMEM((tokens, ff), BF)
    scratch = [square] * 4 + [pltpu.VMEM((width, ff), BF), square, pltpu.VMEM((ff, width), BF), stat, stat] + [wide] * 3
    scratch += [step32] * 3 + [wide32, wide, wide32, wide, wide, big, big, wide, wide, wide]
    scratch += [pltpu.SemaphoreType.DMA((7,)), pltpu.SemaphoreType.DMA((len(outs),))]
    return pl.pallas_call(
        functools.partial(forward_kernel, rows, with_delta),
        out_shape=tuple(jax.ShapeDtypeStruct(*o) for o in outs),
        in_specs=[pl.BlockSpec(memory_space=pltpu.SMEM)] + [vm] * 14 + [hbm] * 7,
        out_specs=(hbm,) * len(outs),
        scratch_shapes=scratch,
        compiler_params=pltpu.CompilerParams(vmem_limit_bytes=60 << 20),
        cost_estimate=pl.CostEstimate(flops=90000000000, bytes_accessed=261000000, transcendentals=0),
        name="forward",
    )(same_s, same, h, g1, b1, fade, bonus, mk, mv, mr, g2, b2, ck, cr, cot, wk, wv, wr, wo, fk, fr, fv)

def norm_backward(source, mean, scale, same, gain, bias, factors, grads, residual, targets, sums, first, second, tokens, width):
    first[...] = jnp.zeros_like(first)
    second[...] = jnp.zeros_like(second)
    def gather(c, _):
        cols = lanes(c)
        hat = (source[:, cols].astype(F32) - mean[...]) * scale[...]
        g = gain[:, cols].astype(F32)
        z = hat * g + bias[:, cols].astype(F32)
        step_up = z - pltpu.roll(z, 1, 0) * same[...]
        straight = jnp.zeros_like(z)
        total = jnp.zeros_like(z)
        for i, (factor, grad) in enumerate(zip(factors, grads)):
            d = grad[:, cols]
            f = factor[:, cols].astype(F32)
            sums[2 + i:3 + i, cols] = jnp.sum(d * step_up, axis=0, keepdims=True)
            straight = straight + d * f
            total = total + d
        dz = straight + pltpu.roll((total - straight) * same[...], tokens - 1, 0)
        sums[0:1, cols] = jnp.sum(dz * hat, axis=0, keepdims=True)
        sums[1:2, cols] = jnp.sum(dz, axis=0, keepdims=True)
        dhat = dz * g
        grads[0][:, cols] = dhat
        first[...] += dhat
        second[...] += dhat * hat
        return 0
    lax.fori_loop(0, width // LANES, gather, 0)
    for ref in (first, second):
        ref[...] = jnp.broadcast_to(jnp.sum(ref[...], axis=1, keepdims=True) * (1.0 / width), ref.shape)
    def finish(c, _):
        cols = lanes(c)
        hat = (source[:, cols].astype(F32) - mean[...]) * scale[...]
        out = residual[:, cols].astype(F32) + scale[...] * (grads[0][:, cols] - first[...] - hat * second[...])
        for t in targets:
            t[:, cols] = out.astype(t.dtype)
        return 0
    lax.fori_loop(0, width // LANES, finish, 0)

def channel_kernel(times, *refs):
    (same, factor_out, factor_gate, g, g2, b2, ck, cr, rect_in, middle_in, fv_in, fk_in, fr_in) = refs[:13]
    n_out = 6
    outs = refs[13:13 + n_out]
    (fv, fk, fr, rect, middle, delta_out, delta_gate, delta_pre, dh, dg, mean, scale, first, second, delta, branch, sums, in_sems, out_sems) = refs[13 + n_out:]
    tokens, width = g.shape
    ff = rect.shape[1]
    tile = 512
    chunks = ff // tile
    first_loads = []
    for j in range(chunks):
        span = slice(j * tile, (j + 1) * tile)
        first_loads += [(fv_in.at[span, :], fv.at[span, :]), (rect_in.at[:, span], rect.at[:, span])]
    loads = fetch(first_loads + [(fr_in, fr), (fk_in, fk), (middle_in, middle)], in_sems)
    saves = []
    def save(source, i):
        saves.append(pltpu.make_async_copy(source, outs[i], out_sems.at[i]))
        saves[-1].start()
    def cols_of(j):
        return pl.ds(pl.multiple_of(j * tile, tile), tile)
    if times:
        def scale_tile(j, _):
            cols = lanes(j)
            x = g[:, cols].astype(F32)
            delta_out[:, cols] = (x * factor_out[:, cols].astype(F32)).astype(BF)
            delta_gate[:, cols] = (x * factor_gate[:, cols].astype(F32)).astype(BF)
            return 0
        lax.fori_loop(0, width // LANES, scale_tile, 0)
        left_out, left_gate = delta_out, delta_gate
    else:
        left_out, left_gate = factor_out, factor_gate
    def pre_tile(j, _):
        cols = cols_of(j)
        pltpu.make_async_copy(fv_in.at[cols, :], fv.at[cols, :], in_sems.at[2 * j]).wait()
        pltpu.make_async_copy(rect_in.at[:, cols], rect.at[:, cols], in_sems.at[2 * j + 1]).wait()
        d = dot_nt(left_out[...], fv[cols, :])
        delta_pre[:, cols] = (d * (2.0 * rect[:, cols].astype(F32))).astype(BF)
        return 0
    lax.fori_loop(0, ff // tile, pre_tile, 0)
    save(delta_pre, 0)
    if times:
        save(delta_out, 4)
        save(delta_gate, 5)
    loads[-1].wait()
    statistics(middle, mean, scale, tokens, width)
    loads[-2].wait()
    loads[-3].wait()
    def hidden_tile(j, _):
        cols = cols_of(j)
        dh[:, cols] = dot_nt(delta_pre[...], fk[cols, :])
        dg[:, cols] = dot_nt(left_gate[...], fr[cols, :])
        return 0
    lax.fori_loop(0, width // tile, hidden_tile, 0)
    norm_backward(middle, mean, scale, same, g2, b2, (ck, cr), (dh, dg), g, (delta, branch), sums, first, second, tokens, width)
    save(delta, 1)
    save(branch, 2)
    save(sums, 3)
    for c in saves:
        c.wait()

def channel(times, same, factor_out, factor_gate, g, p, rect, middle):
    (g1, b1, fade, bonus, mk, mv, mr, wk, wv, wr, wo, g2, b2, ck, cr, fk, fr, fv) = p
    tokens, width = g.shape
    ff = fk.shape[1]
    vm = pl.BlockSpec(memory_space=pltpu.VMEM)
    hbm = pl.BlockSpec(memory_space=pl.ANY)
    outs = [((tokens, ff), BF), ((tokens, width), F32), ((tokens, width), BF), ((8, width), F32)]
    outs += [((tokens, width), BF)] * 2 if times else [((16, LANES), BF)] * 2
    wide, wide32 = pltpu.VMEM((tokens, width), BF), pltpu.VMEM((tokens, width), F32)
    stat = pltpu.VMEM((tokens, LANES), F32)
    big = pltpu.VMEM((tokens, ff), BF)
    scratch = [pltpu.VMEM((ff, width), BF), pltpu.VMEM((width, ff), BF), pltpu.VMEM((width, width), BF), big, wide32, wide, wide, big, wide32, wide32]
    scratch += [stat] * 4 + [wide32, wide, pltpu.VMEM((8, width), F32), pltpu.SemaphoreType.DMA((2 * ff // 512 + 3,)), pltpu.SemaphoreType.DMA((6,))]
    return pl.pallas_call(
        functools.partial(channel_kernel, times),
        out_shape=tuple(jax.ShapeDtypeStruct(*o) for o in outs),
        in_specs=[vm] * 8 + [hbm] * 5,
        out_specs=(hbm,) * 6,
        scratch_shapes=scratch,
        compiler_params=pltpu.CompilerParams(vmem_limit_bytes=60 << 20),
        cost_estimate=pl.CostEstimate(flops=75000000000, bytes_accessed=217500000, transcendentals=0),
        name="channel",
    )(same, factor_out, factor_gate, g, g2, b2, ck, cr, rect, middle, fv, fk, fr)

def time_kernel(rows, *refs):
    (same_s, same, branch, h, g1, b1, fade, bonus, mk, mv, mr, wo_in, gate_in, ks_in, vs_in, wk_in, wv_in, wr_in, delta_in) = refs[:19]
    n_out = 5
    outs = refs[19:19 + n_out]
    (wo, gate, ks, vs, wk, wv, wr, delta, dm, gs, ys, tops, bottoms, dk, dv, dr, ik, iv, ir, mean, scale, first, second, state, sums, in_sems, out_sems) = refs[19 + n_out:]
    tokens, width = h.shape
    each = tokens // rows
    parts = width // LANES
    tile = 512
    loads = fetch([(wo_in, wo), (gate_in, gate), (ks_in, ks), (vs_in, vs), (wk_in, wk), (wv_in, wv), (wr_in, wr), (delta_in, delta)], in_sems)
    saves = []
    def save(source, i):
        saves.append(pltpu.make_async_copy(source, outs[i], out_sems.at[i]))
        saves[-1].start()
    def cols_of(j):
        return pl.ds(pl.multiple_of(j * tile, tile), tile)
    loads[0].wait()
    loads[1].wait()
    def mixed_tile(j, _):
        cols = cols_of(j)
        d = dot_nt(branch[...], wo[cols, :])
        dm[:, cols] = d
        e = d * gate[:, cols]
        for row in range(rows):
            for c in range(tile // LANES):
                gs[pl.ds(row * each * parts + j * (tile // LANES) + c, each, stride=parts), :] = e[row * each:(row + 1) * each, c * LANES:(c + 1) * LANES]
        return 0
    lax.fori_loop(0, width // tile, mixed_tile, 0)
    statistics(h, mean, scale, tokens, width)
    loads[2].wait()
    loads[3].wait()
    rate = jnp.exp(fade[...])
    decay = jnp.exp(-rate)
    extra = bonus[...]
    def step(t, carry):
        following = []
        for row in range(rows):
            here = pl.ds(pl.multiple_of((row * each + t) * parts, parts), parts)
            m = same_s[row, t]
            top, bottom = carry[2 * row] * m, carry[2 * row + 1] * m
            tops[here, :] = top
            bottoms[here, :] = bottom
            k, v = ks[here, :], vs[here, :]
            ek, now = jnp.exp(k), jnp.exp(extra + k)
            inverse = 1.0 / (bottom + now)
            ys[here, :] = (top + now * v) * inverse
            gs[here, :] = gs[here, :] * inverse
            following += [decay * top + ek * v, decay * bottom + ek]
        return tuple(following)
    zero = jnp.zeros(decay.shape, F32)
    lax.fori_loop(0, each, step, (zero,) * (2 * rows), unroll=4)
    def back(i, carry):
        t = each - 1 - i
        dw, du = carry[:2]
        following = []
        for row in range(rows):
            here = pl.ds(pl.multiple_of((row * each + t) * parts, parts), parts)
            a, b = carry[2 + 2 * row], carry[3 + 2 * row]
            k, v = ks[here, :], vs[here, :]
            ek, now = jnp.exp(k), jnp.exp(extra + k)
            ga = gs[here, :]
            gb = -ga * ys[here, :]
            q = now * (v * ga + gb)
            ks[here, :] = ek * (v * a + b) + q
            vs[here, :] = ek * a + now * ga
            du = du + q
            dw = dw + (a * tops[here, :] + b * bottoms[here, :])
            m = same_s[row, t]
            following += [(ga + decay * a) * m, (gb + decay * b) * m]
        return (dw, du, *following)
    done = lax.fori_loop(0, each, back, (zero,) * (2 + 2 * rows), unroll=4)
    dfade = -done[0] * decay * rate
    for c in range(parts):
        sums[5:6, c * LANES:(c + 1) * LANES] = dfade[c:c + 1, :]
        sums[6:7, c * LANES:(c + 1) * LANES] = done[1][c:c + 1, :]
    for row in range(rows):
        def out_step(c, _, row=row):
            span = slice(row * each, (row + 1) * each)
            cols = lanes(c)
            at = pl.ds(row * each * parts + c, each, stride=parts)
            dk[span, cols] = ks[at, :].astype(BF)
            dv[span, cols] = vs[at, :].astype(BF)
            s = gate[span, cols]
            dr[span, cols] = (dm[span, cols] * ys[at, :] * s * (1.0 - s)).astype(BF)
            return 0
        lax.fori_loop(0, parts, out_step, 0)
    for i, z in enumerate((dk, dv, dr)):
        save(z, i)
    for i in (4, 5, 6):
        loads[i].wait()
    def in_tile(j, _):
        cols = cols_of(j)
        ik[:, cols] = dot_nt(dk[...], wk[cols, :])
        iv[:, cols] = dot_nt(dv[...], wv[cols, :])
        ir[:, cols] = dot_nt(dr[...], wr[cols, :])
        return 0
    lax.fori_loop(0, width // tile, in_tile, 0)
    loads[7].wait()
    norm_backward(h, mean, scale, same, g1, b1, (mk, mv, mr), (ik, iv, ir), delta, (state,), sums, first, second, tokens, width)
    save(state, 3)
    save(sums, 4)
    for c in saves:
        c.wait()

def time_mix(rows, dtype, same_s, same, branch, delta, h, p, gate, ks, vs):
    (g1, b1, fade, bonus, mk, mv, mr, wk, wv, wr, wo, g2, b2, ck, cr, fk, fr, fv) = p
    tokens, width = h.shape
    vm = pl.BlockSpec(memory_space=pltpu.VMEM)
    hbm = pl.BlockSpec(memory_space=pl.ANY)
    outs = [((tokens, width), BF)] * 3 + [((tokens, width), dtype), ((8, width), F32)]
    wide, wide32 = pltpu.VMEM((tokens, width), BF), pltpu.VMEM((tokens, width), F32)
    step32 = pltpu.VMEM(ks.shape, F32)
    stat = pltpu.VMEM((tokens, LANES), F32)
    square = pltpu.VMEM((width, width), BF)
    scratch = [square, wide32, step32, step32, square, square, square, wide32, wide32] + [step32] * 4 + [wide] * 3 + [wide32] * 3 + [stat] * 4
    scratch += [pltpu.VMEM((tokens, width), dtype), pltpu.VMEM((8, width), F32), pltpu.SemaphoreType.DMA((8,)), pltpu.SemaphoreType.DMA((5,))]
    return pl.pallas_call(
        functools.partial(time_kernel, rows),
        out_shape=tuple(jax.ShapeDtypeStruct(*o) for o in outs),
        in_specs=[pl.BlockSpec(memory_space=pltpu.SMEM)] + [vm] * 10 + [hbm] * 8,
        out_specs=(hbm,) * 5,
        scratch_shapes=scratch,
        compiler_params=pltpu.CompilerParams(vmem_limit_bytes=60 << 20),
        cost_estimate=pl.CostEstimate(flops=87000000000, bytes_accessed=252300000, transcendentals=0),
        name="time_mix",
    )(same_s, same, branch, h, g1, b1, fade, bonus, mk, mv, mr, wo, gate, ks, vs, wk, wv, wr, delta)


UNIT = 1024


def starts(parts):
    return [sum(c for c, _ in parts[:i]) for i in range(len(parts))]


def terms_kernel(count, parts, shapes, with_sums, *refs):
    bits, refs = refs[0], refs[1:]
    n, np_ = len(shapes), len(parts)
    left_in, right_in, refs = refs[:n], refs[n:2 * n], refs[2 * n:]
    if with_sums:
        early, late, *refs = refs
    outs, refs = refs[:2 * np_], refs[2 * np_:]
    lefts, rights, refs = refs[:n], refs[n:2 * n], refs[2 * n:]
    bufs, (in_sems, out_sems) = refs[:np_], refs[np_:]
    sends, keeps = outs[::2], outs[1::2]
    tile = 256
    columns = starts(parts)

    def place(order, d):
        bit = [(d >> b) & 1 if isinstance(d, int) else lax.rem(lax.div(d, 1 << b), 2) for b in order]
        return bit[0] ^ bits[order[0]], bit[1] * 4 + bit[2] * 2 + bit[3]

    loads = []
    for i in range(n):
        loads.append(pltpu.make_async_copy(right_in[i], rights[i], in_sems.at[2 * i]))
        loads.append(pltpu.make_async_copy(left_in[i], lefts[i], in_sems.at[2 * i + 1]))
    for c in loads:
        c.start()
    waits = []
    base = 0
    for m, ((kin, width), left, right) in enumerate(zip(shapes, lefts, rights)):
        rows = kin // count
        per = max(tile // rows, 1)
        loads[2 * m].wait()
        loads[2 * m + 1].wait()

        def step(j, _, left=left, right=right, rows=rows, per=per, width=width, base=base):
            lhs = left[:, pl.ds(pl.multiple_of(j * tile, tile), tile)]
            for q in range(width // UNIT):
                for i, (cols, order) in enumerate(parts):
                    at = q * UNIT + columns[i]
                    res = lax.dot_general(lhs, right[:, at:at + cols], (((0,), (0,)), ((), ())), preferred_element_type=F32).astype(BF)
                    for s in range(per):
                        relative, index = place(order, j * per + s)
                        bufs[i][relative, index, base + q * rows:base + (q + 1) * rows, :] = res[s * rows:(s + 1) * rows]
                        if rows == tile:
                            source = bufs[i].at[relative, index]
                            for r, target in ((1, sends[i]), (0, keeps[i])):
                                @pl.when(relative == r)
                                def _(source=source, target=target, index=index, i=i):
                                    pltpu.make_async_copy(source, target.at[index], out_sems.at[i, j]).start()
            return 0

        lax.fori_loop(0, kin // tile, step, 0)
        span = rows * (width // UNIT)
        for i in range(np_):
            if rows == tile:
                for j in range(kin // tile):
                    waits.append(pltpu.make_async_copy(bufs[i].at[0, 0], keeps[i].at[0], out_sems.at[i, j]))
            else:
                for r, target in ((1, sends[i]), (0, keeps[i])):
                    c = pltpu.make_async_copy(bufs[i].at[r, :, base:base + span, :], target.at[:, base:base + span, :], out_sems.at[i, 2 * m + r])
                    c.start()
                    waits.append(c)
        base += span
    if with_sums:
        share = early.shape[1] // count
        both = jnp.concatenate([early[...], late[...]], axis=0)
        for buf in bufs:
            buf[:, :, base:base + 16, :] = jnp.zeros(buf.shape[:2] + (16, buf.shape[3]), BF)
        for d in range(count):
            column = d * share // LANES * LANES
            piece = both[:, column:column + LANES]
            if d * share - column:
                piece = pltpu.roll(piece, LANES - (d * share - column), 1)
            relative, index = place(parts[0][1], d)
            bufs[0][relative, index, base:base + 16, 0:LANES] = piece.astype(BF)
        for i in range(np_):
            for r, target in ((1, sends[i]), (0, keeps[i])):
                c = pltpu.make_async_copy(bufs[i].at[r, :, base:base + 16, :], target.at[:, base:base + 16, :], out_sems.at[i, 2 * n + r])
                c.start()
                waits.append(c)
    for c in waits:
        c.wait()


def terms(bits, parts, pairs, sums=()):
    count = 16
    lefts, rights = zip(*pairs)
    shapes = tuple((a.shape[1], b.shape[1]) for a, b in pairs)
    tokens = lefts[0].shape[0]
    rows = sum(kin // count * (width // UNIT) for kin, width in shapes) + (16 if sums else 0)
    outs, bufs = [], []
    for cols, _ in parts:
        outs += [jax.ShapeDtypeStruct((count // 2, rows, cols), BF)] * 2
        bufs.append(pltpu.VMEM((2, count // 2, rows, cols), BF))
    flops = sum(2 * tokens * kin * width for kin, width in shapes)
    result = pl.pallas_call(
        functools.partial(terms_kernel, count, parts, shapes, bool(sums)),
        out_shape=tuple(outs),
        in_specs=[SM] + [HBM] * (2 * len(shapes)) + [VM] * len(sums),
        out_specs=(HBM,) * len(outs),
        scratch_shapes=[pltpu.VMEM(x.shape, BF) for x in (*lefts, *rights)]
        + bufs + [pltpu.SemaphoreType.DMA((2 * len(shapes),)), pltpu.SemaphoreType.DMA((len(parts), 16))],
        compiler_params=pltpu.CompilerParams(vmem_limit_bytes=56 << 20),
        cost_estimate=pl.CostEstimate(flops=39000000000, bytes_accessed=113100000, transcendentals=0),
        name="terms",
    )(bits, *lefts, *rights, *sums)
    return list(zip(result[::2], result[1::2]))


def swap(block, bit):
    count = lax.axis_size("dp")
    return lax.ppermute(block, "dp", [(i, i ^ (1 << bit)) for i in range(count)])


def summed(kept, came, dtype=BF):
    return (kept.astype(F32) + came.astype(F32)).astype(dtype)


def advance_kernel(bits, kept_go, came_go, kept_stay, came_stay, send, keep):
    send[...] = summed(kept_go[...], came_go[...])
    keep[...] = summed(kept_stay[...], came_stay[...])


def advance(bits, kept, came, bit):
    lead, rows, cols = kept.shape
    half = lead // 2
    block = rows // 2 if rows % 32 == 0 else rows
    go = pl.BlockSpec((1, block, cols), lambda g, i, b: ((1 - b[bit]) * half + g, i, 0))
    stay = pl.BlockSpec((1, block, cols), lambda g, i, b: (b[bit] * half + g, i, 0))
    out = pl.BlockSpec((1, block, cols), lambda g, i, b: (g, i, 0))
    return pl.pallas_call(
        advance_kernel,
        out_shape=(jax.ShapeDtypeStruct((half, rows, cols), BF),) * 2,
        grid_spec=pltpu.PrefetchScalarGridSpec(
            num_scalar_prefetch=1, grid=(half, rows // block), in_specs=[go, go, stay, stay], out_specs=(out, out)
        ),
        compiler_params=pltpu.CompilerParams(vmem_limit_bytes=30 << 20),
        cost_estimate=pl.CostEstimate(flops=9000000000, bytes_accessed=26100000, transcendentals=0),
        name="advance",
    )(bits, kept, came, kept, came)


def final_kernel(pieces, parts, *refs):
    n = len(parts)
    ins, outs = refs[:2 * n], refs[2 * n:]
    for (row, rows, blocks, columns), out in zip(pieces, outs):
        for q in range(blocks):
            span = slice(row + q * rows, row + (q + 1) * rows)
            if columns < UNIT:
                out[...] = summed(ins[0][0, span, 0:LANES], ins[1][0, span, 0:LANES], F32)[:, :columns]
                continue
            for i, at in enumerate(starts(parts)):
                out[:, q * UNIT + at:q * UNIT + at + parts[i][0]] = summed(ins[2 * i][0, span, :], ins[2 * i + 1][0, span, :], F32)


def final(parts, pieces, arrays):
    size = sum(a.size for a in arrays)
    return pl.pallas_call(
        functools.partial(final_kernel, pieces, parts),
        out_shape=tuple(jax.ShapeDtypeStruct((rows, blocks * columns), F32) for row, rows, blocks, columns in pieces),
        in_specs=[VM] * len(arrays),
        out_specs=(VM,) * len(pieces),
        compiler_params=pltpu.CompilerParams(vmem_limit_bytes=40 << 20),
        cost_estimate=pl.CostEstimate(flops=4500000000, bytes_accessed=13050000, transcendentals=0),
        name="final",
    )(*arrays)


def after(value, *earlier):
    return lax.optimization_barrier((value, earlier))[0]


class Line:
    def __init__(self, bits, plan, pieces):
        self.bits, self.plan, self.pieces, self.token, self.flight, self.sums = bits, plan, pieces, None, {}, {}

    def tie(self, value):
        return value if self.token is None else after(value, self.token)

    def open(self, group, pairs, sums=()):
        pairs = ((self.tie(pairs[0][0]), pairs[0][1]),) + tuple(pairs[1:])
        found = terms(self.bits, self.plan[group], pairs, sums)
        self.token = found
        for i, (send, keep) in enumerate(found):
            self.flight[group, i] = keep, swap(send, self.plan[group][i][1][0])

    def serve(self, steps):
        for group, i, stage in steps:
            parts = self.plan[group]
            if stage < 4:
                kept, came = self.tie(self.flight[group, i])
                send, keep = advance(self.bits, kept, came, parts[i][1][stage])
                self.token = send, keep
                self.flight[group, i] = keep, swap(send, parts[i][1][stage])
            else:
                self.sums[group, i] = self.flight.pop((group, i))
                if all((group, k) in self.sums for k in range(len(parts))):
                    arrays = [a for k in range(len(parts)) for a in self.sums[group, k]]
                    arrays[0] = self.tie(arrays[0])
                    self.sums[group] = final(parts, self.pieces[group], arrays)
                    self.token = self.sums[group][0]


def halving(left, right=None):
    count = lax.axis_size("dp")
    bits = count.bit_length() - 1
    me = lax.axis_index("dp")
    if right is not None:
        left = lax.dot_general(left, right, (((0,), (0,)), ((), ())), preferred_element_type=F32).astype(BF)
    current = left.reshape((2,) * bits + (left.shape[0] // count, left.shape[1]))
    for bit in range(bits):
        axis = bits - 1 - bit
        mine = (me >> bit) & 1
        send = lax.dynamic_index_in_dim(current, 1 - mine, axis, keepdims=False)
        keep = lax.dynamic_index_in_dim(current, mine, axis, keepdims=False)
        current = summed(keep, swap(send, bit), BF if bit + 1 < bits else F32)
    return current


def unwritten(function, *args):
    shapes, tree = jax.tree.flatten(jax.eval_shape(function, *args))
    outs = pl.pallas_call(
        lambda *refs: None, out_shape=tuple(shapes), out_specs=(HBM,) * len(shapes), name="unwritten"
    )()
    return jax.tree.unflatten(tree, outs)


VECTORS = (0, 1, 5, 6, 2, 3, 4, 8, 9, 10, 11)
PARTS_0 = dict(
    a=((512, (0, 1, 2, 3)), (512, (2, 3, 1, 0))),
    b=((640, (0, 1, 2, 3)), (384, (0, 2, 1, 3))),
    e=((512, (0, 1, 2, 3)), (512, (1, 0, 2, 3))),
)
PARTS_1 = dict(
    a=((640, (2, 1, 3, 0)), (384, (2, 3, 1, 0))),
    b=((384, (2, 1, 3, 0)), (640, (1, 2, 0, 3))),
    e=((512, (0, 2, 3, 1)), (512, (1, 0, 2, 3))),
)
STEPS_0 = (
    (),
    (('a', 0, 1), ('a', 1, 1)),
    (('b', 0, 1), ('a', 0, 2), ('a', 1, 2), ('b', 1, 1), ('a', 0, 3), ('e', 1, 1), ('b', 1, 2), ('b', 0, 2), ('a', 1, 3), ('a', 0, 4), ('e', 0, 1), ('b', 1, 3), ('e', 1, 2), ('a', 1, 4), ('b', 0, 3), ('e', 0, 2), ('b', 1, 4), ('e', 1, 3), ('e', 0, 3), ('b', 0, 4), ('e', 1, 4), ('e', 0, 4)),
)
STEPS_1 = (
    (),
    (('a', 0, 1), ('a', 1, 1)),
    (),
    (('a', 0, 2), ('a', 1, 2), ('e', 0, 1), ('b', 0, 1), ('b', 1, 1), ('a', 0, 3), ('e', 0, 2), ('e', 1, 1), ('a', 1, 3), ('b', 1, 2), ('b', 0, 2), ('e', 0, 3), ('a', 0, 4), ('e', 1, 2), ('a', 1, 4), ('b', 0, 3), ('b', 1, 3), ('e', 1, 3), ('e', 0, 4), ('b', 1, 4), ('e', 1, 4), ('b', 0, 4)),
)


def local(entry_pair, labels, *params):
    count = lax.axis_size("dp")
    section = lax.axis_index("section")
    rows, each, width = entry_pair.shape[1:]
    own = entry_pair.reshape(rows * each, width)
    share = width // count
    p = [e if e.ndim == 2 else e[0] for e in params]
    ff = p[15].shape[1]
    for i in (2, 3):
        p[i] = p[i].reshape(width // LANES, LANES).astype(F32)
    first = jnp.zeros((rows, 1), F32)
    same_s = jnp.concatenate([first, (labels[:, 1:] == labels[:, :-1]).astype(F32)], axis=1)
    same = jnp.broadcast_to(same_s.reshape(rows * each, 1), (rows * each, LANES))
    fast = count == 16 and width == UNIT
    me = lax.axis_index("dp")
    bits = jnp.stack([(me >> i) & 1 for i in range(4)])
    wide = ff // width
    pieces = dict(
        a=((0, ff // count, 1, width),),
        b=((0, share, wide, width), (share * wide, share, 1, width), (share * (wide + 1), share, 1, width)),
        e=tuple((i * share, share, 1, width) for i in range(3)) + tuple((3 * share + i, 1, 1, share) for i in VECTORS),
    )

    def plain_rest(pairs, sums):
        together = jnp.concatenate(sums).astype(BF).reshape(16, count, share).transpose(1, 0, 2).reshape(count * 16, share)
        vectors = halving(together)
        return tuple(halving(*pair) for pair in pairs) + tuple(vectors[i:i + 1] for i in VECTORS)

    def start():
        return forward(rows, False, same_s, same, own, p, own)

    def middle_part(received):
        kept = forward(rows, True, same_s, same, received, p, own)
        (key_in, value_in, recept_in, ks, vs, gate, mixed, middle, hidden_in, gate_in, rect, act, result, delta_out, delta_gate) = kept
        line = Line(bits, PARTS_1, pieces)
        if fast:
            line.open("a", ((act, delta_out),))
        delta_pre, delta, branch, late, _, _ = channel(False, same, delta_out, delta_gate, line.tie(own), p, rect, middle)
        line.token = branch
        if fast:
            line.serve(STEPS_1[0])
        dk, dv, dr, state, early = time_mix(rows, BF, same_s, same, line.tie(branch), delta, received, p, gate, ks, vs)
        key_pairs = ((hidden_in, delta_pre), (gate_in, delta_gate), (mixed, branch))
        begun = list(line.flight.values()) if fast else (act, delta_out)
        return state, result, begun, (early, late), key_pairs, ((key_in, dk), (value_in, dv), (recept_in, dr))

    def end_first(received, kept):
        (key_in, value_in, recept_in, ks, vs, gate, mixed, middle, hidden_in, gate_in, rect, act, result, factor_out, factor_gate) = kept
        line = Line(bits, PARTS_0, pieces)
        if fast:
            line.open("a", ((act, (received.astype(F32) * factor_out.astype(F32)).astype(BF)),))
        g = line.tie(received)
        delta_pre, delta, branch, late, delta_out, delta_gate = channel(True, same, factor_out, factor_gate, g, p, rect, middle)
        key_pairs = ((hidden_in, delta_pre), (gate_in, delta_gate), (mixed, branch))
        line.token = branch
        if fast:
            line.serve(STEPS_0[0])
            line.open("b", key_pairs)
            line.serve(STEPS_0[1])
        dk, dv, dr, state, early = time_mix(rows, F32, same_s, same, line.tie(branch), delta, own, p, gate, ks, vs)
        rest_pairs = ((key_in, dk), (value_in, dv), (recept_in, dr))
        if not fast:
            return state, (halving(act, delta_out),), tuple(halving(*pair) for pair in key_pairs), plain_rest(rest_pairs, (early, late))
        line.token = state
        line.open("e", rest_pairs, (early, late))
        line.serve(STEPS_0[2])
        return state, line.sums["a"], line.sums["b"], line.sums["e"]

    def end_second(result, begun, sums, key_pairs, rest_pairs):
        if not fast:
            return result.astype(F32), (halving(*begun),), tuple(halving(*pair) for pair in key_pairs), plain_rest(rest_pairs, sums)
        line = Line(bits, PARTS_1, pieces)
        line.flight = {("a", i): pair for i, pair in enumerate(begun)}
        line.serve(STEPS_1[1])
        line.open("b", key_pairs)
        line.serve(STEPS_1[2])
        line.open("e", rest_pairs, sums)
        line.serve(STEPS_1[3])
        return result.astype(F32), line.sums["a"], line.sums["b"], line.sums["e"]

    kept = lax.cond(section == 0, start, lambda: unwritten(start))
    received = lax.ppermute(kept[12], "section", [(0, 1)])
    delta, *pending = lax.cond(section == 1, middle_part, lambda r: unwritten(middle_part, r), received)
    received = lax.ppermute(delta, "section", [(1, 0)])
    ends, (value_sum,), (key_sum, gate_sum, exit_sum), rest = lax.cond(
        section == 0, lambda r, k, q: end_first(r, k), lambda r, k, q: end_second(*q), received, kept, pending
    )
    ends = ends.reshape(rows, each, width)
    everything = (ends, *(z[0] for z in rest[3:10]), *rest[:3], exit_sum, *(z[0] for z in rest[10:14]), key_sum, gate_sum, value_sum)
    return tuple(e[None] for e in everything)


def solution(mesh):
    vec, mat = P("section", None), P("section", None, None)
    in_specs = (P("section", "dp", None, None), P("dp", None)) + (vec,) * 7 + (mat,) * 4 + (vec,) * 4 + (mat,) * 3
    vec, mat = P("section", "dp"), P("section", "dp", None)
    out_specs = (P("section", "dp", None, None),) + (vec,) * 7 + (mat,) * 4 + (vec,) * 4 + (mat,) * 3
    return jax.shard_map(local, mesh=mesh, in_specs=in_specs, out_specs=out_specs, check_vma=False)
```

```python
import functools

import jax
import jax.numpy as jnp
from jax import lax
from jax.experimental import pallas as pl
from jax.experimental.pallas import tpu as pltpu
from jax.sharding import PartitionSpec as P

BF = jnp.bfloat16
F32 = jnp.float32
LANES = 128
VM = pl.BlockSpec(memory_space=pltpu.VMEM)
HBM = pl.BlockSpec(memory_space=pl.ANY)
SM = pl.BlockSpec(memory_space=pltpu.SMEM)

def dot(left, right):
    return jnp.dot(left, right, preferred_element_type=F32)

def dot_nt(left, right):
    return lax.dot_general(left, right, (((1,), (1,)), ((), ())), preferred_element_type=F32)

def lanes(c):
    return pl.ds(pl.multiple_of(c * LANES, LANES), LANES)

def statistics(source, mean, scale, tokens, width, chunk=128):
    def step(i, _):
        at = pl.ds(pl.multiple_of(i * chunk, chunk), chunk)
        x = source[at, :].astype(F32)
        m = jnp.sum(x, axis=1, keepdims=True) * (1.0 / width)
        x = x - m
        v = jnp.sum(x * x, axis=1, keepdims=True) * (1.0 / width)
        mean[at, :] = jnp.broadcast_to(m, (chunk, LANES))
        scale[at, :] = jnp.broadcast_to(lax.rsqrt(v + 1e-05), (chunk, LANES))
        return 0
    lax.fori_loop(0, tokens // chunk, step, 0)

def mix_into(source, mean, scale, same, gain, bias, factors, targets, width):
    def step(c, _):
        cols = lanes(c)
        z = (source[:, cols].astype(F32) - mean[...]) * scale[...] * gain[:, cols].astype(F32) + bias[:, cols].astype(F32)
        before = pltpu.roll(z, 1, 0) * same[...]
        step_up = z - before
        for factor, target in zip(factors, targets):
            target[:, cols] = (before + step_up * factor[:, cols].astype(F32)).astype(BF)
        return 0
    lax.fori_loop(0, width // LANES, step, 0)

def fetch(pairs, sems):
    copies = [pltpu.make_async_copy(s, d, sems.at[i]) for i, (s, d) in enumerate(pairs)]
    for c in copies:
        c.start()
    return copies

def forward_kernel(rows, with_delta, *refs):
    (same_s, same, h, g1, b1, fade, bonus, mk, mv, mr, g2, b2, ck, cr, cot) = refs[:15]
    weights = refs[15:22]
    n_out = 16
    outs = refs[22:22 + n_out]
    (wk, wv, wr, wo, fk, fr, fv, mean, scale, key_in, value_in, recept_in, ks, vs, ys, tops, bottoms, gate, mixed, middle,
     hidden_in, gate_in, act, in_sems, out_sems) = refs[22 + n_out:]
    tokens, width = h.shape
    each = tokens // rows
    parts = width // LANES
    tile = 1024
    ff = act.shape[1]
    loads = fetch(list(zip(weights, (wk, wv, wr, wo, fk, fr, fv))), in_sems)
    saves = []

    def save(source):
        i = len(saves)
        saves.append(pltpu.make_async_copy(source, outs[i], out_sems.at[i]))
        saves[-1].start()

    statistics(h, mean, scale, tokens, width)
    mix_into(h, mean, scale, same, g1, b1, (mk, mv, mr), (key_in, value_in, recept_in), width)
    for z in (key_in, value_in, recept_in):
        save(z)

    def cols_of(j):
        return pl.ds(pl.multiple_of(j * tile, tile), tile)

    def steps_tile(values, target, j):
        for row in range(rows):
            for c in range(tile // LANES):
                target[pl.ds(row * each * parts + j * (tile // LANES) + c, each, stride=parts), :] = values[row * each:(row + 1) * each, c * LANES:(c + 1) * LANES]

    loads[0].wait()
    def key_tile(j, _):
        steps_tile(dot(key_in[...], wk[:, cols_of(j)]), ks, j)
        return 0
    lax.fori_loop(0, width // tile, key_tile, 0)
    loads[1].wait()
    def value_tile(j, _):
        steps_tile(dot(value_in[...], wv[:, cols_of(j)]), vs, j)
        return 0
    lax.fori_loop(0, width // tile, value_tile, 0)
    save(ks)
    save(vs)
    loads[2].wait()
    def accept_tile(j, _):
        gate[:, cols_of(j)] = jax.nn.sigmoid(dot(recept_in[...], wr[:, cols_of(j)]))
        return 0
    lax.fori_loop(0, width // tile, accept_tile, 0)
    save(gate)

    decay = jnp.exp(-jnp.exp(fade[...]))
    extra = bonus[...]
    def step(t, carry):
        following = []
        for row in range(rows):
            here = pl.ds(pl.multiple_of((row * each + t) * parts, parts), parts)
            m = same_s[row, t]
            top, bottom = carry[2 * row] * m, carry[2 * row + 1] * m
            tops[here, :] = top
            bottoms[here, :] = bottom
            k, v = ks[here, :], vs[here, :]
            ek, now = jnp.exp(k), jnp.exp(extra + k)
            ys[here, :] = (top + now * v) / (bottom + now)
            following += [decay * top + ek * v, decay * bottom + ek]
        return tuple(following)
    zero = jnp.zeros(decay.shape, F32)
    lax.fori_loop(0, each, step, (zero,) * (2 * rows), unroll=4)
    save(tops)
    save(bottoms)

    for row in range(rows):
        def mixed_step(c, _, row=row):
            y = ys[pl.ds(row * each * parts + c, each, stride=parts), :]
            mixed[row * each:(row + 1) * each, lanes(c)] = (gate[row * each:(row + 1) * each, lanes(c)] * y).astype(BF)
            return 0
        lax.fori_loop(0, parts, mixed_step, 0)
    save(mixed)
    loads[3].wait()
    def middle_tile(j, _):
        middle[:, cols_of(j)] = h[:, cols_of(j)].astype(F32) + dot(mixed[...], wo[:, cols_of(j)])
        return 0
    lax.fori_loop(0, width // tile, middle_tile, 0)
    save(middle)

    statistics(middle, mean, scale, tokens, width)
    mix_into(middle, mean, scale, same, g2, b2, (ck, cr), (hidden_in, gate_in), width)
    save(hidden_in)
    save(gate_in)
    loads[4].wait()
    def hidden_tile(j, _):
        r = jnp.maximum(dot(hidden_in[...], fk[:, cols_of(j)]), 0.0)
        act[:, cols_of(j)] = (r * r).astype(BF)
        return 0
    lax.fori_loop(0, ff // tile, hidden_tile, 0)
    save(act)
    for i in (0, 1, 2, 5):
        saves[i].wait()
    result, delta_out, delta_gate = key_in, value_in, recept_in
    loads[5].wait()
    def gate_tile(j, _):
        gate[:, cols_of(j)] = jax.nn.sigmoid(dot(gate_in[...], fr[:, cols_of(j)]))
        return 0
    lax.fori_loop(0, width // tile, gate_tile, 0)
    loads[6].wait()
    def out_tile(j, _):
        cols = cols_of(j)
        o = dot(act[...], fv[:, cols])
        s = gate[:, cols]
        result[:, cols] = (middle[:, cols] + s * o).astype(BF)
        g = cot[:, cols].astype(F32)
        if with_delta:
            delta_out[:, cols] = (g * s).astype(BF)
            delta_gate[:, cols] = (g * o * s * (1.0 - s)).astype(BF)
        else:
            delta_out[:, cols] = s.astype(BF)
            delta_gate[:, cols] = (o * s * (1.0 - s)).astype(BF)
        return 0
    lax.fori_loop(0, width // tile, out_tile, 0)
    save(result)
    save(delta_out)
    save(delta_gate)
    for i, c in enumerate(saves):
        if i not in (0, 1, 2, 5):
            c.wait()

def forward(rows, with_delta, same_s, same, h, p, cot):
    (g1, b1, fade, bonus, mk, mv, mr, wk, wv, wr, wo, g2, b2, ck, cr, fk, fr, fv) = p
    tokens, width = h.shape
    ff = fk.shape[1]
    vm = pl.BlockSpec(memory_space=pltpu.VMEM)
    hbm = pl.BlockSpec(memory_space=pl.ANY)
    slabs = tokens * width // LANES
    outs = [((tokens, width), BF)] * 3 + [((slabs, LANES), F32)] * 2 + [((tokens, width), F32)] + [((slabs, LANES), F32)] * 2
    outs += [((tokens, width), BF), ((tokens, width), F32)]
    outs += [((tokens, width), BF)] * 2 + [((tokens, ff), BF)] + [((tokens, width), BF)] * 3
    outs = outs[:14] if False else outs
    wide, wide32, step32 = pltpu.VMEM((tokens, width), BF), pltpu.VMEM((tokens, width), F32), pltpu.VMEM((slabs, LANES), F32)
    stat = pltpu.VMEM((tokens, LANES), F32)
    square = pltpu.VMEM((width, width), BF)
    big = pltpu.VMEM((tokens, ff), BF)
    scratch = [square] * 4 + [pltpu.VMEM((width, ff), BF), square, pltpu.VMEM((ff, width), BF), stat, stat] + [wide] * 3
    scratch += [step32] * 5 + [wide32, wide, wide32, wide, wide, big]
    scratch += [pltpu.SemaphoreType.DMA((7,)), pltpu.SemaphoreType.DMA((len(outs),))]
    return pl.pallas_call(
        functools.partial(forward_kernel, rows, with_delta),
        out_shape=tuple(jax.ShapeDtypeStruct(*o) for o in outs),
        in_specs=[pl.BlockSpec(memory_space=pltpu.SMEM)] + [vm] * 14 + [hbm] * 7,
        out_specs=(hbm,) * len(outs),
        scratch_shapes=scratch,
        compiler_params=pltpu.CompilerParams(vmem_limit_bytes=60 << 20),
        cost_estimate=pl.CostEstimate(flops=90000000000, bytes_accessed=261000000, transcendentals=0),
        name="forward",
    )(same_s, same, h, g1, b1, fade, bonus, mk, mv, mr, g2, b2, ck, cr, cot, wk, wv, wr, wo, fk, fr, fv)

def norm_backward(source, mean, scale, same, gain, bias, factors, grads, residual, targets, sums, hats, first, second, rows):
    tokens, width = source.shape
    each = tokens // rows
    spans = [slice(row * each, (row + 1) * each) for row in range(rows)]

    def gather(c, carry):
        cols = lanes(c)
        g, b = gain[:, cols].astype(F32), bias[:, cols].astype(F32)
        following = []
        totals = [0.0] * (2 + len(grads))
        for row, at in enumerate(spans):
            hat = (source[at, cols].astype(F32) - mean[at, :]) * scale[at, :]
            z = hat * g + b
            step_up = z - pltpu.roll(z, 1, 0) * same[at, :]
            straight = rest = None
            for i, (factor, grad) in enumerate(zip(factors, grads)):
                d = grad[at, cols]
                df = d * factor[:, cols].astype(F32)
                totals[2 + i] += jnp.sum(d * step_up, axis=0, keepdims=True)
                straight = df if i == 0 else straight + df
                rest = d - df if i == 0 else rest + (d - df)
            dz = straight + pltpu.roll(rest * same[at, :], each - 1, 0)
            totals[0] += jnp.sum(dz * hat, axis=0, keepdims=True)
            totals[1] += jnp.sum(dz, axis=0, keepdims=True)
            dhat = dz * g
            hats[at, cols] = dhat
            following += [carry[2 * row] + dhat, carry[2 * row + 1] + dhat * hat]
        for i, total in enumerate(totals):
            sums[i:i + 1, cols] = total
        return tuple(following)

    zero = jnp.zeros((each, LANES), F32)
    done = lax.fori_loop(0, width // LANES, gather, (zero,) * (2 * rows))
    for row, at in enumerate(spans):
        for ref, value in ((first, done[2 * row]), (second, done[2 * row + 1])):
            ref[at, :] = jnp.broadcast_to(jnp.sum(value, axis=1, keepdims=True) * (1.0 / width), (each, LANES))

    def finish(c, _):
        cols = lanes(c)
        for at in spans:
            hat = (source[at, cols].astype(F32) - mean[at, :]) * scale[at, :]
            out = residual[at, cols].astype(F32) + scale[at, :] * (hats[at, cols] - first[at, :] - hat * second[at, :])
            for t in targets:
                t[at, cols] = out.astype(t.dtype)
        return 0

    lax.fori_loop(0, width // LANES, finish, 0)


def channel_kernel(rows, times, *refs):
    (same, factor_out, factor_gate, g, g2, b2, ck, cr, rect_in, middle_in, fv_in, fk_in, fr_in) = refs[:13]
    n_out = 6
    outs = refs[13:13 + n_out]
    (fv, fk, fr, rect, middle, delta_out, delta_gate, delta_pre, dh, dg, mean, scale, first, second, hats, delta, branch, sums, in_sems, out_sems) = refs[13 + n_out:]
    tokens, width = g.shape
    ff = rect.shape[1]
    tile = 1024
    chunks = ff // tile
    first_loads = []
    for j in range(chunks):
        span = slice(j * tile, (j + 1) * tile)
        first_loads += [(fv_in.at[span, :], fv.at[span, :]), (rect_in.at[:, span], rect.at[:, span])]
    sums[...] = jnp.zeros_like(sums)
    loads = fetch(first_loads + [(fr_in, fr), (fk_in, fk), (middle_in, middle)], in_sems)
    saves = []
    def save(source, i):
        saves.append(pltpu.make_async_copy(source, outs[i], out_sems.at[i]))
        saves[-1].start()
    def cols_of(j):
        return pl.ds(pl.multiple_of(j * tile, tile), tile)
    if times:
        def scale_tile(j, _):
            cols = lanes(j)
            x = g[:, cols].astype(F32)
            delta_out[:, cols] = (x * factor_out[:, cols].astype(F32)).astype(BF)
            delta_gate[:, cols] = (x * factor_gate[:, cols].astype(F32)).astype(BF)
            return 0
        lax.fori_loop(0, width // LANES, scale_tile, 0)
        left_out, left_gate = delta_out, delta_gate
    else:
        left_out, left_gate = factor_out, factor_gate
    def pre_tile(j, _):
        cols = cols_of(j)
        pltpu.make_async_copy(fv_in.at[cols, :], fv.at[cols, :], in_sems.at[2 * j]).wait()
        pltpu.make_async_copy(rect_in.at[:, cols], rect.at[:, cols], in_sems.at[2 * j + 1]).wait()
        d = dot_nt(left_out[...], fv[cols, :])
        delta_pre[:, cols] = (d * (2.0 * jnp.sqrt(rect[:, cols].astype(F32)))).astype(BF)
        return 0
    lax.fori_loop(0, ff // tile, pre_tile, 0)
    save(delta_pre, 0)
    if times:
        save(delta_out, 4)
        save(delta_gate, 5)
    loads[-1].wait()
    statistics(middle, mean, scale, tokens, width)
    loads[-2].wait()
    loads[-3].wait()
    def hidden_tile(j, _):
        cols = cols_of(j)
        dh[:, cols] = dot_nt(delta_pre[...], fk[cols, :])
        dg[:, cols] = dot_nt(left_gate[...], fr[cols, :])
        return 0
    lax.fori_loop(0, width // tile, hidden_tile, 0)
    norm_backward(middle, mean, scale, same, g2, b2, (ck, cr), (dh, dg), g, (delta, branch), sums, hats, first, second, rows)
    save(delta, 1)
    save(branch, 2)
    save(sums, 3)
    for c in saves:
        c.wait()

def channel(rows, times, same, factor_out, factor_gate, g, p, rect, middle):
    (g1, b1, fade, bonus, mk, mv, mr, wk, wv, wr, wo, g2, b2, ck, cr, fk, fr, fv) = p
    tokens, width = g.shape
    ff = fk.shape[1]
    vm = pl.BlockSpec(memory_space=pltpu.VMEM)
    hbm = pl.BlockSpec(memory_space=pl.ANY)
    outs = [((tokens, ff), BF), ((tokens, width), F32), ((tokens, width), BF), ((8, width), F32)]
    outs += [((tokens, width), BF)] * 2 if times else [((16, LANES), BF)] * 2
    wide, wide32 = pltpu.VMEM((tokens, width), BF), pltpu.VMEM((tokens, width), F32)
    stat = pltpu.VMEM((tokens, LANES), F32)
    big = pltpu.VMEM((tokens, ff), BF)
    scratch = [pltpu.VMEM((ff, width), BF), pltpu.VMEM((width, ff), BF), pltpu.VMEM((width, width), BF), big, wide32, wide, wide, big, wide32, wide32]
    scratch += [stat] * 4 + [wide32, wide32, wide, pltpu.VMEM((8, width), F32), pltpu.SemaphoreType.DMA((2 * ff // 1024 + 3,)), pltpu.SemaphoreType.DMA((6,))]
    return pl.pallas_call(
        functools.partial(channel_kernel, rows, times),
        out_shape=tuple(jax.ShapeDtypeStruct(*o) for o in outs),
        in_specs=[vm] * 8 + [hbm] * 5,
        out_specs=(hbm,) * 6,
        scratch_shapes=scratch,
        compiler_params=pltpu.CompilerParams(vmem_limit_bytes=60 << 20),
        cost_estimate=pl.CostEstimate(flops=75000000000, bytes_accessed=217500000, transcendentals=0),
        name="channel",
    )(same, factor_out, factor_gate, g, g2, b2, ck, cr, rect, middle, fv, fk, fr)

def time_kernel(rows, *refs):
    (same_s, same, branch, h, g1, b1, fade, bonus, mk, mv, mr, wo_in, gate_in, ks_in, vs_in, tops_in, bottoms_in, wk_in, wv_in, wr_in, delta_in) = refs[:21]
    n_out = 5
    outs = refs[21:21 + n_out]
    (wo, gate, ks, vs, wk, wv, wr, delta, dm, gs, ys, tops, bottoms, dks, dvs, dk, dv, dr, ik, iv, ir, mean, scale, first, second, hats, state, sums, in_sems, out_sems) = refs[21 + n_out:]
    tokens, width = h.shape
    each = tokens // rows
    parts = width // LANES
    tile = 1024
    sums[...] = jnp.zeros_like(sums)
    loads = fetch([(wo_in, wo), (gate_in, gate), (ks_in, ks), (vs_in, vs), (tops_in, tops), (bottoms_in, bottoms), (wk_in, wk), (wv_in, wv), (wr_in, wr), (delta_in, delta)], in_sems)
    saves = []
    def save(source, i):
        saves.append(pltpu.make_async_copy(source, outs[i], out_sems.at[i]))
        saves[-1].start()
    def cols_of(j):
        return pl.ds(pl.multiple_of(j * tile, tile), tile)
    statistics(h, mean, scale, tokens, width)
    loads[0].wait()
    loads[1].wait()
    def mixed_tile(j, _):
        cols = cols_of(j)
        d = dot_nt(branch[...], wo[cols, :])
        dm[:, cols] = d
        e = d * gate[:, cols]
        for row in range(rows):
            for c in range(tile // LANES):
                gs[pl.ds(row * each * parts + j * (tile // LANES) + c, each, stride=parts), :] = e[row * each:(row + 1) * each, c * LANES:(c + 1) * LANES]
        return 0
    lax.fori_loop(0, width // tile, mixed_tile, 0)
    for i in (2, 3, 4, 5):
        loads[i].wait()
    rate = jnp.exp(fade[...])
    decay = jnp.exp(-rate)
    extra = bonus[...]
    zero = jnp.zeros(decay.shape, F32)
    def back(i, carry):
        t = each - 1 - i
        dw, du = carry[:2]
        following = []
        for row in range(rows):
            here = pl.ds(pl.multiple_of((row * each + t) * parts, parts), parts)
            a, b = carry[2 + 2 * row], carry[3 + 2 * row]
            k, v = ks[here, :], vs[here, :]
            ek, now = jnp.exp(k), jnp.exp(extra + k)
            inverse = 1.0 / (bottoms[here, :] + now)
            y = (tops[here, :] + now * v) * inverse
            ys[here, :] = y
            ga = gs[here, :] * inverse
            gb = -ga * y
            q = now * (v * ga + gb)
            dks[here, :] = ek * (v * a + b) + q
            dvs[here, :] = ek * a + now * ga
            du = du + q
            dw = dw + (a * tops[here, :] + b * bottoms[here, :])
            m = same_s[row, t]
            following += [(ga + decay * a) * m, (gb + decay * b) * m]
        return (dw, du, *following)
    done = lax.fori_loop(0, each, back, (zero,) * (2 + 2 * rows), unroll=4)
    dfade = -done[0] * decay * rate
    for c in range(parts):
        sums[5:6, c * LANES:(c + 1) * LANES] = dfade[c:c + 1, :]
        sums[6:7, c * LANES:(c + 1) * LANES] = done[1][c:c + 1, :]
    for row in range(rows):
        def out_step(c, _, row=row):
            span = slice(row * each, (row + 1) * each)
            cols = lanes(c)
            at = pl.ds(row * each * parts + c, each, stride=parts)
            dk[span, cols] = dks[at, :].astype(BF)
            dv[span, cols] = dvs[at, :].astype(BF)
            s = gate[span, cols]
            dr[span, cols] = (dm[span, cols] * ys[at, :] * s * (1.0 - s)).astype(BF)
            return 0
        lax.fori_loop(0, parts, out_step, 0)
    for i, z in enumerate((dk, dv, dr)):
        save(z, i)
    for i in (6, 7, 8):
        loads[i].wait()
    def in_tile(j, _):
        cols = cols_of(j)
        ik[:, cols] = dot_nt(dk[...], wk[cols, :])
        iv[:, cols] = dot_nt(dv[...], wv[cols, :])
        ir[:, cols] = dot_nt(dr[...], wr[cols, :])
        return 0
    lax.fori_loop(0, width // tile, in_tile, 0)
    loads[9].wait()
    norm_backward(h, mean, scale, same, g1, b1, (mk, mv, mr), (ik, iv, ir), delta, (state,), sums, hats, first, second, rows)
    save(state, 3)
    save(sums, 4)
    for c in saves:
        c.wait()

def time_mix(rows, dtype, same_s, same, branch, delta, h, p, gate, ks, vs, tops, bottoms):
    (g1, b1, fade, bonus, mk, mv, mr, wk, wv, wr, wo, g2, b2, ck, cr, fk, fr, fv) = p
    tokens, width = h.shape
    vm = pl.BlockSpec(memory_space=pltpu.VMEM)
    hbm = pl.BlockSpec(memory_space=pl.ANY)
    outs = [((tokens, width), BF)] * 3 + [((tokens, width), dtype), ((8, width), F32)]
    wide, wide32 = pltpu.VMEM((tokens, width), BF), pltpu.VMEM((tokens, width), F32)
    step32 = pltpu.VMEM(ks.shape, F32)
    stat = pltpu.VMEM((tokens, LANES), F32)
    square = pltpu.VMEM((width, width), BF)
    scratch = [square, wide32, step32, step32, square, square, square, wide32, wide32] + [step32] * 6 + [wide] * 3 + [wide32] * 3 + [stat] * 4 + [wide32]
    scratch += [pltpu.VMEM((tokens, width), dtype), pltpu.VMEM((8, width), F32), pltpu.SemaphoreType.DMA((10,)), pltpu.SemaphoreType.DMA((5,))]
    return pl.pallas_call(
        functools.partial(time_kernel, rows),
        out_shape=tuple(jax.ShapeDtypeStruct(*o) for o in outs),
        in_specs=[pl.BlockSpec(memory_space=pltpu.SMEM)] + [vm] * 10 + [hbm] * 10,
        out_specs=(hbm,) * 5,
        scratch_shapes=scratch,
        compiler_params=pltpu.CompilerParams(vmem_limit_bytes=60 << 20),
        cost_estimate=pl.CostEstimate(flops=87000000000, bytes_accessed=252300000, transcendentals=0),
        name="time_mix",
    )(same_s, same, branch, h, g1, b1, fade, bonus, mk, mv, mr, wo, gate, ks, vs, tops, bottoms, wk, wv, wr, delta)


UNIT = 1024


def starts(parts):
    return [sum(c for c, _ in parts[:i]) for i in range(len(parts))]


def terms_kernel(count, parts, shapes, with_sums, with_factor, *refs):
    bits, refs = refs[0], refs[1:]
    if with_factor:
        factor, refs = refs[0], refs[1:]
    n, np_ = len(shapes), len(parts)
    left_in, right_in, refs = refs[:n], refs[n:2 * n], refs[2 * n:]
    if with_sums:
        early, late, *refs = refs
    outs, refs = refs[:2 * np_], refs[2 * np_:]
    lefts, rights, refs = refs[:n], refs[n:2 * n], refs[2 * n:]
    bufs, (in_sems, out_sems) = refs[:np_], refs[np_:]
    sends, keeps = outs[::2], outs[1::2]
    tile = 512
    columns = starts(parts)

    def place(order, d):
        bit = [(d >> b) & 1 if isinstance(d, int) else lax.rem(lax.div(d, 1 << b), 2) for b in order]
        return bit[0] ^ bits[order[0]], bit[1] * 4 + bit[2] * 2 + bit[3]

    chunk_base = [sum(kin // tile for kin, _ in shapes[:m]) for m in range(n)]

    def load(m, j):
        cols = pl.ds(pl.multiple_of(j * tile, tile), tile)
        return pltpu.make_async_copy(left_in[m].at[:, cols], lefts[m].at[:, cols], in_sems.at[chunk_base[m] + j])

    right_base = [chunk_base[-1] + shapes[-1][0] // tile + sum(width // UNIT for _, width in shapes[:m]) for m in range(n)]

    def load_right(m, q):
        cols = slice(q * UNIT, (q + 1) * UNIT)
        return pltpu.make_async_copy(right_in[m].at[:, cols], rights[m].at[:, cols], in_sems.at[right_base[m] + q])

    for m, (kin, width) in enumerate(shapes):
        load_right(m, 0).start()
        for j in range(kin // tile):
            load(m, j).start()
        for q in range(1, width // UNIT):
            load_right(m, q).start()
    waits = []
    base = 0
    blocks = 0
    for m, ((kin, width), left, right) in enumerate(zip(shapes, lefts, rights)):
        rows = kin // count
        per = tile // rows
        for q in range(width // UNIT):
            load_right(m, q).wait()
            if with_factor:
                right[...] = (right[...].astype(F32) * factor[...].astype(F32)).astype(BF)

            def step(j, _, m=m, q=q, left=left, right=right, rows=rows, per=per, base=base):
                if q == 0:
                    load(m, j).wait()
                lhs = left[:, pl.ds(pl.multiple_of(j * tile, tile), tile)]
                for i, (cols, order) in enumerate(parts):
                    at = q * UNIT + columns[i]
                    res = lax.dot_general(lhs, right[:, at:at + cols], (((0,), (0,)), ((), ())), preferred_element_type=F32).astype(BF)
                    for s in range(per):
                        relative, index = place(order, j * per + s)
                        bufs[i][relative, index, base:base + rows, :] = res[s * rows:(s + 1) * rows]
                        if rows >= 256:
                            source = bufs[i].at[relative, index]
                            for r, target in ((1, sends[i]), (0, keeps[i])):
                                @pl.when(relative == r)
                                def _(source=source, target=target, index=index, i=i):
                                    pltpu.make_async_copy(source, target.at[index], out_sems.at[i, j * per + s]).start()
                return 0

            lax.fori_loop(0, kin // tile, step, 0)
            for i in range(np_):
                if rows >= 256:
                    for j in range(count):
                        waits.append(pltpu.make_async_copy(bufs[i].at[0, 0], keeps[i].at[0], out_sems.at[i, j]))
                else:
                    for r, target in ((1, sends[i]), (0, keeps[i])):
                        c = pltpu.make_async_copy(bufs[i].at[r, :, base:base + rows, :], target.at[:, base:base + rows, :], out_sems.at[i, 2 * blocks + r])
                        c.start()
                        waits.append(c)
            base += rows
            blocks += 1
    if with_sums:
        share = early.shape[1] // count
        both = jnp.concatenate([early[...], late[...]], axis=0)
        for buf in bufs:
            buf[:, :, base:base + 16, :] = jnp.zeros(buf.shape[:2] + (16, buf.shape[3]), BF)
        for d in range(count):
            column = d * share // LANES * LANES
            piece = both[:, column:column + LANES]
            if d * share - column:
                piece = pltpu.roll(piece, LANES - (d * share - column), 1)
            relative, index = place(parts[0][1], d)
            bufs[0][relative, index, base:base + 16, 0:LANES] = piece.astype(BF)
        for i in range(np_):
            for r, target in ((1, sends[i]), (0, keeps[i])):
                c = pltpu.make_async_copy(bufs[i].at[r, :, base:base + 16, :], target.at[:, base:base + 16, :], out_sems.at[i, 2 * blocks + r])
                c.start()
                waits.append(c)
    for c in waits:
        c.wait()


def terms(bits, parts, pairs, sums=(), factor=None):
    count = 16
    lefts, rights = zip(*pairs)
    shapes = tuple((a.shape[1], b.shape[1]) for a, b in pairs)
    tokens = lefts[0].shape[0]
    rows = sum(kin // count * (width // UNIT) for kin, width in shapes) + (16 if sums else 0)
    outs, bufs = [], []
    for cols, _ in parts:
        outs += [jax.ShapeDtypeStruct((count // 2, rows, cols), BF)] * 2
        bufs.append(pltpu.VMEM((2, count // 2, rows, cols), BF))
    flops = sum(2 * tokens * kin * width for kin, width in shapes)
    result = pl.pallas_call(
        functools.partial(terms_kernel, count, parts, shapes, bool(sums), factor is not None),
        out_shape=tuple(outs),
        in_specs=[SM] + [VM] * (factor is not None) + [HBM] * (2 * len(shapes)) + [VM] * len(sums),
        out_specs=(HBM,) * len(outs),
        scratch_shapes=[pltpu.VMEM(x.shape, BF) for x in (*lefts, *rights)]
        + bufs + [pltpu.SemaphoreType.DMA((sum(kin // 512 + width // UNIT for kin, width in shapes),)), pltpu.SemaphoreType.DMA((len(parts), 16))],
        compiler_params=pltpu.CompilerParams(vmem_limit_bytes=56 << 20),
        cost_estimate=pl.CostEstimate(flops=39000000000, bytes_accessed=113100000, transcendentals=0),
        name="terms",
    )(bits, *(() if factor is None else (factor,)), *lefts, *rights, *sums)
    return list(zip(result[::2], result[1::2]))


def swap(block, bit):
    count = lax.axis_size("dp")
    return lax.ppermute(block, "dp", [(i, i ^ (1 << bit)) for i in range(count)])


def summed(kept, came, dtype=BF):
    return (kept.astype(F32) + came.astype(F32)).astype(dtype)


def advance_kernel(bits, kept_go, came_go, kept_stay, came_stay, send, keep):
    send[...] = summed(kept_go[...], came_go[...])
    keep[...] = summed(kept_stay[...], came_stay[...])


def advance(bits, kept, came, bit):
    lead, rows, cols = kept.shape
    half = lead // 2
    block = rows
    go = pl.BlockSpec((1, block, cols), lambda g, i, b: ((1 - b[bit]) * half + g, i, 0))
    stay = pl.BlockSpec((1, block, cols), lambda g, i, b: (b[bit] * half + g, i, 0))
    out = pl.BlockSpec((1, block, cols), lambda g, i, b: (g, i, 0))
    return pl.pallas_call(
        advance_kernel,
        out_shape=(jax.ShapeDtypeStruct((half, rows, cols), BF),) * 2,
        grid_spec=pltpu.PrefetchScalarGridSpec(
            num_scalar_prefetch=1, grid=(half, rows // block), in_specs=[go, go, stay, stay], out_specs=(out, out)
        ),
        compiler_params=pltpu.CompilerParams(vmem_limit_bytes=30 << 20),
        cost_estimate=pl.CostEstimate(flops=9000000000, bytes_accessed=26100000, transcendentals=0),
        name="advance",
    )(bits, kept, came, kept, came)


def final_kernel(pieces, parts, *refs):
    n = len(parts)
    ins, outs = refs[:2 * n], refs[2 * n:]
    for (row, rows, blocks, columns), out in zip(pieces, outs):
        for q in range(blocks):
            span = slice(row + q * rows, row + (q + 1) * rows)
            if columns < UNIT:
                out[...] = summed(ins[0][0, span, 0:LANES], ins[1][0, span, 0:LANES], F32)[:, :columns]
                continue
            for i, at in enumerate(starts(parts)):
                out[:, q * UNIT + at:q * UNIT + at + parts[i][0]] = summed(ins[2 * i][0, span, :], ins[2 * i + 1][0, span, :], F32)


def final(parts, pieces, arrays):
    size = sum(a.size for a in arrays)
    return pl.pallas_call(
        functools.partial(final_kernel, pieces, parts),
        out_shape=tuple(jax.ShapeDtypeStruct((rows, blocks * columns), F32) for row, rows, blocks, columns in pieces),
        in_specs=[VM] * len(arrays),
        out_specs=(VM,) * len(pieces),
        compiler_params=pltpu.CompilerParams(vmem_limit_bytes=40 << 20),
        cost_estimate=pl.CostEstimate(flops=4500000000, bytes_accessed=13050000, transcendentals=0),
        name="final",
    )(*arrays)


def after(value, *earlier):
    return lax.optimization_barrier((value, earlier))[0]


class Line:
    def __init__(self, bits, plan, pieces):
        self.bits, self.plan, self.pieces, self.token, self.flight, self.sums = bits, plan, pieces, None, {}, {}

    def tie(self, value):
        return value if self.token is None else after(value, self.token)

    def open(self, group, pairs, sums=(), factor=None):
        pairs = ((self.tie(pairs[0][0]), pairs[0][1]),) + tuple(pairs[1:])
        found = terms(self.bits, self.plan[group], pairs, sums, factor)
        self.token = found
        for i, (send, keep) in enumerate(found):
            self.flight[group, i] = keep, swap(send, self.plan[group][i][1][0])

    def serve(self, steps):
        for group, i, stage in steps:
            parts = self.plan[group]
            if stage < 4:
                kept, came = self.tie(self.flight[group, i])
                send, keep = advance(self.bits, kept, came, parts[i][1][stage])
                self.token = send, keep
                self.flight[group, i] = keep, swap(send, parts[i][1][stage])
            else:
                self.sums[group, i] = self.flight.pop((group, i))
                if all((group, k) in self.sums for k in range(len(parts))):
                    arrays = [a for k in range(len(parts)) for a in self.sums[group, k]]
                    arrays[0] = self.tie(arrays[0])
                    self.sums[group] = final(parts, self.pieces[group], arrays)
                    self.token = self.sums[group][0]


def halving(left, right=None):
    count = lax.axis_size("dp")
    bits = count.bit_length() - 1
    me = lax.axis_index("dp")
    if right is not None:
        left = lax.dot_general(left, right, (((0,), (0,)), ((), ())), preferred_element_type=F32).astype(BF)
    current = left.reshape((2,) * bits + (left.shape[0] // count, left.shape[1]))
    for bit in range(bits):
        axis = bits - 1 - bit
        mine = (me >> bit) & 1
        send = lax.dynamic_index_in_dim(current, 1 - mine, axis, keepdims=False)
        keep = lax.dynamic_index_in_dim(current, mine, axis, keepdims=False)
        current = summed(keep, swap(send, bit), BF if bit + 1 < bits else F32)
    return current


def unwritten(function, *args):
    shapes, tree = jax.tree.flatten(jax.eval_shape(function, *args))
    outs = pl.pallas_call(
        lambda *refs: None, out_shape=tuple(shapes), out_specs=(HBM,) * len(shapes), name="unwritten"
    )()
    return jax.tree.unflatten(tree, outs)


VECTORS = (0, 1, 5, 6, 2, 3, 4, 8, 9, 10, 11)
PARTS_0 = dict(
    a=((512, (2, 1, 0, 3)), (512, (1, 0, 2, 3))),
    b=((512, (1, 0, 2, 3)), (512, (2, 1, 0, 3))),
    e=((512, (1, 0, 2, 3)), (512, (0, 1, 2, 3))),
)
PARTS_1 = dict(
    a=((512, (0, 1, 2, 3)), (512, (2, 0, 1, 3))),
    b=((512, (0, 2, 3, 1)), (512, (2, 0, 1, 3))),
    e=((512, (0, 1, 2, 3)), (512, (1, 0, 2, 3))),
)
STEPS_0 = (
    (),
    (('a', 0, 1), ('a', 1, 1)),
    (('a', 1, 2), ('b', 0, 1), ('a', 0, 2), ('b', 1, 1), ('a', 1, 3), ('e', 1, 1), ('e', 0, 1), ('a', 1, 4), ('b', 0, 2), ('a', 0, 3), ('b', 1, 2), ('e', 0, 2), ('e', 1, 2), ('b', 0, 3), ('a', 0, 4), ('b', 1, 3), ('e', 0, 3), ('e', 1, 3), ('b', 0, 4), ('b', 1, 4), ('e', 0, 4), ('e', 1, 4)),
)
STEPS_1 = (
    (),
    (('a', 0, 1), ('a', 1, 1)),
    (),
    (('a', 0, 2), ('a', 1, 2), ('b', 0, 1), ('e', 1, 1), ('a', 1, 3), ('b', 1, 1), ('e', 0, 1), ('a', 0, 3), ('e', 1, 2), ('e', 0, 2), ('b', 0, 2), ('b', 1, 2), ('a', 0, 4), ('a', 1, 4), ('e', 1, 3), ('e', 0, 3), ('b', 1, 3), ('e', 1, 4), ('b', 0, 3), ('e', 0, 4), ('b', 0, 4), ('b', 1, 4)),
)


def local(entry_pair, labels, *params):
    count = lax.axis_size("dp")
    section = lax.axis_index("section")
    rows, each, width = entry_pair.shape[1:]
    own = entry_pair.reshape(rows * each, width)
    share = width // count
    p = [e if e.ndim == 2 else e[0] for e in params]
    ff = p[15].shape[1]
    for i in (2, 3):
        p[i] = p[i].reshape(width // LANES, LANES).astype(F32)
    first = jnp.zeros((rows, 1), F32)
    same_s = jnp.concatenate([first, (labels[:, 1:] == labels[:, :-1]).astype(F32)], axis=1)
    same = jnp.broadcast_to(same_s.reshape(rows * each, 1), (rows * each, LANES))
    fast = count == 16 and width == UNIT
    me = lax.axis_index("dp")
    bits = jnp.stack([(me >> i) & 1 for i in range(4)])
    wide = ff // width
    pieces = dict(
        a=((0, ff // count, 1, width),),
        b=((0, share, wide, width), (share * wide, share, 1, width), (share * (wide + 1), share, 1, width)),
        e=tuple((i * share, share, 1, width) for i in range(3)) + tuple((3 * share + i, 1, 1, share) for i in VECTORS),
    )

    def plain_rest(pairs, sums):
        together = jnp.concatenate(sums).astype(BF).reshape(16, count, share).transpose(1, 0, 2).reshape(count * 16, share)
        vectors = halving(together)
        return tuple(halving(*pair) for pair in pairs) + tuple(vectors[i:i + 1] for i in VECTORS)

    def start():
        return forward(rows, False, same_s, same, own, p, own)

    def middle_part(received):
        kept = forward(rows, True, same_s, same, received, p, own)
        (key_in, value_in, recept_in, ks, vs, gate, tops, bottoms, mixed, middle, hidden_in, gate_in, act, result, delta_out, delta_gate) = kept
        line = Line(bits, PARTS_1, pieces)
        if fast:
            line.open("a", ((act, delta_out),))
        delta_pre, delta, branch, late, _, _ = channel(rows, False, same, delta_out, delta_gate, line.tie(own), p, act, middle)
        line.token = branch
        if fast:
            line.serve(STEPS_1[0])
        dk, dv, dr, state, early = time_mix(rows, BF, same_s, same, line.tie(branch), delta, received, p, gate, ks, vs, tops, bottoms)
        key_pairs = ((hidden_in, delta_pre), (gate_in, delta_gate), (mixed, branch))
        begun = list(line.flight.values()) if fast else (act, delta_out)
        return state, result, begun, (early, late), key_pairs, ((key_in, dk), (value_in, dv), (recept_in, dr))

    def end_first(received, kept):
        (key_in, value_in, recept_in, ks, vs, gate, tops, bottoms, mixed, middle, hidden_in, gate_in, act, result, factor_out, factor_gate) = kept
        line = Line(bits, PARTS_0, pieces)
        if fast:
            line.open("a", ((act, received),), factor=factor_out)
        g = line.tie(received)
        delta_pre, delta, branch, late, delta_out, delta_gate = channel(rows, True, same, factor_out, factor_gate, g, p, act, middle)
        key_pairs = ((hidden_in, delta_pre), (gate_in, delta_gate), (mixed, branch))
        line.token = branch
        if fast:
            line.serve(STEPS_0[0])
            line.open("b", key_pairs)
            line.serve(STEPS_0[1])
        dk, dv, dr, state, early = time_mix(rows, F32, same_s, same, line.tie(branch), delta, own, p, gate, ks, vs, tops, bottoms)
        rest_pairs = ((key_in, dk), (value_in, dv), (recept_in, dr))
        if not fast:
            return state, (halving(act, delta_out),), tuple(halving(*pair) for pair in key_pairs), plain_rest(rest_pairs, (early, late))
        line.token = state
        line.open("e", rest_pairs, (early, late))
        line.serve(STEPS_0[2])
        return state, line.sums["a"], line.sums["b"], line.sums["e"]

    def end_second(result, begun, sums, key_pairs, rest_pairs):
        if not fast:
            return result.astype(F32), (halving(*begun),), tuple(halving(*pair) for pair in key_pairs), plain_rest(rest_pairs, sums)
        line = Line(bits, PARTS_1, pieces)
        line.flight = {("a", i): pair for i, pair in enumerate(begun)}
        line.serve(STEPS_1[1])
        line.open("b", key_pairs)
        line.serve(STEPS_1[2])
        line.open("e", rest_pairs, sums)
        line.serve(STEPS_1[3])
        return result.astype(F32), line.sums["a"], line.sums["b"], line.sums["e"]

    kept = lax.cond(section == 0, start, lambda: unwritten(start))
    received = lax.ppermute(kept[13], "section", [(0, 1)])
    delta, *pending = lax.cond(section == 1, middle_part, lambda r: unwritten(middle_part, r), received)
    received = lax.ppermute(delta, "section", [(1, 0)])
    ends, (value_sum,), (key_sum, gate_sum, exit_sum), rest = lax.cond(
        section == 0, lambda r, k, q: end_first(r, k), lambda r, k, q: end_second(*q), received, kept, pending
    )
    ends = ends.reshape(rows, each, width)
    everything = (ends, *(z[0] for z in rest[3:10]), *rest[:3], exit_sum, *(z[0] for z in rest[10:14]), key_sum, gate_sum, value_sum)
    return tuple(e[None] for e in everything)


def solution(mesh):
    vec, mat = P("section", None), P("section", None, None)
    in_specs = (P("section", "dp", None, None), P("dp", None)) + (vec,) * 7 + (mat,) * 4 + (vec,) * 4 + (mat,) * 3
    vec, mat = P("section", "dp"), P("section", "dp", None)
    out_specs = (P("section", "dp", None, None),) + (vec,) * 7 + (mat,) * 4 + (vec,) * 4 + (mat,) * 3
    return jax.shard_map(local, mesh=mesh, in_specs=in_specs, out_specs=out_specs, check_vma=False)
```

```python
import functools

import jax
import jax.numpy as jnp
from jax import lax
from jax.experimental import pallas as pl
from jax.experimental.pallas import tpu as pltpu
from jax.sharding import PartitionSpec as P

BF = jnp.bfloat16
F32 = jnp.float32
LANES = 128
VM = pl.BlockSpec(memory_space=pltpu.VMEM)
HBM = pl.BlockSpec(memory_space=pl.ANY)
SM = pl.BlockSpec(memory_space=pltpu.SMEM)

def dot(left, right):
    return jnp.dot(left, right, preferred_element_type=F32)

def dot_nt(left, right):
    return lax.dot_general(left, right, (((1,), (1,)), ((), ())), preferred_element_type=F32)

def lanes(c):
    return pl.ds(pl.multiple_of(c * LANES, LANES), LANES)

def slabs(vector, scratch):
    for c in range(scratch.shape[0]):
        scratch[c:c + 1, :] = vector[:, c * LANES:(c + 1) * LANES].astype(F32)
    return scratch[...]

def statistics(source, mean, scale, tokens, width, chunk=128):
    def step(i, _):
        at = pl.ds(pl.multiple_of(i * chunk, chunk), chunk)
        x = source[at, :].astype(F32)
        m = jnp.sum(x, axis=1, keepdims=True) * (1.0 / width)
        x = x - m
        v = jnp.sum(x * x, axis=1, keepdims=True) * (1.0 / width)
        mean[at, :] = jnp.broadcast_to(m, (chunk, LANES))
        scale[at, :] = jnp.broadcast_to(lax.rsqrt(v + 1e-05), (chunk, LANES))
        return 0
    lax.fori_loop(0, tokens // chunk, step, 0)

def mix_into(source, mean, scale, same, gain, bias, factors, targets, width):
    def step(c, _):
        cols = lanes(c)
        z = (source[:, cols].astype(F32) - mean[...]) * scale[...] * gain[:, cols].astype(F32) + bias[:, cols].astype(F32)
        before = pltpu.roll(z, 1, 0) * same[...]
        step_up = z - before
        for factor, target in zip(factors, targets):
            target[:, cols] = (before + step_up * factor[:, cols].astype(F32)).astype(BF)
        return 0
    lax.fori_loop(0, width // LANES, step, 0)

def fetch(pairs, sems):
    copies = [pltpu.make_async_copy(s, d, sems.at[i]) for i, (s, d) in enumerate(pairs)]
    for c in copies:
        c.start()
    return copies

def forward_kernel(rows, with_delta, *refs):
    (same_s, same, h, g1, b1, fade, bonus, mk, mv, mr, g2, b2, ck, cr, cot) = refs[:15]
    weights = refs[15:22]
    n_out = 20
    outs = refs[22:22 + n_out]
    (wk, wv, wr, wo, fk, fr, fv, mean, scale, mean2, scale2, key_in, value_in, recept_in, ks, vs, ys, tops, bottoms, gate, mixed, middle,
     hidden_in, gate_in, act, slab, in_sems, out_sems) = refs[22 + n_out:]
    tokens, width = h.shape
    each = tokens // rows
    parts = width // LANES
    tile = 1024
    ff = act.shape[1]
    loads = fetch(list(zip(weights, (wk, wv, wr, wo, fk, fr, fv))), in_sems)
    saves = []

    def save(source):
        i = len(saves)
        saves.append(pltpu.make_async_copy(source, outs[i], out_sems.at[i]))
        saves[-1].start()

    statistics(h, mean, scale, tokens, width)
    mix_into(h, mean, scale, same, g1, b1, (mk, mv, mr), (key_in, value_in, recept_in), width)
    for z in (key_in, value_in, recept_in):
        save(z)

    def cols_of(j):
        return pl.ds(pl.multiple_of(j * tile, tile), tile)

    def steps_tile(values, target, j):
        for row in range(rows):
            for c in range(tile // LANES):
                target[pl.ds(row * each * parts + j * (tile // LANES) + c, each, stride=parts), :] = values[row * each:(row + 1) * each, c * LANES:(c + 1) * LANES]

    loads[0].wait()
    def key_tile(j, _):
        steps_tile(dot(key_in[...], wk[:, cols_of(j)]), ks, j)
        return 0
    lax.fori_loop(0, width // tile, key_tile, 0)
    loads[1].wait()
    def value_tile(j, _):
        steps_tile(dot(value_in[...], wv[:, cols_of(j)]), vs, j)
        return 0
    lax.fori_loop(0, width // tile, value_tile, 0)
    save(ks)
    save(vs)
    loads[2].wait()
    def accept_tile(j, _):
        gate[:, cols_of(j)] = jax.nn.sigmoid(dot(recept_in[...], wr[:, cols_of(j)]))
        return 0
    lax.fori_loop(0, width // tile, accept_tile, 0)
    save(gate)

    decay = jnp.exp(-jnp.exp(slabs(fade, slab)))
    extra = slabs(bonus, slab)
    def step(t, carry):
        following = []
        for row in range(rows):
            here = pl.ds(pl.multiple_of((row * each + t) * parts, parts), parts)
            m = same_s[row, t]
            top, bottom = carry[2 * row] * m, carry[2 * row + 1] * m
            tops[here, :] = top
            bottoms[here, :] = bottom
            k, v = ks[here, :], vs[here, :]
            ek, now = jnp.exp(k), jnp.exp(extra + k)
            ys[here, :] = (top + now * v) / (bottom + now)
            following += [decay * top + ek * v, decay * bottom + ek]
        return tuple(following)
    zero = jnp.zeros(decay.shape, F32)
    lax.fori_loop(0, each, step, (zero,) * (2 * rows), unroll=4)
    save(tops)
    save(bottoms)

    for row in range(rows):
        def mixed_step(c, _, row=row):
            y = ys[pl.ds(row * each * parts + c, each, stride=parts), :]
            mixed[row * each:(row + 1) * each, lanes(c)] = (gate[row * each:(row + 1) * each, lanes(c)] * y).astype(BF)
            return 0
        lax.fori_loop(0, parts, mixed_step, 0)
    save(mixed)
    loads[3].wait()
    def middle_tile(j, _):
        middle[:, cols_of(j)] = h[:, cols_of(j)].astype(F32) + dot(mixed[...], wo[:, cols_of(j)])
        return 0
    lax.fori_loop(0, width // tile, middle_tile, 0)
    save(middle)

    statistics(middle, mean2, scale2, tokens, width)
    mix_into(middle, mean2, scale2, same, g2, b2, (ck, cr), (hidden_in, gate_in), width)
    save(hidden_in)
    save(gate_in)
    loads[4].wait()
    def hidden_tile(j, _):
        r = jnp.maximum(dot(hidden_in[...], fk[:, cols_of(j)]), 0.0)
        act[:, cols_of(j)] = (r * r).astype(BF)
        return 0
    lax.fori_loop(0, ff // tile, hidden_tile, 0)
    save(act)
    for i in (0, 1, 2, 5):
        saves[i].wait()
    result, delta_out, delta_gate = key_in, value_in, recept_in
    loads[5].wait()
    def gate_tile(j, _):
        gate[:, cols_of(j)] = jax.nn.sigmoid(dot(gate_in[...], fr[:, cols_of(j)]))
        return 0
    lax.fori_loop(0, width // tile, gate_tile, 0)
    loads[6].wait()
    def out_tile(j, _):
        cols = cols_of(j)
        o = dot(act[...], fv[:, cols])
        s = gate[:, cols]
        result[:, cols] = (middle[:, cols] + s * o).astype(BF)
        g = cot[:, cols].astype(F32)
        if with_delta:
            delta_out[:, cols] = (g * s).astype(BF)
            delta_gate[:, cols] = (g * o * s * (1.0 - s)).astype(BF)
        else:
            delta_out[:, cols] = s.astype(BF)
            delta_gate[:, cols] = (o * s * (1.0 - s)).astype(BF)
        return 0
    lax.fori_loop(0, width // tile, out_tile, 0)
    save(result)
    save(delta_out)
    save(delta_gate)
    for z in (mean, scale, mean2, scale2):
        save(z)
    for i, c in enumerate(saves):
        if i not in (0, 1, 2, 5):
            c.wait()

def forward(rows, with_delta, same_s, same, h, p, cot):
    (g1, b1, fade, bonus, mk, mv, mr, wk, wv, wr, wo, g2, b2, ck, cr, fk, fr, fv) = p
    tokens, width = h.shape
    ff = fk.shape[1]
    vm = pl.BlockSpec(memory_space=pltpu.VMEM)
    hbm = pl.BlockSpec(memory_space=pl.ANY)
    slabs = tokens * width // LANES
    outs = [((tokens, width), BF)] * 3 + [((slabs, LANES), F32)] * 2 + [((tokens, width), F32)] + [((slabs, LANES), F32)] * 2
    outs += [((tokens, width), BF), ((tokens, width), F32)]
    outs += [((tokens, width), BF)] * 2 + [((tokens, ff), BF)] + [((tokens, width), BF)] * 3
    outs = outs[:14] if False else outs
    outs += [((tokens, LANES), F32)] * 4
    wide, wide32, step32 = pltpu.VMEM((tokens, width), BF), pltpu.VMEM((tokens, width), F32), pltpu.VMEM((slabs, LANES), F32)
    stat = pltpu.VMEM((tokens, LANES), F32)
    square = pltpu.VMEM((width, width), BF)
    big = pltpu.VMEM((tokens, ff), BF)
    scratch = [square] * 4 + [pltpu.VMEM((width, ff), BF), square, pltpu.VMEM((ff, width), BF), stat, stat, stat, stat] + [wide] * 3
    scratch += [step32] * 5 + [wide32, wide, wide32, wide, wide, big]
    scratch += [pltpu.VMEM((width // LANES, LANES), F32), pltpu.SemaphoreType.DMA((7,)), pltpu.SemaphoreType.DMA((len(outs),))]
    return pl.pallas_call(
        functools.partial(forward_kernel, rows, with_delta),
        out_shape=tuple(jax.ShapeDtypeStruct(*o) for o in outs),
        in_specs=[pl.BlockSpec(memory_space=pltpu.SMEM)] + [vm] * 14 + [hbm] * 7,
        out_specs=(hbm,) * len(outs),
        scratch_shapes=scratch,
        compiler_params=pltpu.CompilerParams(vmem_limit_bytes=60 << 20),
        cost_estimate=pl.CostEstimate(flops=90000000000, bytes_accessed=261000000, transcendentals=0),
        name="forward",
    )(same_s, same, h, g1, b1, fade, bonus, mk, mv, mr, g2, b2, ck, cr, cot, wk, wv, wr, wo, fk, fr, fv)

def norm_backward(source, mean, scale, same, gain, bias, factors, grads, residual, targets, sums, hats, first, second, rows, leave):
    tokens, width = source.shape
    each = tokens // rows
    spans = [slice(row * each, (row + 1) * each) for row in range(rows)]

    def gather(c, carry):
        cols = lanes(c)
        g, b = gain[:, cols].astype(F32), bias[:, cols].astype(F32)
        following = []
        totals = [0.0] * (2 + len(grads))
        for row, at in enumerate(spans):
            hat = (source[at, cols].astype(F32) - mean[at, :]) * scale[at, :]
            z = hat * g + b
            step_up = z - pltpu.roll(z, 1, 0) * same[at, :]
            straight = rest = None
            for i, (factor, grad) in enumerate(zip(factors, grads)):
                d = grad[at, cols]
                df = d * factor[:, cols].astype(F32)
                totals[2 + i] += jnp.sum(d * step_up, axis=0, keepdims=True)
                straight = df if i == 0 else straight + df
                rest = d - df if i == 0 else rest + (d - df)
            dz = straight + pltpu.roll(rest * same[at, :], each - 1, 0)
            totals[0] += jnp.sum(dz * hat, axis=0, keepdims=True)
            totals[1] += jnp.sum(dz, axis=0, keepdims=True)
            dhat = dz * g
            hats[at, cols] = dhat
            following += [carry[2 * row] + dhat, carry[2 * row + 1] + dhat * hat]
        for i, total in enumerate(totals):
            sums[i:i + 1, cols] = total
        return tuple(following)

    zero = jnp.zeros((each, LANES), F32)
    done = lax.fori_loop(0, width // LANES, gather, (zero,) * (2 * rows))
    for row, at in enumerate(spans):
        for ref, value in ((first, done[2 * row]), (second, done[2 * row + 1])):
            ref[at, :] = jnp.broadcast_to(jnp.sum(value, axis=1, keepdims=True) * (1.0 / width), (each, LANES))

    for at in spans:
        def finish(c, _, at=at):
            cols = lanes(c)
            hat = (source[at, cols].astype(F32) - mean[at, :]) * scale[at, :]
            out = residual[at, cols].astype(F32) + scale[at, :] * (hats[at, cols] - first[at, :] - hat * second[at, :])
            for t in targets:
                t[at, cols] = out.astype(t.dtype)
            return 0

        lax.fori_loop(0, width // LANES, finish, 0)
        leave(at)


def channel_kernel(rows, times, *refs):
    (same, factor_out, factor_gate, g, g2, b2, ck, cr, rect_in, middle_in, mean_in, scale_in, fv_in, fk_in, fr_in) = refs[:15]
    n_out = 6
    outs = refs[15:15 + n_out]
    (fv, fk, fr, rect, middle, delta_out, delta_gate, delta_pre, dh, dg, mean, scale, first, second, hats, delta, branch, sums, in_sems, out_sems, row_sems) = refs[15 + n_out:]
    tokens, width = g.shape
    ff = rect.shape[1]
    tile = 1024
    chunks = ff // tile
    first_loads = []
    for j in range(chunks):
        span = slice(j * tile, (j + 1) * tile)
        first_loads += [(fv_in.at[span, :], fv.at[span, :]), (rect_in.at[:, span], rect.at[:, span])]
    sums[...] = jnp.zeros_like(sums)
    loads = fetch(first_loads + [(fr_in, fr), (fk_in, fk), (middle_in, middle), (mean_in, mean), (scale_in, scale)], in_sems)
    saves = []
    def save(source, i):
        saves.append(pltpu.make_async_copy(source, outs[i], out_sems.at[i]))
        saves[-1].start()
    def cols_of(j):
        return pl.ds(pl.multiple_of(j * tile, tile), tile)
    if times:
        def scale_tile(j, _):
            cols = lanes(j)
            x = g[:, cols].astype(F32)
            delta_out[:, cols] = (x * factor_out[:, cols].astype(F32)).astype(BF)
            delta_gate[:, cols] = (x * factor_gate[:, cols].astype(F32)).astype(BF)
            return 0
        lax.fori_loop(0, width // LANES, scale_tile, 0)
        left_out, left_gate = delta_out, delta_gate
    else:
        left_out, left_gate = factor_out, factor_gate
    def pre_tile(j, _):
        cols = cols_of(j)
        pltpu.make_async_copy(fv_in.at[cols, :], fv.at[cols, :], in_sems.at[2 * j]).wait()
        pltpu.make_async_copy(rect_in.at[:, cols], rect.at[:, cols], in_sems.at[2 * j + 1]).wait()
        d = dot_nt(left_out[...], fv[cols, :])
        delta_pre[:, cols] = (d * (2.0 * jnp.sqrt(rect[:, cols].astype(F32)))).astype(BF)
        return 0
    lax.fori_loop(0, ff // tile, pre_tile, 0)
    save(delta_pre, 0)
    if times:
        save(delta_out, 4)
        save(delta_gate, 5)
    for c in loads[-5:]:
        c.wait()
    def hidden_tile(j, _):
        cols = cols_of(j)
        dh[:, cols] = dot_nt(delta_pre[...], fk[cols, :])
        dg[:, cols] = dot_nt(left_gate[...], fr[cols, :])
        return 0
    lax.fori_loop(0, width // tile, hidden_tile, 0)
    def leave(at):
        for i, z in ((1, delta), (2, branch)):
            saves.append(pltpu.make_async_copy(z.at[at, :], outs[i].at[at, :], row_sems.at[i - 1, at.start // (tokens // rows)]))
            saves[-1].start()
    norm_backward(middle, mean, scale, same, g2, b2, (ck, cr), (dh, dg), g, (delta, branch), sums, hats, first, second, rows, leave)
    save(sums, 3)
    for c in saves:
        c.wait()

def channel(rows, times, same, factor_out, factor_gate, g, p, rect, middle, mean, scale):
    (g1, b1, fade, bonus, mk, mv, mr, wk, wv, wr, wo, g2, b2, ck, cr, fk, fr, fv) = p
    tokens, width = g.shape
    ff = fk.shape[1]
    vm = pl.BlockSpec(memory_space=pltpu.VMEM)
    hbm = pl.BlockSpec(memory_space=pl.ANY)
    outs = [((tokens, ff), BF), ((tokens, width), F32), ((tokens, width), BF), ((8, width), F32)]
    outs += [((tokens, width), BF)] * 2 if times else [((16, LANES), BF)] * 2
    wide, wide32 = pltpu.VMEM((tokens, width), BF), pltpu.VMEM((tokens, width), F32)
    stat = pltpu.VMEM((tokens, LANES), F32)
    big = pltpu.VMEM((tokens, ff), BF)
    scratch = [pltpu.VMEM((ff, width), BF), pltpu.VMEM((width, ff), BF), pltpu.VMEM((width, width), BF), big, wide32, wide, wide, big, wide32, wide32]
    scratch += [stat] * 4 + [wide32, wide32, wide, pltpu.VMEM((8, width), F32), pltpu.SemaphoreType.DMA((2 * ff // 1024 + 5,)), pltpu.SemaphoreType.DMA((6,)), pltpu.SemaphoreType.DMA((2, rows))]
    return pl.pallas_call(
        functools.partial(channel_kernel, rows, times),
        out_shape=tuple(jax.ShapeDtypeStruct(*o) for o in outs),
        in_specs=[vm] * 8 + [hbm] * 7,
        out_specs=(hbm,) * 6,
        scratch_shapes=scratch,
        compiler_params=pltpu.CompilerParams(vmem_limit_bytes=60 << 20),
        cost_estimate=pl.CostEstimate(flops=75000000000, bytes_accessed=217500000, transcendentals=0),
        name="channel",
    )(same, factor_out, factor_gate, g, g2, b2, ck, cr, rect, middle, mean, scale, fv, fk, fr)

def time_kernel(rows, *refs):
    (same_s, same, branch, h, g1, b1, fade, bonus, mk, mv, mr, wo_in, gate_in, ks_in, vs_in, tops_in, bottoms_in, wk_in, wv_in, wr_in, delta_in, mean_in, scale_in) = refs[:23]
    n_out = 5
    outs = refs[23:23 + n_out]
    (wo, gate, ks, vs, wk, wv, wr, delta, dm, gs, ys, tops, bottoms, dks, dvs, dk, dv, dr, ik, iv, ir, mean, scale, first, second, hats, state, sums, slab, in_sems, out_sems, row_sems) = refs[23 + n_out:]
    tokens, width = h.shape
    each = tokens // rows
    parts = width // LANES
    tile = 1024
    sums[...] = jnp.zeros_like(sums)
    loads = fetch([(wo_in, wo), (gate_in, gate), (ks_in, ks), (vs_in, vs), (tops_in, tops), (bottoms_in, bottoms), (wk_in, wk), (wv_in, wv), (wr_in, wr), (delta_in, delta), (mean_in, mean), (scale_in, scale)], in_sems)
    saves = []
    def save(source, i):
        saves.append(pltpu.make_async_copy(source, outs[i], out_sems.at[i]))
        saves[-1].start()
    def cols_of(j):
        return pl.ds(pl.multiple_of(j * tile, tile), tile)
    loads[0].wait()
    loads[1].wait()
    def mixed_tile(j, _):
        cols = cols_of(j)
        d = dot_nt(branch[...], wo[cols, :])
        dm[:, cols] = d
        e = d * gate[:, cols]
        for row in range(rows):
            for c in range(tile // LANES):
                gs[pl.ds(row * each * parts + j * (tile // LANES) + c, each, stride=parts), :] = e[row * each:(row + 1) * each, c * LANES:(c + 1) * LANES]
        return 0
    lax.fori_loop(0, width // tile, mixed_tile, 0)
    for i in (2, 3, 4, 5):
        loads[i].wait()
    rate = jnp.exp(slabs(fade, slab))
    decay = jnp.exp(-rate)
    extra = slabs(bonus, slab)
    zero = jnp.zeros(decay.shape, F32)
    def back(i, carry):
        t = each - 1 - i
        dw, du = carry[:2]
        following = []
        for row in range(rows):
            here = pl.ds(pl.multiple_of((row * each + t) * parts, parts), parts)
            a, b = carry[2 + 2 * row], carry[3 + 2 * row]
            k, v = ks[here, :], vs[here, :]
            ek, now = jnp.exp(k), jnp.exp(extra + k)
            inverse = 1.0 / (bottoms[here, :] + now)
            y = (tops[here, :] + now * v) * inverse
            ys[here, :] = y
            ga = gs[here, :] * inverse
            gb = -ga * y
            q = now * (v * ga + gb)
            dks[here, :] = ek * (v * a + b) + q
            dvs[here, :] = ek * a + now * ga
            du = du + q
            dw = dw + (a * tops[here, :] + b * bottoms[here, :])
            m = same_s[row, t]
            following += [(ga + decay * a) * m, (gb + decay * b) * m]
        return (dw, du, *following)
    done = lax.fori_loop(0, each, back, (zero,) * (2 + 2 * rows), unroll=4)
    dfade = -done[0] * decay * rate
    for c in range(parts):
        sums[5:6, c * LANES:(c + 1) * LANES] = dfade[c:c + 1, :]
        sums[6:7, c * LANES:(c + 1) * LANES] = done[1][c:c + 1, :]
    for row in range(rows):
        def out_step(c, _, row=row):
            span = slice(row * each, (row + 1) * each)
            cols = lanes(c)
            at = pl.ds(row * each * parts + c, each, stride=parts)
            dk[span, cols] = dks[at, :].astype(BF)
            dv[span, cols] = dvs[at, :].astype(BF)
            s = gate[span, cols]
            dr[span, cols] = (dm[span, cols] * ys[at, :] * s * (1.0 - s)).astype(BF)
            return 0
        lax.fori_loop(0, parts, out_step, 0)
    for i, z in enumerate((dk, dv, dr)):
        save(z, i)
    for i in (6, 7, 8):
        loads[i].wait()
    def in_tile(j, _):
        cols = cols_of(j)
        ik[:, cols] = dot_nt(dk[...], wk[cols, :])
        iv[:, cols] = dot_nt(dv[...], wv[cols, :])
        ir[:, cols] = dot_nt(dr[...], wr[cols, :])
        return 0
    lax.fori_loop(0, width // tile, in_tile, 0)
    for c in loads[9:]:
        c.wait()
    def leave(at):
        saves.append(pltpu.make_async_copy(state.at[at, :], outs[3].at[at, :], row_sems.at[at.start // each]))
        saves[-1].start()
    norm_backward(h, mean, scale, same, g1, b1, (mk, mv, mr), (ik, iv, ir), delta, (state,), sums, hats, first, second, rows, leave)
    save(sums, 4)
    for c in saves:
        c.wait()

def time_mix(rows, dtype, same_s, same, branch, delta, h, p, gate, ks, vs, tops, bottoms, mean, scale):
    (g1, b1, fade, bonus, mk, mv, mr, wk, wv, wr, wo, g2, b2, ck, cr, fk, fr, fv) = p
    tokens, width = h.shape
    vm = pl.BlockSpec(memory_space=pltpu.VMEM)
    hbm = pl.BlockSpec(memory_space=pl.ANY)
    outs = [((tokens, width), BF)] * 3 + [((tokens, width), dtype), ((8, width), F32)]
    wide, wide32 = pltpu.VMEM((tokens, width), BF), pltpu.VMEM((tokens, width), F32)
    step32 = pltpu.VMEM(ks.shape, F32)
    stat = pltpu.VMEM((tokens, LANES), F32)
    square = pltpu.VMEM((width, width), BF)
    scratch = [square, wide32, step32, step32, square, square, square, wide32, wide32] + [step32] * 6 + [wide] * 3 + [wide32] * 3 + [stat] * 4 + [wide32]
    scratch += [pltpu.VMEM((tokens, width), dtype), pltpu.VMEM((8, width), F32), pltpu.VMEM((width // LANES, LANES), F32), pltpu.SemaphoreType.DMA((12,)), pltpu.SemaphoreType.DMA((5,)), pltpu.SemaphoreType.DMA((rows,))]
    return pl.pallas_call(
        functools.partial(time_kernel, rows),
        out_shape=tuple(jax.ShapeDtypeStruct(*o) for o in outs),
        in_specs=[pl.BlockSpec(memory_space=pltpu.SMEM)] + [vm] * 10 + [hbm] * 12,
        out_specs=(hbm,) * 5,
        scratch_shapes=scratch,
        compiler_params=pltpu.CompilerParams(vmem_limit_bytes=60 << 20),
        cost_estimate=pl.CostEstimate(flops=87000000000, bytes_accessed=252300000, transcendentals=0),
        name="time_mix",
    )(same_s, same, branch, h, g1, b1, fade, bonus, mk, mv, mr, wo, gate, ks, vs, tops, bottoms, wk, wv, wr, delta, mean, scale)


UNIT = 1024


def starts(parts):
    return [sum(c for c, _ in parts[:i]) for i in range(len(parts))]


def terms_kernel(count, parts, shapes, with_sums, with_factor, *refs):
    bits, refs = refs[0], refs[1:]
    if with_factor:
        factor, refs = refs[0], refs[1:]
    n, np_ = len(shapes), len(parts)
    left_in, right_in, refs = refs[:n], refs[n:2 * n], refs[2 * n:]
    if with_sums:
        early, late, *refs = refs
    outs, refs = refs[:2 * np_], refs[2 * np_:]
    lefts, rights, refs = refs[:n], refs[n:2 * n], refs[2 * n:]
    bufs, (in_sems, out_sems) = refs[:np_], refs[np_:]
    sends, keeps = outs[::2], outs[1::2]
    tile = 512
    columns = starts(parts)

    def place(order, d):
        bit = [(d >> b) & 1 if isinstance(d, int) else lax.rem(lax.div(d, 1 << b), 2) for b in order]
        return bit[0] ^ bits[order[0]], bit[1] * 4 + bit[2] * 2 + bit[3]

    chunk_base = [sum(kin // tile for kin, _ in shapes[:m]) for m in range(n)]

    def load(m, j):
        cols = pl.ds(pl.multiple_of(j * tile, tile), tile)
        return pltpu.make_async_copy(left_in[m].at[:, cols], lefts[m].at[:, cols], in_sems.at[chunk_base[m] + j])

    right_base = [chunk_base[-1] + shapes[-1][0] // tile + sum(width // UNIT for _, width in shapes[:m]) for m in range(n)]

    def load_right(m, q):
        cols = slice(q * UNIT, (q + 1) * UNIT)
        return pltpu.make_async_copy(right_in[m].at[:, cols], rights[m].at[:, cols], in_sems.at[right_base[m] + q])

    for m, (kin, width) in enumerate(shapes):
        load_right(m, 0).start()
        for j in range(kin // tile):
            load(m, j).start()
        for q in range(1, width // UNIT):
            load_right(m, q).start()
    waits = []
    base = 0
    blocks = 0
    for m, ((kin, width), left, right) in enumerate(zip(shapes, lefts, rights)):
        rows = kin // count
        per = tile // rows
        for q in range(width // UNIT):
            load_right(m, q).wait()
            if with_factor:
                right[...] = (right[...].astype(F32) * factor[...].astype(F32)).astype(BF)

            def step(j, _, m=m, q=q, left=left, right=right, rows=rows, per=per, base=base):
                if q == 0:
                    load(m, j).wait()
                lhs = left[:, pl.ds(pl.multiple_of(j * tile, tile), tile)]
                for i, (cols, order) in enumerate(parts):
                    at = q * UNIT + columns[i]
                    res = lax.dot_general(lhs, right[:, at:at + cols], (((0,), (0,)), ((), ())), preferred_element_type=F32).astype(BF)
                    for s in range(per):
                        relative, index = place(order, j * per + s)
                        bufs[i][relative, index, base:base + rows, :] = res[s * rows:(s + 1) * rows]
                        if rows >= 256:
                            source = bufs[i].at[relative, index]
                            for r, target in ((1, sends[i]), (0, keeps[i])):
                                @pl.when(relative == r)
                                def _(source=source, target=target, index=index, i=i):
                                    pltpu.make_async_copy(source, target.at[index], out_sems.at[i, j * per + s]).start()
                return 0

            lax.fori_loop(0, kin // tile, step, 0)
            for i in range(np_):
                if rows >= 256:
                    for j in range(count):
                        waits.append(pltpu.make_async_copy(bufs[i].at[0, 0], keeps[i].at[0], out_sems.at[i, j]))
                else:
                    for r, target in ((1, sends[i]), (0, keeps[i])):
                        c = pltpu.make_async_copy(bufs[i].at[r, :, base:base + rows, :], target.at[:, base:base + rows, :], out_sems.at[i, 2 * blocks + r])
                        c.start()
                        waits.append(c)
            base += rows
            blocks += 1
    if with_sums:
        share = early.shape[1] // count
        both = jnp.concatenate([early[...], late[...]], axis=0)
        for buf in bufs:
            buf[:, :, base:base + 16, :] = jnp.zeros(buf.shape[:2] + (16, buf.shape[3]), BF)
        for d in range(count):
            column = d * share // LANES * LANES
            piece = both[:, column:column + LANES]
            if d * share - column:
                piece = pltpu.roll(piece, LANES - (d * share - column), 1)
            relative, index = place(parts[0][1], d)
            bufs[0][relative, index, base:base + 16, 0:LANES] = piece.astype(BF)
        for i in range(np_):
            for r, target in ((1, sends[i]), (0, keeps[i])):
                c = pltpu.make_async_copy(bufs[i].at[r, :, base:base + 16, :], target.at[:, base:base + 16, :], out_sems.at[i, 2 * blocks + r])
                c.start()
                waits.append(c)
    for c in waits:
        c.wait()


def terms(bits, parts, pairs, sums=(), factor=None):
    count = 16
    lefts, rights = zip(*pairs)
    shapes = tuple((a.shape[1], b.shape[1]) for a, b in pairs)
    tokens = lefts[0].shape[0]
    rows = sum(kin // count * (width // UNIT) for kin, width in shapes) + (16 if sums else 0)
    outs, bufs = [], []
    for cols, _ in parts:
        outs += [jax.ShapeDtypeStruct((count // 2, rows, cols), BF)] * 2
        bufs.append(pltpu.VMEM((2, count // 2, rows, cols), BF))
    flops = sum(2 * tokens * kin * width for kin, width in shapes)
    result = pl.pallas_call(
        functools.partial(terms_kernel, count, parts, shapes, bool(sums), factor is not None),
        out_shape=tuple(outs),
        in_specs=[SM] + [VM] * (factor is not None) + [HBM] * (2 * len(shapes)) + [VM] * len(sums),
        out_specs=(HBM,) * len(outs),
        scratch_shapes=[pltpu.VMEM(x.shape, BF) for x in (*lefts, *rights)]
        + bufs + [pltpu.SemaphoreType.DMA((sum(kin // 512 + width // UNIT for kin, width in shapes),)), pltpu.SemaphoreType.DMA((len(parts), 16))],
        compiler_params=pltpu.CompilerParams(vmem_limit_bytes=56 << 20),
        cost_estimate=pl.CostEstimate(flops=39000000000, bytes_accessed=113100000, transcendentals=0),
        name="terms",
    )(bits, *(() if factor is None else (factor,)), *lefts, *rights, *sums)
    return list(zip(result[::2], result[1::2]))


def swap(block, bit):
    count = lax.axis_size("dp")
    return lax.ppermute(block, "dp", [(i, i ^ (1 << bit)) for i in range(count)])


def summed(kept, came, dtype=BF):
    return (kept.astype(F32) + came.astype(F32)).astype(dtype)


def advance_kernel(bits, kept_go, came_go, kept_stay, came_stay, send, keep):
    send[...] = summed(kept_go[...], came_go[...])
    keep[...] = summed(kept_stay[...], came_stay[...])


def advance(bits, kept, came, bit):
    lead, rows, cols = kept.shape
    half = lead // 2
    block = rows
    go = pl.BlockSpec((1, block, cols), lambda g, i, b: ((1 - b[bit]) * half + g, i, 0))
    stay = pl.BlockSpec((1, block, cols), lambda g, i, b: (b[bit] * half + g, i, 0))
    out = pl.BlockSpec((1, block, cols), lambda g, i, b: (g, i, 0))
    return pl.pallas_call(
        advance_kernel,
        out_shape=(jax.ShapeDtypeStruct((half, rows, cols), BF),) * 2,
        grid_spec=pltpu.PrefetchScalarGridSpec(
            num_scalar_prefetch=1, grid=(half, rows // block), in_specs=[go, go, stay, stay], out_specs=(out, out)
        ),
        compiler_params=pltpu.CompilerParams(vmem_limit_bytes=30 << 20),
        cost_estimate=pl.CostEstimate(flops=9000000000, bytes_accessed=26100000, transcendentals=0),
        name="advance",
    )(bits, kept, came, kept, came)


def final_kernel(pieces, parts, *refs):
    n = len(parts)
    ins, outs = refs[:2 * n], refs[2 * n:]
    for (row, rows, blocks, columns), out in zip(pieces, outs):
        for q in range(blocks):
            span = slice(row + q * rows, row + (q + 1) * rows)
            if columns < UNIT:
                out[...] = summed(ins[0][0, span, 0:LANES], ins[1][0, span, 0:LANES], F32)[:, :columns]
                continue
            for i, at in enumerate(starts(parts)):
                out[:, q * UNIT + at:q * UNIT + at + parts[i][0]] = summed(ins[2 * i][0, span, :], ins[2 * i + 1][0, span, :], F32)


def final(parts, pieces, arrays):
    size = sum(a.size for a in arrays)
    return pl.pallas_call(
        functools.partial(final_kernel, pieces, parts),
        out_shape=tuple(jax.ShapeDtypeStruct((rows, blocks * columns), F32) for row, rows, blocks, columns in pieces),
        in_specs=[VM] * len(arrays),
        out_specs=(VM,) * len(pieces),
        compiler_params=pltpu.CompilerParams(vmem_limit_bytes=40 << 20),
        cost_estimate=pl.CostEstimate(flops=4500000000, bytes_accessed=13050000, transcendentals=0),
        name="final",
    )(*arrays)


def after(value, *earlier):
    return lax.optimization_barrier((value, earlier))[0]


class Line:
    def __init__(self, bits, plan, pieces):
        self.bits, self.plan, self.pieces, self.token, self.flight, self.sums = bits, plan, pieces, None, {}, {}

    def tie(self, value):
        return value if self.token is None else after(value, self.token)

    def open(self, group, pairs, sums=(), factor=None):
        pairs = ((self.tie(pairs[0][0]), pairs[0][1]),) + tuple(pairs[1:])
        found = terms(self.bits, self.plan[group], pairs, sums, factor)
        self.token = found
        for i, (send, keep) in enumerate(found):
            self.flight[group, i] = keep, swap(send, self.plan[group][i][1][0])

    def serve(self, steps):
        for group, i, stage in steps:
            parts = self.plan[group]
            if stage < 4:
                kept, came = self.tie(self.flight[group, i])
                send, keep = advance(self.bits, kept, came, parts[i][1][stage])
                self.token = send, keep
                self.flight[group, i] = keep, swap(send, parts[i][1][stage])
            else:
                self.sums[group, i] = self.flight.pop((group, i))
                if all((group, k) in self.sums for k in range(len(parts))):
                    arrays = [a for k in range(len(parts)) for a in self.sums[group, k]]
                    arrays[0] = self.tie(arrays[0])
                    self.sums[group] = final(parts, self.pieces[group], arrays)
                    self.token = self.sums[group][0]


def halving(left, right=None):
    count = lax.axis_size("dp")
    bits = count.bit_length() - 1
    me = lax.axis_index("dp")
    if right is not None:
        left = lax.dot_general(left, right, (((0,), (0,)), ((), ())), preferred_element_type=F32).astype(BF)
    current = left.reshape((2,) * bits + (left.shape[0] // count, left.shape[1]))
    for bit in range(bits):
        axis = bits - 1 - bit
        mine = (me >> bit) & 1
        send = lax.dynamic_index_in_dim(current, 1 - mine, axis, keepdims=False)
        keep = lax.dynamic_index_in_dim(current, mine, axis, keepdims=False)
        current = summed(keep, swap(send, bit), BF if bit + 1 < bits else F32)
    return current


def unwritten(function, *args):
    shapes, tree = jax.tree.flatten(jax.eval_shape(function, *args))
    outs = pl.pallas_call(
        lambda *refs: None, out_shape=tuple(shapes), out_specs=(HBM,) * len(shapes), name="unwritten"
    )()
    return jax.tree.unflatten(tree, outs)


VECTORS = (0, 1, 5, 6, 2, 3, 4, 8, 9, 10, 11)
PARTS_0 = dict(
    a=((512, (2, 1, 0, 3)), (512, (1, 0, 2, 3))),
    b=((512, (0, 1, 2, 3)), (512, (2, 1, 0, 3))),
    e=((512, (0, 2, 1, 3)), (512, (1, 0, 2, 3))),
)
PARTS_1 = dict(
    a=((512, (2, 0, 3, 1)), (512, (1, 0, 2, 3))),
    b=((512, (1, 2, 0, 3)), (512, (0, 1, 2, 3))),
    e=((512, (1, 2, 0, 3)), (512, (2, 0, 1, 3))),
)
STEPS_0 = (
    (),
    (('a', 0, 1), ('a', 1, 1)),
    (('a', 0, 2), ('b', 0, 1), ('b', 1, 1), ('a', 1, 2), ('e', 1, 1), ('a', 1, 3), ('e', 0, 1), ('a', 0, 3), ('a', 1, 4), ('b', 0, 2), ('e', 1, 2), ('e', 0, 2), ('b', 1, 2), ('a', 0, 4), ('e', 0, 3), ('b', 0, 3), ('b', 1, 3), ('e', 0, 4), ('e', 1, 3), ('b', 0, 4), ('b', 1, 4), ('e', 1, 4)),
)
STEPS_1 = (
    (),
    (('a', 0, 1), ('a', 1, 1)),
    (),
    (('a', 0, 2), ('a', 1, 2), ('e', 1, 1), ('b', 1, 1), ('a', 0, 3), ('b', 0, 1), ('a', 1, 3), ('e', 0, 1), ('e', 1, 2), ('b', 0, 2), ('a', 1, 4), ('b', 1, 2), ('a', 0, 4), ('e', 0, 2), ('b', 0, 3), ('e', 1, 3), ('b', 1, 3), ('e', 0, 3), ('b', 0, 4), ('e', 1, 4), ('b', 1, 4), ('e', 0, 4)),
)


def local(entry_pair, labels, *params):
    count = lax.axis_size("dp")
    section = lax.axis_index("section")
    rows, each, width = entry_pair.shape[1:]
    own = entry_pair.reshape(rows * each, width)
    share = width // count
    p = [e if e.ndim == 2 else e[0] for e in params]
    ff = p[15].shape[1]
    first = jnp.zeros((rows, 1), F32)
    same_s = jnp.concatenate([first, (labels[:, 1:] == labels[:, :-1]).astype(F32)], axis=1)
    same = jnp.broadcast_to(same_s.reshape(rows * each, 1), (rows * each, LANES))
    fast = count == 16 and width == UNIT
    me = lax.axis_index("dp")
    bits = jnp.stack([(me >> i) & 1 for i in range(4)])
    wide = ff // width
    pieces = dict(
        a=((0, ff // count, 1, width),),
        b=((0, share, wide, width), (share * wide, share, 1, width), (share * (wide + 1), share, 1, width)),
        e=tuple((i * share, share, 1, width) for i in range(3)) + tuple((3 * share + i, 1, 1, share) for i in VECTORS),
    )

    def plain_rest(pairs, sums):
        together = jnp.concatenate(sums).astype(BF).reshape(16, count, share).transpose(1, 0, 2).reshape(count * 16, share)
        vectors = halving(together)
        return tuple(halving(*pair) for pair in pairs) + tuple(vectors[i:i + 1] for i in VECTORS)

    def start():
        return forward(rows, False, same_s, same, own, p, own)

    def middle_part(received):
        kept = forward(rows, True, same_s, same, received, p, own)
        (key_in, value_in, recept_in, ks, vs, gate, tops, bottoms, mixed, middle, hidden_in, gate_in, act, result, delta_out, delta_gate, mean, scale, mean2, scale2) = kept
        line = Line(bits, PARTS_1, pieces)
        if fast:
            line.open("a", ((act, delta_out),))
        delta_pre, delta, branch, late, _, _ = channel(rows, False, same, delta_out, delta_gate, line.tie(own), p, act, middle, mean2, scale2)
        line.token = branch
        if fast:
            line.serve(STEPS_1[0])
        dk, dv, dr, state, early = time_mix(rows, BF, same_s, same, line.tie(branch), delta, received, p, gate, ks, vs, tops, bottoms, mean, scale)
        key_pairs = ((hidden_in, delta_pre), (gate_in, delta_gate), (mixed, branch))
        begun = list(line.flight.values()) if fast else (act, delta_out)
        return state, result, begun, (early, late), key_pairs, ((key_in, dk), (value_in, dv), (recept_in, dr))

    def end_first(received, kept):
        (key_in, value_in, recept_in, ks, vs, gate, tops, bottoms, mixed, middle, hidden_in, gate_in, act, result, factor_out, factor_gate, mean, scale, mean2, scale2) = kept
        line = Line(bits, PARTS_0, pieces)
        if fast:
            line.open("a", ((act, received),), factor=factor_out)
        g = line.tie(received)
        delta_pre, delta, branch, late, delta_out, delta_gate = channel(rows, True, same, factor_out, factor_gate, g, p, act, middle, mean2, scale2)
        key_pairs = ((hidden_in, delta_pre), (gate_in, delta_gate), (mixed, branch))
        line.token = branch
        if fast:
            line.serve(STEPS_0[0])
            line.open("b", key_pairs)
            line.serve(STEPS_0[1])
        dk, dv, dr, state, early = time_mix(rows, F32, same_s, same, line.tie(branch), delta, own, p, gate, ks, vs, tops, bottoms, mean, scale)
        rest_pairs = ((key_in, dk), (value_in, dv), (recept_in, dr))
        if not fast:
            return state, (halving(act, delta_out),), tuple(halving(*pair) for pair in key_pairs), plain_rest(rest_pairs, (early, late))
        line.token = state
        line.open("e", rest_pairs, (early, late))
        line.serve(STEPS_0[2])
        return state, line.sums["a"], line.sums["b"], line.sums["e"]

    def end_second(result, begun, sums, key_pairs, rest_pairs):
        if not fast:
            return result.astype(F32), (halving(*begun),), tuple(halving(*pair) for pair in key_pairs), plain_rest(rest_pairs, sums)
        line = Line(bits, PARTS_1, pieces)
        line.flight = {("a", i): pair for i, pair in enumerate(begun)}
        line.serve(STEPS_1[1])
        line.open("b", key_pairs)
        line.serve(STEPS_1[2])
        line.open("e", rest_pairs, sums)
        line.serve(STEPS_1[3])
        return result.astype(F32), line.sums["a"], line.sums["b"], line.sums["e"]

    kept = lax.cond(section == 0, start, lambda: unwritten(start))
    received = lax.ppermute(kept[13], "section", [(0, 1)])
    delta, *pending = lax.cond(section == 1, middle_part, lambda r: unwritten(middle_part, r), received)
    received = lax.ppermute(delta, "section", [(1, 0)])
    ends, (value_sum,), (key_sum, gate_sum, exit_sum), rest = lax.cond(
        section == 0, lambda r, k, q: end_first(r, k), lambda r, k, q: end_second(*q), received, kept, pending
    )
    ends = ends.reshape(rows, each, width)
    everything = (ends, *(z[0] for z in rest[3:10]), *rest[:3], exit_sum, *(z[0] for z in rest[10:14]), key_sum, gate_sum, value_sum)
    return tuple(e[None] for e in everything)


def solution(mesh):
    vec, mat = P("section", None), P("section", None, None)
    in_specs = (P("section", "dp", None, None), P("dp", None)) + (vec,) * 7 + (mat,) * 4 + (vec,) * 4 + (mat,) * 3
    vec, mat = P("section", "dp"), P("section", "dp", None)
    out_specs = (P("section", "dp", None, None),) + (vec,) * 7 + (mat,) * 4 + (vec,) * 4 + (mat,) * 3
    return jax.shard_map(local, mesh=mesh, in_specs=in_specs, out_specs=out_specs, check_vma=False)
```

```python
import functools

import jax
import jax.numpy as jnp
from jax import lax
from jax.experimental import pallas as pl
from jax.experimental.pallas import tpu as pltpu
from jax.sharding import PartitionSpec as P

BF = jnp.bfloat16
F32 = jnp.float32
LANES = 128
VM = pl.BlockSpec(memory_space=pltpu.VMEM)
HBM = pl.BlockSpec(memory_space=pl.ANY)
SM = pl.BlockSpec(memory_space=pltpu.SMEM)

def dot(left, right):
    return jnp.dot(left, right, preferred_element_type=F32)

def dot_nt(left, right):
    return lax.dot_general(left, right, (((1,), (1,)), ((), ())), preferred_element_type=F32)

def lanes(c):
    return pl.ds(pl.multiple_of(c * LANES, LANES), LANES)

def slabs(vector, scratch):
    for c in range(scratch.shape[0]):
        scratch[c:c + 1, :] = vector[:, c * LANES:(c + 1) * LANES].astype(F32)
    return scratch[...]

def statistics(source, mean, scale, tokens, width, chunk=128):
    def step(i, _):
        at = pl.ds(pl.multiple_of(i * chunk, chunk), chunk)
        x = source[at, :].astype(F32)
        m = jnp.sum(x, axis=1, keepdims=True) * (1.0 / width)
        x = x - m
        v = jnp.sum(x * x, axis=1, keepdims=True) * (1.0 / width)
        mean[at, :] = jnp.broadcast_to(m, (chunk, LANES))
        scale[at, :] = jnp.broadcast_to(lax.rsqrt(v + 1e-05), (chunk, LANES))
        return 0
    lax.fori_loop(0, tokens // chunk, step, 0)

def mix_into(source, mean, scale, same, gain, bias, factors, targets, width):
    def step(c, _):
        cols = lanes(c)
        z = (source[:, cols].astype(F32) - mean[...]) * scale[...] * gain[:, cols].astype(F32) + bias[:, cols].astype(F32)
        before = pltpu.roll(z, 1, 0) * same[...]
        step_up = z - before
        for factor, target in zip(factors, targets):
            target[:, cols] = (before + step_up * factor[:, cols].astype(F32)).astype(BF)
        return 0
    lax.fori_loop(0, width // LANES, step, 0)

def fetch(pairs, sems):
    copies = [pltpu.make_async_copy(s, d, sems.at[i]) for i, (s, d) in enumerate(pairs)]
    for c in copies:
        c.start()
    return copies

def forward_kernel(rows, with_delta, orders, *refs):
    if orders:
        bits, refs = refs[0], refs[1:]
    (same_s, same, h, g1, b1, fade, bonus, mk, mv, mr, g2, b2, ck, cr, cot) = refs[:15]
    weights = refs[15:22]
    n_out = 20
    outs = refs[22:22 + n_out]
    if orders:
        pieces, piece_sems, refs = refs[22 + n_out:26 + n_out], refs[-1], refs[:22 + n_out] + refs[26 + n_out:-1]
    (wk, wv, wr, wo, fk, fr, fv, mean, scale, mean2, scale2, key_in, value_in, recept_in, ks, vs, ys, tops, bottoms, gate, mixed, middle,
     hidden_in, gate_in, act, slab, in_sems, out_sems) = refs[22 + n_out:]
    tokens, width = h.shape
    each = tokens // rows
    parts = width // LANES
    tile = 512
    large = 1024
    ff = act.shape[1]
    loads = fetch(list(zip(weights, (wk, wv, wr, wo, fk, fr, fv))), in_sems)
    saves = []

    def save(source):
        i = len(saves)
        saves.append(pltpu.make_async_copy(source, outs[i], out_sems.at[i]))
        saves[-1].start()

    statistics(h, mean, scale, tokens, width)
    mix_into(h, mean, scale, same, g1, b1, (mk, mv, mr), (key_in, value_in, recept_in), width)
    for z in (key_in, value_in, recept_in):
        save(z)

    def cols_of(j):
        return pl.ds(pl.multiple_of(j * tile, tile), tile)

    def steps_tile(values, target, j):
        for row in range(rows):
            for c in range(tile // LANES):
                target[pl.ds(row * each * parts + j * (tile // LANES) + c, each, stride=parts), :] = values[row * each:(row + 1) * each, c * LANES:(c + 1) * LANES]

    loads[0].wait()
    def key_tile(j, _):
        steps_tile(dot(key_in[...], wk[:, cols_of(j)]), ks, j)
        return 0
    lax.fori_loop(0, width // tile, key_tile, 0)
    loads[1].wait()
    def value_tile(j, _):
        steps_tile(dot(value_in[...], wv[:, cols_of(j)]), vs, j)
        return 0
    lax.fori_loop(0, width // tile, value_tile, 0)
    save(ks)
    save(vs)
    loads[2].wait()
    def accept_tile(j, _):
        gate[:, cols_of(j)] = jax.nn.sigmoid(dot(recept_in[...], wr[:, cols_of(j)]))
        return 0
    lax.fori_loop(0, width // tile, accept_tile, 0)
    save(gate)

    decay = jnp.exp(-jnp.exp(slabs(fade, slab)))
    extra = slabs(bonus, slab)
    def step(t, carry):
        following = []
        for row in range(rows):
            here = pl.ds(pl.multiple_of((row * each + t) * parts, parts), parts)
            m = same_s[row, t]
            top, bottom = carry[2 * row] * m, carry[2 * row + 1] * m
            tops[here, :] = top
            bottoms[here, :] = bottom
            k, v = ks[here, :], vs[here, :]
            ek, now = jnp.exp(k), jnp.exp(extra + k)
            ys[here, :] = (top + now * v) / (bottom + now)
            following += [decay * top + ek * v, decay * bottom + ek]
        return tuple(following)
    zero = jnp.zeros(decay.shape, F32)
    lax.fori_loop(0, each, step, (zero,) * (2 * rows), unroll=4)
    save(tops)
    save(bottoms)

    for row in range(rows):
        def mixed_step(c, _, row=row):
            y = ys[pl.ds(row * each * parts + c, each, stride=parts), :]
            mixed[row * each:(row + 1) * each, lanes(c)] = (gate[row * each:(row + 1) * each, lanes(c)] * y).astype(BF)
            return 0
        lax.fori_loop(0, parts, mixed_step, 0)
    save(mixed)
    loads[3].wait()
    def middle_tile(j, _):
        middle[:, cols_of(j)] = h[:, cols_of(j)].astype(F32) + dot(mixed[...], wo[:, cols_of(j)])
        return 0
    lax.fori_loop(0, width // tile, middle_tile, 0)
    save(middle)

    statistics(middle, mean2, scale2, tokens, width)
    mix_into(middle, mean2, scale2, same, g2, b2, (ck, cr), (hidden_in, gate_in), width)
    save(hidden_in)
    save(gate_in)
    loads[4].wait()
    def hidden_tile(j, _):
        cols = pl.ds(pl.multiple_of(j * large, large), large)
        r = jnp.maximum(dot(hidden_in[...], fk[:, cols]), 0.0)
        act[:, cols] = (r * r).astype(BF)
        return 0
    lax.fori_loop(0, ff // large, hidden_tile, 0)
    save(act)
    piece_waits = []
    if orders:
        share = ff // 16
        for d in range(16):
            first, one, two = orders[d >> 3][:3]
            source = act.at[:, d * share:(d + 1) * share]
            column = (((d >> one) & 1) * 2 + ((d >> two) & 1)) * share
            relative = ((d >> first) & 1) ^ bits[first]
            for r, target in ((1, pieces[2 * (d >> 3)]), (0, pieces[2 * (d >> 3) + 1])):
                copy = pltpu.make_async_copy(source, target.at[:, column:column + share], piece_sems.at[d])
                @pl.when(relative == r)
                def _(copy=copy):
                    copy.start()
            piece_waits.append(copy)
    for i in (0, 1, 2, 5):
        saves[i].wait()
    result, delta_out, delta_gate = key_in, value_in, recept_in
    loads[5].wait()
    def gate_tile(j, _):
        gate[:, cols_of(j)] = jax.nn.sigmoid(dot(gate_in[...], fr[:, cols_of(j)]))
        return 0
    lax.fori_loop(0, width // tile, gate_tile, 0)
    loads[6].wait()
    def out_tile(j, _):
        cols = cols_of(j)
        o = dot(act[...], fv[:, cols])
        s = gate[:, cols]
        result[:, cols] = (middle[:, cols] + s * o).astype(BF)
        g = cot[:, cols].astype(F32)
        if with_delta:
            delta_out[:, cols] = (g * s).astype(BF)
            delta_gate[:, cols] = (g * o * s * (1.0 - s)).astype(BF)
        else:
            delta_out[:, cols] = s.astype(BF)
            delta_gate[:, cols] = (o * s * (1.0 - s)).astype(BF)
        return 0
    lax.fori_loop(0, width // tile, out_tile, 0)
    save(result)
    save(delta_out)
    save(delta_gate)
    for z in (mean, scale, mean2, scale2):
        save(z)
    if orders and with_delta:
        for i in (0, 1):
            piece_waits.append(pltpu.make_async_copy(delta_out, pieces[2 * i].at[:, width:2 * width], piece_sems.at[16 + i]))
            piece_waits[-1].start()
    for copy in piece_waits:
        copy.wait()
    for i, c in enumerate(saves):
        if i not in (0, 1, 2, 5):
            c.wait()

def forward(rows, with_delta, same_s, same, h, p, cot, bits=None, orders=None):
    (g1, b1, fade, bonus, mk, mv, mr, wk, wv, wr, wo, g2, b2, ck, cr, fk, fr, fv) = p
    tokens, width = h.shape
    ff = fk.shape[1]
    vm = pl.BlockSpec(memory_space=pltpu.VMEM)
    hbm = pl.BlockSpec(memory_space=pl.ANY)
    slabs = tokens * width // LANES
    outs = [((tokens, width), BF)] * 3 + [((slabs, LANES), F32)] * 2 + [((tokens, width), F32)] + [((slabs, LANES), F32)] * 2
    outs += [((tokens, width), BF), ((tokens, width), F32)]
    outs += [((tokens, width), BF)] * 2 + [((tokens, ff), BF)] + [((tokens, width), BF)] * 3
    outs = outs[:14] if False else outs
    outs += [((tokens, LANES), F32)] * 4
    wide, wide32, step32 = pltpu.VMEM((tokens, width), BF), pltpu.VMEM((tokens, width), F32), pltpu.VMEM((slabs, LANES), F32)
    stat = pltpu.VMEM((tokens, LANES), F32)
    square = pltpu.VMEM((width, width), BF)
    big = pltpu.VMEM((tokens, ff), BF)
    scratch = [square] * 4 + [pltpu.VMEM((width, ff), BF), square, pltpu.VMEM((ff, width), BF), stat, stat, stat, stat] + [wide] * 3
    scratch += [step32] * 5 + [wide32, wide, wide32, wide, wide, big]
    scratch += [pltpu.VMEM((width // LANES, LANES), F32), pltpu.SemaphoreType.DMA((7,)), pltpu.SemaphoreType.DMA((len(outs),))]
    if orders:
        sent = (tokens, width * (1 + with_delta))
        outs += [(sent, BF), ((tokens, width), BF)] * 2
        scratch.append(pltpu.SemaphoreType.DMA((18,)))
    smem = pl.BlockSpec(memory_space=pltpu.SMEM)
    return pl.pallas_call(
        functools.partial(forward_kernel, rows, with_delta, orders),
        out_shape=tuple(jax.ShapeDtypeStruct(*o) for o in outs),
        in_specs=[smem] * (orders is not None) + [smem] + [vm] * 14 + [hbm] * 7,
        out_specs=(hbm,) * len(outs),
        scratch_shapes=scratch,
        compiler_params=pltpu.CompilerParams(vmem_limit_bytes=60 << 20),
        cost_estimate=pl.CostEstimate(flops=90000000000, bytes_accessed=261000000, transcendentals=0),
        name="forward",
    )(*([bits] if orders else []), same_s, same, h, g1, b1, fade, bonus, mk, mv, mr, g2, b2, ck, cr, cot, wk, wv, wr, wo, fk, fr, fv)

def norm_backward(source, mean, scale, same, gain, bias, factors, grads, residual, targets, sums, hats, first, second, rows, leave):
    tokens, width = source.shape
    each = tokens // rows
    spans = [slice(row * each, (row + 1) * each) for row in range(rows)]

    def gather(c, carry):
        cols = lanes(c)
        g, b = gain[:, cols].astype(F32), bias[:, cols].astype(F32)
        following = []
        totals = [0.0] * (2 + len(grads))
        for row, at in enumerate(spans):
            hat = (source[at, cols].astype(F32) - mean[at, :]) * scale[at, :]
            z = hat * g + b
            step_up = z - pltpu.roll(z, 1, 0) * same[at, :]
            straight = rest = None
            for i, (factor, grad) in enumerate(zip(factors, grads)):
                d = grad[at, cols]
                df = d * factor[:, cols].astype(F32)
                totals[2 + i] += jnp.sum(d * step_up, axis=0, keepdims=True)
                straight = df if i == 0 else straight + df
                rest = d - df if i == 0 else rest + (d - df)
            dz = straight + pltpu.roll(rest * same[at, :], each - 1, 0)
            totals[0] += jnp.sum(dz * hat, axis=0, keepdims=True)
            totals[1] += jnp.sum(dz, axis=0, keepdims=True)
            dhat = dz * g
            hats[at, cols] = dhat
            following += [carry[2 * row] + dhat, carry[2 * row + 1] + dhat * hat]
        for i, total in enumerate(totals):
            sums[i:i + 1, cols] = total
        return tuple(following)

    zero = jnp.zeros((each, LANES), F32)
    done = lax.fori_loop(0, width // LANES, gather, (zero,) * (2 * rows))
    for row, at in enumerate(spans):
        for ref, value in ((first, done[2 * row]), (second, done[2 * row + 1])):
            ref[at, :] = jnp.broadcast_to(jnp.sum(value, axis=1, keepdims=True) * (1.0 / width), (each, LANES))

    for at in spans:
        def finish(c, _, at=at):
            cols = lanes(c)
            hat = (source[at, cols].astype(F32) - mean[at, :]) * scale[at, :]
            out = residual[at, cols].astype(F32) + scale[at, :] * (hats[at, cols] - first[at, :] - hat * second[at, :])
            for t in targets:
                t[at, cols] = out.astype(t.dtype)
            return 0

        lax.fori_loop(0, width // LANES, finish, 0)
        leave(at)


def channel_kernel(rows, times, *refs):
    (same, factor_out, factor_gate, g, g2, b2, ck, cr, rect_in, middle_in, mean_in, scale_in, fv_in, fk_in, fr_in) = refs[:15]
    n_out = 6
    outs = refs[15:15 + n_out]
    (fv, fk, fr, rect, middle, delta_out, delta_gate, delta_pre, dh, dg, mean, scale, first, second, hats, delta, branch, sums, in_sems, out_sems, row_sems) = refs[15 + n_out:]
    tokens, width = g.shape
    ff = rect.shape[1]
    tile = 512
    chunks = ff // tile
    first_loads = []
    for j in range(chunks):
        span = slice(j * tile, (j + 1) * tile)
        first_loads += [(fv_in.at[span, :], fv.at[span, :]), (rect_in.at[:, span], rect.at[:, span])]
    sums[...] = jnp.zeros_like(sums)
    loads = fetch(first_loads + [(fr_in, fr), (fk_in, fk), (middle_in, middle), (mean_in, mean), (scale_in, scale)], in_sems)
    saves = []
    def save(source, i):
        saves.append(pltpu.make_async_copy(source, outs[i], out_sems.at[i]))
        saves[-1].start()
    def cols_of(j):
        return pl.ds(pl.multiple_of(j * tile, tile), tile)
    if times:
        def scale_tile(j, _):
            cols = lanes(j)
            x = g[:, cols].astype(F32)
            delta_out[:, cols] = (x * factor_out[:, cols].astype(F32)).astype(BF)
            delta_gate[:, cols] = (x * factor_gate[:, cols].astype(F32)).astype(BF)
            return 0
        lax.fori_loop(0, width // LANES, scale_tile, 0)
        left_out, left_gate = delta_out, delta_gate
    else:
        left_out, left_gate = factor_out, factor_gate
    def pre_tile(j, _):
        cols = cols_of(j)
        pltpu.make_async_copy(fv_in.at[cols, :], fv.at[cols, :], in_sems.at[2 * j]).wait()
        pltpu.make_async_copy(rect_in.at[:, cols], rect.at[:, cols], in_sems.at[2 * j + 1]).wait()
        d = dot_nt(left_out[...], fv[cols, :])
        delta_pre[:, cols] = (d * (2.0 * jnp.sqrt(rect[:, cols].astype(F32)))).astype(BF)
        return 0
    lax.fori_loop(0, ff // tile, pre_tile, 0)
    save(delta_pre, 0)
    if times:
        save(delta_out, 4)
        save(delta_gate, 5)
    for c in loads[-5:]:
        c.wait()
    def hidden_tile(j, _):
        cols = cols_of(j)
        dh[:, cols] = dot_nt(delta_pre[...], fk[cols, :])
        dg[:, cols] = dot_nt(left_gate[...], fr[cols, :])
        return 0
    lax.fori_loop(0, width // tile, hidden_tile, 0)
    def leave(at):
        for i, z in ((1, delta), (2, branch)):
            saves.append(pltpu.make_async_copy(z.at[at, :], outs[i].at[at, :], row_sems.at[i - 1, at.start // (tokens // rows)]))
            saves[-1].start()
    norm_backward(middle, mean, scale, same, g2, b2, (ck, cr), (dh, dg), g, (delta, branch), sums, hats, first, second, rows, leave)
    save(sums, 3)
    for c in saves:
        c.wait()

def channel(rows, times, same, factor_out, factor_gate, g, p, rect, middle, mean, scale):
    (g1, b1, fade, bonus, mk, mv, mr, wk, wv, wr, wo, g2, b2, ck, cr, fk, fr, fv) = p
    tokens, width = g.shape
    ff = fk.shape[1]
    vm = pl.BlockSpec(memory_space=pltpu.VMEM)
    hbm = pl.BlockSpec(memory_space=pl.ANY)
    outs = [((tokens, ff), BF), ((tokens, width), F32), ((tokens, width), BF), ((8, width), F32)]
    outs += [((tokens, width), BF)] * 2 if times else [((16, LANES), BF)] * 2
    wide, wide32 = pltpu.VMEM((tokens, width), BF), pltpu.VMEM((tokens, width), F32)
    stat = pltpu.VMEM((tokens, LANES), F32)
    big = pltpu.VMEM((tokens, ff), BF)
    scratch = [pltpu.VMEM((ff, width), BF), pltpu.VMEM((width, ff), BF), pltpu.VMEM((width, width), BF), big, wide32, wide, wide, big, wide32, wide32]
    scratch += [stat] * 4 + [wide32, wide32, wide, pltpu.VMEM((8, width), F32), pltpu.SemaphoreType.DMA((2 * ff // 512 + 5,)), pltpu.SemaphoreType.DMA((6,)), pltpu.SemaphoreType.DMA((2, rows))]
    return pl.pallas_call(
        functools.partial(channel_kernel, rows, times),
        out_shape=tuple(jax.ShapeDtypeStruct(*o) for o in outs),
        in_specs=[vm] * 8 + [hbm] * 7,
        out_specs=(hbm,) * 6,
        scratch_shapes=scratch,
        compiler_params=pltpu.CompilerParams(vmem_limit_bytes=60 << 20),
        cost_estimate=pl.CostEstimate(flops=75000000000, bytes_accessed=217500000, transcendentals=0),
        name="channel",
    )(same, factor_out, factor_gate, g, g2, b2, ck, cr, rect, middle, mean, scale, fv, fk, fr)

def time_kernel(rows, *refs):
    (same_s, same, branch, h, g1, b1, fade, bonus, mk, mv, mr, wo_in, gate_in, ks_in, vs_in, tops_in, bottoms_in, wk_in, wv_in, wr_in, delta_in, mean_in, scale_in) = refs[:23]
    n_out = 5
    outs = refs[23:23 + n_out]
    (wo, gate, ks, vs, wk, wv, wr, delta, dm, gs, ys, tops, bottoms, dks, dvs, dk, dv, dr, ik, iv, ir, mean, scale, first, second, hats, state, sums, slab, in_sems, out_sems, row_sems) = refs[23 + n_out:]
    tokens, width = h.shape
    each = tokens // rows
    parts = width // LANES
    tile = 512
    sums[...] = jnp.zeros_like(sums)
    loads = fetch([(wo_in, wo), (gate_in, gate), (ks_in, ks), (vs_in, vs), (tops_in, tops), (bottoms_in, bottoms), (wk_in, wk), (wv_in, wv), (wr_in, wr), (delta_in, delta), (mean_in, mean), (scale_in, scale)], in_sems)
    saves = []
    def save(source, i):
        saves.append(pltpu.make_async_copy(source, outs[i], out_sems.at[i]))
        saves[-1].start()
    def cols_of(j):
        return pl.ds(pl.multiple_of(j * tile, tile), tile)
    loads[0].wait()
    loads[1].wait()
    def mixed_tile(j, _):
        cols = cols_of(j)
        d = dot_nt(branch[...], wo[cols, :])
        dm[:, cols] = d
        e = d * gate[:, cols]
        for row in range(rows):
            for c in range(tile // LANES):
                gs[pl.ds(row * each * parts + j * (tile // LANES) + c, each, stride=parts), :] = e[row * each:(row + 1) * each, c * LANES:(c + 1) * LANES]
        return 0
    lax.fori_loop(0, width // tile, mixed_tile, 0)
    for i in (2, 3, 4, 5):
        loads[i].wait()
    rate = jnp.exp(slabs(fade, slab))
    decay = jnp.exp(-rate)
    extra = slabs(bonus, slab)
    zero = jnp.zeros(decay.shape, F32)
    def back(i, carry):
        t = each - 1 - i
        dw, du = carry[:2]
        following = []
        for row in range(rows):
            here = pl.ds(pl.multiple_of((row * each + t) * parts, parts), parts)
            a, b = carry[2 + 2 * row], carry[3 + 2 * row]
            k, v = ks[here, :], vs[here, :]
            ek, now = jnp.exp(k), jnp.exp(extra + k)
            inverse = 1.0 / (bottoms[here, :] + now)
            y = (tops[here, :] + now * v) * inverse
            ys[here, :] = y
            ga = gs[here, :] * inverse
            gb = -ga * y
            q = now * (v * ga + gb)
            dks[here, :] = ek * (v * a + b) + q
            dvs[here, :] = ek * a + now * ga
            du = du + q
            dw = dw + (a * tops[here, :] + b * bottoms[here, :])
            m = same_s[row, t]
            following += [(ga + decay * a) * m, (gb + decay * b) * m]
        return (dw, du, *following)
    done = lax.fori_loop(0, each, back, (zero,) * (2 + 2 * rows), unroll=4)
    dfade = -done[0] * decay * rate
    for c in range(parts):
        sums[5:6, c * LANES:(c + 1) * LANES] = dfade[c:c + 1, :]
        sums[6:7, c * LANES:(c + 1) * LANES] = done[1][c:c + 1, :]
    for row in range(rows):
        def out_step(c, _, row=row):
            span = slice(row * each, (row + 1) * each)
            cols = lanes(c)
            at = pl.ds(row * each * parts + c, each, stride=parts)
            dk[span, cols] = dks[at, :].astype(BF)
            dv[span, cols] = dvs[at, :].astype(BF)
            s = gate[span, cols]
            dr[span, cols] = (dm[span, cols] * ys[at, :] * s * (1.0 - s)).astype(BF)
            return 0
        lax.fori_loop(0, parts, out_step, 0)
    for i, z in enumerate((dk, dv, dr)):
        save(z, i)
    for i in (6, 7, 8):
        loads[i].wait()
    def in_tile(j, _):
        cols = cols_of(j)
        ik[:, cols] = dot_nt(dk[...], wk[cols, :])
        iv[:, cols] = dot_nt(dv[...], wv[cols, :])
        ir[:, cols] = dot_nt(dr[...], wr[cols, :])
        return 0
    lax.fori_loop(0, width // tile, in_tile, 0)
    for c in loads[9:]:
        c.wait()
    def leave(at):
        saves.append(pltpu.make_async_copy(state.at[at, :], outs[3].at[at, :], row_sems.at[at.start // each]))
        saves[-1].start()
    norm_backward(h, mean, scale, same, g1, b1, (mk, mv, mr), (ik, iv, ir), delta, (state,), sums, hats, first, second, rows, leave)
    save(sums, 4)
    for c in saves:
        c.wait()

def time_mix(rows, dtype, same_s, same, branch, delta, h, p, gate, ks, vs, tops, bottoms, mean, scale):
    (g1, b1, fade, bonus, mk, mv, mr, wk, wv, wr, wo, g2, b2, ck, cr, fk, fr, fv) = p
    tokens, width = h.shape
    vm = pl.BlockSpec(memory_space=pltpu.VMEM)
    hbm = pl.BlockSpec(memory_space=pl.ANY)
    outs = [((tokens, width), BF)] * 3 + [((tokens, width), dtype), ((8, width), F32)]
    wide, wide32 = pltpu.VMEM((tokens, width), BF), pltpu.VMEM((tokens, width), F32)
    step32 = pltpu.VMEM(ks.shape, F32)
    stat = pltpu.VMEM((tokens, LANES), F32)
    square = pltpu.VMEM((width, width), BF)
    scratch = [square, wide32, step32, step32, square, square, square, wide32, wide32] + [step32] * 6 + [wide] * 3 + [wide32] * 3 + [stat] * 4 + [wide32]
    scratch += [pltpu.VMEM((tokens, width), dtype), pltpu.VMEM((8, width), F32), pltpu.VMEM((width // LANES, LANES), F32), pltpu.SemaphoreType.DMA((12,)), pltpu.SemaphoreType.DMA((5,)), pltpu.SemaphoreType.DMA((rows,))]
    return pl.pallas_call(
        functools.partial(time_kernel, rows),
        out_shape=tuple(jax.ShapeDtypeStruct(*o) for o in outs),
        in_specs=[pl.BlockSpec(memory_space=pltpu.SMEM)] + [vm] * 10 + [hbm] * 12,
        out_specs=(hbm,) * 5,
        scratch_shapes=scratch,
        compiler_params=pltpu.CompilerParams(vmem_limit_bytes=60 << 20),
        cost_estimate=pl.CostEstimate(flops=87000000000, bytes_accessed=252300000, transcendentals=0),
        name="time_mix",
    )(same_s, same, branch, h, g1, b1, fade, bonus, mk, mv, mr, wo, gate, ks, vs, tops, bottoms, wk, wv, wr, delta, mean, scale)


UNIT = 1024


def starts(parts):
    return [sum(c for c, _ in parts[:i]) for i in range(len(parts))]


def terms_kernel(count, parts, shapes, with_sums, with_factor, *refs):
    bits, refs = refs[0], refs[1:]
    if with_factor:
        factor, refs = refs[0], refs[1:]
    n, np_ = len(shapes), len(parts)
    left_in, right_in, refs = refs[:n], refs[n:2 * n], refs[2 * n:]
    if with_sums:
        early, late, *refs = refs
    outs, refs = refs[:2 * np_], refs[2 * np_:]
    lefts, rights, refs = refs[:n], refs[n:2 * n], refs[2 * n:]
    bufs, (in_sems, out_sems) = refs[:np_], refs[np_:]
    sends, keeps = outs[::2], outs[1::2]
    tile = 512
    columns = starts(parts)

    def place(order, d):
        bit = [(d >> b) & 1 if isinstance(d, int) else lax.rem(lax.div(d, 1 << b), 2) for b in order]
        return bit[0] ^ bits[order[0]], bit[1] * 4 + bit[2] * 2 + bit[3]

    chunk_base = [sum(kin // tile for kin, _ in shapes[:m]) for m in range(n)]

    def load(m, j):
        cols = pl.ds(pl.multiple_of(j * tile, tile), tile)
        return pltpu.make_async_copy(left_in[m].at[:, cols], lefts[m].at[:, cols], in_sems.at[chunk_base[m] + j])

    right_base = [chunk_base[-1] + shapes[-1][0] // tile + sum(width // UNIT for _, width in shapes[:m]) for m in range(n)]

    def load_right(m, q):
        cols = slice(q * UNIT, (q + 1) * UNIT)
        return pltpu.make_async_copy(right_in[m].at[:, cols], rights[m].at[:, cols], in_sems.at[right_base[m] + q])

    for m, (kin, width) in enumerate(shapes):
        load_right(m, 0).start()
        for j in range(kin // tile):
            load(m, j).start()
        for q in range(1, width // UNIT):
            load_right(m, q).start()
    waits = []
    base = 0
    blocks = 0
    for m, ((kin, width), left, right) in enumerate(zip(shapes, lefts, rights)):
        rows = kin // count
        per = tile // rows
        for q in range(width // UNIT):
            load_right(m, q).wait()
            if with_factor:
                right[...] = (right[...].astype(F32) * factor[...].astype(F32)).astype(BF)

            def step(j, _, m=m, q=q, left=left, right=right, rows=rows, per=per, base=base):
                if q == 0:
                    load(m, j).wait()
                lhs = left[:, pl.ds(pl.multiple_of(j * tile, tile), tile)]
                for i, (cols, order) in enumerate(parts):
                    at = q * UNIT + columns[i]
                    res = lax.dot_general(lhs, right[:, at:at + cols], (((0,), (0,)), ((), ())), preferred_element_type=F32).astype(BF)
                    for s in range(per):
                        relative, index = place(order, j * per + s)
                        bufs[i][relative, index, base:base + rows, :] = res[s * rows:(s + 1) * rows]
                        if rows >= 256:
                            source = bufs[i].at[relative, index]
                            for r, target in ((1, sends[i]), (0, keeps[i])):
                                @pl.when(relative == r)
                                def _(source=source, target=target, index=index, i=i):
                                    pltpu.make_async_copy(source, target.at[index], out_sems.at[i, j * per + s]).start()
                return 0

            lax.fori_loop(0, kin // tile, step, 0)
            for i in range(np_):
                if rows >= 256:
                    for j in range(count):
                        waits.append(pltpu.make_async_copy(bufs[i].at[0, 0], keeps[i].at[0], out_sems.at[i, j]))
                else:
                    for r, target in ((1, sends[i]), (0, keeps[i])):
                        c = pltpu.make_async_copy(bufs[i].at[r, :, base:base + rows, :], target.at[:, base:base + rows, :], out_sems.at[i, 2 * blocks + r])
                        c.start()
                        waits.append(c)
            base += rows
            blocks += 1
    if with_sums:
        share = early.shape[1] // count
        both = jnp.concatenate([early[...], late[...]], axis=0)
        for buf in bufs:
            buf[:, :, base:base + 16, :] = jnp.zeros(buf.shape[:2] + (16, buf.shape[3]), BF)
        for d in range(count):
            column = d * share // LANES * LANES
            piece = both[:, column:column + LANES]
            if d * share - column:
                piece = pltpu.roll(piece, LANES - (d * share - column), 1)
            relative, index = place(parts[0][1], d)
            bufs[0][relative, index, base:base + 16, 0:LANES] = piece.astype(BF)
        for i in range(np_):
            for r, target in ((1, sends[i]), (0, keeps[i])):
                c = pltpu.make_async_copy(bufs[i].at[r, :, base:base + 16, :], target.at[:, base:base + 16, :], out_sems.at[i, 2 * blocks + r])
                c.start()
                waits.append(c)
    for c in waits:
        c.wait()


def terms(bits, parts, pairs, sums=(), factor=None):
    count = 16
    lefts, rights = zip(*pairs)
    shapes = tuple((a.shape[1], b.shape[1]) for a, b in pairs)
    tokens = lefts[0].shape[0]
    rows = sum(kin // count * (width // UNIT) for kin, width in shapes) + (16 if sums else 0)
    outs, bufs = [], []
    for cols, _ in parts:
        outs += [jax.ShapeDtypeStruct((count // 2, rows, cols), BF)] * 2
        bufs.append(pltpu.VMEM((2, count // 2, rows, cols), BF))
    flops = sum(2 * tokens * kin * width for kin, width in shapes)
    result = pl.pallas_call(
        functools.partial(terms_kernel, count, parts, shapes, bool(sums), factor is not None),
        out_shape=tuple(outs),
        in_specs=[SM] + [VM] * (factor is not None) + [HBM] * (2 * len(shapes)) + [VM] * len(sums),
        out_specs=(HBM,) * len(outs),
        scratch_shapes=[pltpu.VMEM(x.shape, BF) for x in (*lefts, *rights)]
        + bufs + [pltpu.SemaphoreType.DMA((sum(kin // 512 + width // UNIT for kin, width in shapes),)), pltpu.SemaphoreType.DMA((len(parts), 16))],
        compiler_params=pltpu.CompilerParams(vmem_limit_bytes=56 << 20),
        cost_estimate=pl.CostEstimate(flops=39000000000, bytes_accessed=113100000, transcendentals=0),
        name="terms",
    )(bits, *(() if factor is None else (factor,)), *lefts, *rights, *sums)
    return list(zip(result[::2], result[1::2]))


def swap(block, bit):
    count = lax.axis_size("dp")
    return lax.ppermute(block, "dp", [(i, i ^ (1 << bit)) for i in range(count)])


def summed(kept, came, dtype=BF):
    return (kept.astype(F32) + came.astype(F32)).astype(dtype)


def advance_kernel(bits, kept_go, came_go, kept_stay, came_stay, send, keep):
    send[...] = summed(kept_go[...], came_go[...])
    keep[...] = summed(kept_stay[...], came_stay[...])


def advance(bits, kept, came, bit):
    lead, rows, cols = kept.shape
    half = lead // 2
    block = rows
    go = pl.BlockSpec((1, block, cols), lambda g, i, b: ((1 - b[bit]) * half + g, i, 0))
    stay = pl.BlockSpec((1, block, cols), lambda g, i, b: (b[bit] * half + g, i, 0))
    out = pl.BlockSpec((1, block, cols), lambda g, i, b: (g, i, 0))
    return pl.pallas_call(
        advance_kernel,
        out_shape=(jax.ShapeDtypeStruct((half, rows, cols), BF),) * 2,
        grid_spec=pltpu.PrefetchScalarGridSpec(
            num_scalar_prefetch=1, grid=(half, rows // block), in_specs=[go, go, stay, stay], out_specs=(out, out)
        ),
        compiler_params=pltpu.CompilerParams(vmem_limit_bytes=30 << 20),
        cost_estimate=pl.CostEstimate(flops=9000000000, bytes_accessed=26100000, transcendentals=0),
        name="advance",
    )(bits, kept, came, kept, came)


def final_kernel(pieces, parts, *refs):
    n = len(parts)
    ins, outs = refs[:2 * n], refs[2 * n:]
    for (row, rows, blocks, columns), out in zip(pieces, outs):
        for q in range(blocks):
            span = slice(row + q * rows, row + (q + 1) * rows)
            if columns < UNIT:
                out[...] = summed(ins[0][0, span, 0:LANES], ins[1][0, span, 0:LANES], F32)[:, :columns]
                continue
            for i, at in enumerate(starts(parts)):
                out[:, q * UNIT + at:q * UNIT + at + parts[i][0]] = summed(ins[2 * i][0, span, :], ins[2 * i + 1][0, span, :], F32)


def final(parts, pieces, arrays):
    size = sum(a.size for a in arrays)
    return pl.pallas_call(
        functools.partial(final_kernel, pieces, parts),
        out_shape=tuple(jax.ShapeDtypeStruct((rows, blocks * columns), F32) for row, rows, blocks, columns in pieces),
        in_specs=[VM] * len(arrays),
        out_specs=(VM,) * len(pieces),
        compiler_params=pltpu.CompilerParams(vmem_limit_bytes=40 << 20),
        cost_estimate=pl.CostEstimate(flops=4500000000, bytes_accessed=13050000, transcendentals=0),
        name="final",
    )(*arrays)


def after(value, *earlier):
    return lax.optimization_barrier((value, earlier))[0]


def values_kernel(orders, offset, bits, own, *refs):
    ins, refs = refs[:6], refs[6:]
    outs, refs = refs[:4], refs[4:]
    held, mine_d, (bufs, in_sems, out_sems) = refs[:6], refs[6], refs[7:]
    width = mine_d.shape[1]
    loads = [pltpu.make_async_copy(own, mine_d, in_sems.at[0])]
    for i in (0, 1):
        kept, came, delta = ins[3 * i:3 * i + 3]
        loads += [
            pltpu.make_async_copy(kept, held[3 * i], in_sems.at[3 * i + 1]),
            pltpu.make_async_copy(came.at[:, 0:width], held[3 * i + 1], in_sems.at[3 * i + 2]),
            pltpu.make_async_copy(delta.at[:, offset:offset + width], held[3 * i + 2], in_sems.at[3 * i + 3]),
        ]
    for c in loads:
        c.start()
    loads[0].wait()
    tile = 512
    waits = []

    def dot_tn(left, right):
        return lax.dot_general(left, right, (((0,), (0,)), ((), ())), preferred_element_type=F32)

    for i in (0, 1):
        for c in loads[3 * i + 1:3 * i + 4]:
            c.wait()
        kept, came, delta = held[3 * i:3 * i + 3]

        def step(n, _, i=i, kept=kept, came=came, delta=delta):
            j, q = n // 2, n % 2
            rows = pl.ds(pl.multiple_of(j * tile, tile), tile)
            cols = pl.ds(pl.multiple_of(q * tile, tile), tile)
            res = (dot_tn(kept[:, rows], mine_d[:, cols]) + dot_tn(came[:, rows], delta[:, cols])).astype(BF)
            for s in (0, 1):
                bufs[i, j, s, :, cols] = res[s * 256:(s + 1) * 256]
            return 0

        lax.fori_loop(0, 4, step, 0)
        for j in (0, 1):
            for r, target in ((1, outs[2 * i]), (0, outs[2 * i + 1])):
                copy = pltpu.make_async_copy(bufs.at[i, j], target, out_sems.at[i, j])
                @pl.when((j ^ bits[orders[i][1]]) == r)
                def _(copy=copy):
                    copy.start()
            waits.append(copy)
    for c in waits:
        c.wait()


def values(bits, orders, offset, own, parts):
    tokens, width = own.shape
    out = jax.ShapeDtypeStruct((2, 256, width), BF)
    wide = pltpu.VMEM((tokens, width), BF)
    result = pl.pallas_call(
        functools.partial(values_kernel, orders, offset),
        out_shape=(out,) * 4,
        in_specs=[SM] + [HBM] * 7,
        out_specs=(HBM,) * 4,
        scratch_shapes=[wide] * 7 + [pltpu.VMEM((2, 2, 2, 256, width), BF), pltpu.SemaphoreType.DMA((7,)), pltpu.SemaphoreType.DMA((2, 2))],
        compiler_params=pltpu.CompilerParams(vmem_limit_bytes=56 << 20),
        cost_estimate=pl.CostEstimate(flops=30000000000, bytes_accessed=87000000, transcendentals=0),
        name="values",
    )(bits, own, *parts[0], *parts[1])
    return list(zip(result[::2], result[1::2]))


def cross_kernel(bits, kept_a, came_a, kept_b, came_b, send, keep):
    low, high = summed(kept_a[...], came_a[...]), summed(kept_b[...], came_b[...])

    @pl.when(bits[3] == 0)
    def _():
        send[...] = high
        keep[...] = low

    @pl.when(bits[3] == 1)
    def _():
        send[...] = low
        keep[...] = high


def cross(bits, arrays):
    out = jax.ShapeDtypeStruct(arrays[0].shape, BF)
    return pl.pallas_call(
        cross_kernel,
        out_shape=(out, out),
        in_specs=[SM] + [VM] * 4,
        out_specs=(VM, VM),
        compiler_params=pltpu.CompilerParams(vmem_limit_bytes=30 << 20),
        cost_estimate=pl.CostEstimate(flops=4500000000, bytes_accessed=13050000, transcendentals=0),
        name="cross",
    )(bits, *arrays)


class Line:
    def __init__(self, bits, plan, pieces):
        self.bits, self.plan, self.pieces, self.token, self.flight, self.sums = bits, plan, pieces, None, {}, {}

    def tie(self, value):
        return value if self.token is None else after(value, self.token)

    def open(self, group, pairs, sums=(), factor=None):
        pairs = ((self.tie(pairs[0][0]), pairs[0][1]),) + tuple(pairs[1:])
        found = terms(self.bits, self.plan[group], pairs, sums, factor)
        self.token = found
        for i, (send, keep) in enumerate(found):
            self.flight[group, i] = keep, swap(send, self.plan[group][i][1][0])

    def join(self, offset, own, parts):
        orders = tuple(order for _, order in self.plan["a"])
        found = values(self.bits, orders, offset, self.tie(own), parts)
        self.token = found
        for i, (send, keep) in enumerate(found):
            self.flight["a", i] = keep, swap(send, orders[i][1])

    def serve(self, steps):
        for group, i, stage in steps:
            parts = self.plan[group]
            if group == "a" and stage == 3:
                send, keep = cross(self.bits, self.tie(self.flight.pop(("a", 0)) + self.flight.pop(("a", 1))))
                self.token = send, keep
                self.flight["a", 0] = keep, swap(send, 3)
            elif group == "a" and stage == 4:
                self.sums["a"] = final(((UNIT, None),), self.pieces["a"], self.tie(list(self.flight.pop(("a", 0)))))
                self.token = self.sums["a"][0]
            elif stage < 4:
                kept, came = self.tie(self.flight[group, i])
                send, keep = advance(self.bits, kept, came, parts[i][1][stage])
                self.token = send, keep
                self.flight[group, i] = keep, swap(send, parts[i][1][stage])
            else:
                self.sums[group, i] = self.flight.pop((group, i))
                if all((group, k) in self.sums for k in range(len(parts))):
                    arrays = [a for k in range(len(parts)) for a in self.sums[group, k]]
                    arrays[0] = self.tie(arrays[0])
                    self.sums[group] = final(parts, self.pieces[group], arrays)
                    self.token = self.sums[group][0]


def halving(left, right=None):
    count = lax.axis_size("dp")
    bits = count.bit_length() - 1
    me = lax.axis_index("dp")
    if right is not None:
        left = lax.dot_general(left, right, (((0,), (0,)), ((), ())), preferred_element_type=F32).astype(BF)
    current = left.reshape((2,) * bits + (left.shape[0] // count, left.shape[1]))
    for bit in range(bits):
        axis = bits - 1 - bit
        mine = (me >> bit) & 1
        send = lax.dynamic_index_in_dim(current, 1 - mine, axis, keepdims=False)
        keep = lax.dynamic_index_in_dim(current, mine, axis, keepdims=False)
        current = summed(keep, swap(send, bit), BF if bit + 1 < bits else F32)
    return current


def unwritten(function, *args):
    shapes, tree = jax.tree.flatten(jax.eval_shape(function, *args))
    outs = pl.pallas_call(
        lambda *refs: None, out_shape=tuple(shapes), out_specs=(HBM,) * len(shapes), name="unwritten"
    )()
    return jax.tree.unflatten(tree, outs)


VECTORS = (0, 1, 5, 6, 2, 3, 4, 8, 9, 10, 11)
PARTS_0 = dict(
    a=((512, (2, 1, 0, 3)), (512, (1, 2, 0, 3))),
    b=((512, (1, 2, 0, 3)), (512, (0, 1, 2, 3))),
    e=((512, (2, 0, 1, 3)), (512, (1, 0, 2, 3))),
)
PARTS_1 = dict(
    a=((512, (1, 2, 0, 3)), (512, (2, 1, 0, 3))),
    b=((512, (2, 0, 1, 3)), (512, (0, 2, 1, 3))),
    e=((512, (1, 0, 2, 3)), (512, (2, 0, 1, 3))),
)
ORDER_1 = ('a', 'b', 'e')
STEPS_0 = (('a', 1, 2), ('b', 0, 1), ('a', 0, 2), ('b', 1, 1), ('e', 1, 1), ('e', 0, 1), ('a', 0, 3), ('b', 1, 2), ('b', 0, 2), ('e', 1, 2), ('a', 0, 4), ('e', 0, 2), ('b', 1, 3), ('b', 0, 3), ('e', 0, 3), ('e', 1, 3), ('b', 1, 4), ('b', 0, 4), ('e', 0, 4), ('e', 1, 4))
STEPS_1 = (('a', 0, 2), ('a', 1, 2), ('b', 0, 1), ('e', 0, 1), ('b', 1, 1), ('e', 1, 1), ('a', 0, 3), ('b', 1, 2), ('b', 0, 2), ('a', 0, 4), ('b', 1, 3), ('b', 0, 3), ('e', 0, 2), ('b', 1, 4), ('b', 0, 4), ('e', 1, 2), ('e', 0, 3), ('e', 1, 3), ('e', 0, 4), ('e', 1, 4))


def local(entry_pair, labels, *params):
    count = lax.axis_size("dp")
    section = lax.axis_index("section")
    rows, each, width = entry_pair.shape[1:]
    own = entry_pair.reshape(rows * each, width)
    share = width // count
    p = [e if e.ndim == 2 else e[0] for e in params]
    ff = p[15].shape[1]
    first = jnp.zeros((rows, 1), F32)
    same_s = jnp.concatenate([first, (labels[:, 1:] == labels[:, :-1]).astype(F32)], axis=1)
    same = jnp.broadcast_to(same_s.reshape(rows * each, 1), (rows * each, LANES))
    fast = count == 16 and width == UNIT
    me = lax.axis_index("dp")
    bits = jnp.stack([(me >> i) & 1 for i in range(4)])
    wide = ff // width
    pieces = dict(
        a=((0, ff // count, 1, width),),
        b=((0, share, wide, width), (share * wide, share, 1, width), (share * (wide + 1), share, 1, width)),
        e=tuple((i * share, share, 1, width) for i in range(3)) + tuple((3 * share + i, 1, 1, share) for i in VECTORS),
    )

    def plain_rest(pairs, sums):
        together = jnp.concatenate(sums).astype(BF).reshape(16, count, share).transpose(1, 0, 2).reshape(count * 16, share)
        vectors = halving(together)
        return tuple(halving(*pair) for pair in pairs) + tuple(vectors[i:i + 1] for i in VECTORS)

    def orders(plan):
        return tuple(order for _, order in plan["a"]) if fast else None

    def start():
        return forward(rows, False, same_s, same, own, p, own, bits, orders(PARTS_0))

    def middle_part(received):
        kept = forward(rows, True, same_s, same, received, p, own, bits, orders(PARTS_1))
        (key_in, value_in, recept_in, ks, vs, gate, tops, bottoms, mixed, middle, hidden_in, gate_in, act, result, delta_out, delta_gate, mean, scale, mean2, scale2, *acts) = kept
        begun = act, delta_out
        if fast:
            came = [swap(acts[2 * i], PARTS_1["a"][i][1][0]) for i in (0, 1)]
            begun = delta_out, [(acts[2 * i + 1], came[i]) for i in (0, 1)]
        g = after(own, acts[0]) if fast else own
        delta_pre, delta, branch, late, _, _ = channel(rows, False, same, delta_out, delta_gate, g, p, act, middle, mean2, scale2)
        dk, dv, dr, state, early = time_mix(rows, BF, same_s, same, branch, delta, received, p, gate, ks, vs, tops, bottoms, mean, scale)
        key_pairs = ((hidden_in, delta_pre), (gate_in, delta_gate), (mixed, branch))
        return state, result, begun, (early, late), key_pairs, ((key_in, dk), (value_in, dv), (recept_in, dr))

    def end_first(received, kept, acts_came):
        (key_in, value_in, recept_in, ks, vs, gate, tops, bottoms, mixed, middle, hidden_in, gate_in, act, result, factor_out, factor_gate, mean, scale, mean2, scale2, *acts) = kept
        line = Line(bits, PARTS_0, pieces)
        if fast:
            own_delta = (received.astype(F32) * factor_out.astype(F32)).astype(BF)
            came = [swap(own_delta, PARTS_0["a"][i][1][0]) for i in (0, 1)]
            line.token = own_delta
        g = line.tie(received)
        delta_pre, delta, branch, late, delta_out, delta_gate = channel(rows, True, same, factor_out, factor_gate, g, p, act, middle, mean2, scale2)
        key_pairs = ((hidden_in, delta_pre), (gate_in, delta_gate), (mixed, branch))
        line.token = branch
        if fast:
            line.open("b", key_pairs)
            line.join(0, own_delta, [(acts[2 * i + 1], acts_came[i], came[i]) for i in (0, 1)])
        dk, dv, dr, state, early = time_mix(rows, F32, same_s, same, line.tie(branch), delta, own, p, gate, ks, vs, tops, bottoms, mean, scale)
        rest_pairs = ((key_in, dk), (value_in, dv), (recept_in, dr))
        if not fast:
            return state, (halving(act, delta_out),), tuple(halving(*pair) for pair in key_pairs), plain_rest(rest_pairs, (early, late))
        line.token = state
        line.open("e", rest_pairs, (early, late))
        line.serve(STEPS_0)
        return state, line.sums["a"], line.sums["b"], line.sums["e"]

    def end_second(result, begun, sums, key_pairs, rest_pairs):
        if not fast:
            return result.astype(F32), (halving(*begun),), tuple(halving(*pair) for pair in key_pairs), plain_rest(rest_pairs, sums)
        line = Line(bits, PARTS_1, pieces)
        for name in ORDER_1:
            if name == "a":
                line.join(width, begun[0], [(kept, came, came) for kept, came in begun[1]])
            elif name == "b":
                line.open("b", key_pairs)
            else:
                line.open("e", rest_pairs, sums)
        line.serve(STEPS_1)
        return result.astype(F32), line.sums["a"], line.sums["b"], line.sums["e"]

    def swap_first(block, bit):
        return lax.ppermute(block, ("section", "dp"), [(i, i ^ (1 << bit)) for i in range(count)])

    kept = lax.cond(section == 0, start, lambda: unwritten(start))
    received = lax.ppermute(kept[13], "section", [(0, 1)])
    acts_came = [swap_first(kept[20 + 2 * i], PARTS_0["a"][i][1][0]) for i in (0, 1)] if fast else []
    delta, *pending = lax.cond(section == 1, middle_part, lambda r: unwritten(middle_part, r), received)
    received = lax.ppermute(delta, "section", [(1, 0)])
    ends, (value_sum,), (key_sum, gate_sum, exit_sum), rest = lax.cond(
        section == 0, lambda r, k, a, q: end_first(r, k, a), lambda r, k, a, q: end_second(*q), received, kept, acts_came, pending
    )
    ends = ends.reshape(rows, each, width)
    everything = (ends, *(z[0] for z in rest[3:10]), *rest[:3], exit_sum, *(z[0] for z in rest[10:14]), key_sum, gate_sum, value_sum)
    return tuple(e[None] for e in everything)


def solution(mesh):
    vec, mat = P("section", None), P("section", None, None)
    in_specs = (P("section", "dp", None, None), P("dp", None)) + (vec,) * 7 + (mat,) * 4 + (vec,) * 4 + (mat,) * 3
    vec, mat = P("section", "dp"), P("section", "dp", None)
    out_specs = (P("section", "dp", None, None),) + (vec,) * 7 + (mat,) * 4 + (vec,) * 4 + (mat,) * 3
    return jax.shard_map(local, mesh=mesh, in_specs=in_specs, out_specs=out_specs, check_vma=False)
```

```python
import functools

import jax
import jax.numpy as jnp
from jax import lax
from jax.experimental import pallas as pl
from jax.experimental.pallas import tpu as pltpu
from jax.sharding import PartitionSpec as P

BF = jnp.bfloat16
F32 = jnp.float32
LANES = 128
VM = pl.BlockSpec(memory_space=pltpu.VMEM)
HBM = pl.BlockSpec(memory_space=pl.ANY)
SM = pl.BlockSpec(memory_space=pltpu.SMEM)

def dot(left, right):
    return jnp.dot(left, right, preferred_element_type=F32)

def dot_nt(left, right):
    return lax.dot_general(left, right, (((1,), (1,)), ((), ())), preferred_element_type=F32)

def lanes(c):
    return pl.ds(pl.multiple_of(c * LANES, LANES), LANES)

def slabs(vector, scratch):
    for c in range(scratch.shape[0]):
        scratch[c:c + 1, :] = vector[:, c * LANES:(c + 1) * LANES].astype(F32)
    return scratch[...]

def statistics(source, mean, scale, tokens, width, chunk=128):
    def step(i, _):
        at = pl.ds(pl.multiple_of(i * chunk, chunk), chunk)
        x = source[at, :].astype(F32)
        m = jnp.sum(x, axis=1, keepdims=True) * (1.0 / width)
        x = x - m
        v = jnp.sum(x * x, axis=1, keepdims=True) * (1.0 / width)
        mean[at, :] = jnp.broadcast_to(m, (chunk, LANES))
        scale[at, :] = jnp.broadcast_to(lax.rsqrt(v + 1e-05), (chunk, LANES))
        return 0
    lax.fori_loop(0, tokens // chunk, step, 0)

def mix_into(source, mean, scale, same, gain, bias, factors, targets, width):
    def step(c, _):
        cols = lanes(c)
        z = (source[:, cols].astype(F32) - mean[...]) * scale[...] * gain[:, cols].astype(F32) + bias[:, cols].astype(F32)
        before = pltpu.roll(z, 1, 0) * same[...]
        step_up = z - before
        for factor, target in zip(factors, targets):
            target[:, cols] = (before + step_up * factor[:, cols].astype(F32)).astype(BF)
        return 0
    lax.fori_loop(0, width // LANES, step, 0)

def fetch(pairs, sems):
    copies = [pltpu.make_async_copy(s, d, sems.at[i]) for i, (s, d) in enumerate(pairs)]
    for c in copies:
        c.start()
    return copies

def forward_kernel(rows, with_delta, orders, *refs):
    if orders:
        bits, refs = refs[0], refs[1:]
    (same_s, same, h, g1, b1, fade, bonus, mk, mv, mr, g2, b2, ck, cr, cot) = refs[:15]
    weights = refs[15:22]
    n_out = 20
    outs = refs[22:22 + n_out]
    if orders:
        pieces, piece_sems, refs = refs[22 + n_out:26 + n_out], refs[-1], refs[:22 + n_out] + refs[26 + n_out:-1]
    (wk, wv, wr, wo, fk, fr, fv, mean, scale, mean2, scale2, key_in, value_in, recept_in, ks, vs, ys, tops, bottoms, gate, mixed, middle,
     hidden_in, gate_in, act, slab, in_sems, out_sems) = refs[22 + n_out:]
    tokens, width = h.shape
    each = tokens // rows
    parts = width // LANES
    tile = 512
    large = 1024
    ff = act.shape[1]
    loads = fetch(list(zip(weights, (wk, wv, wr, wo, fk, fr, fv))), in_sems)
    saves = []

    def save(source):
        i = len(saves)
        saves.append(pltpu.make_async_copy(source, outs[i], out_sems.at[i]))
        saves[-1].start()

    statistics(h, mean, scale, tokens, width)
    mix_into(h, mean, scale, same, g1, b1, (mk, mv, mr), (key_in, value_in, recept_in), width)
    for z in (key_in, value_in, recept_in):
        save(z)

    def cols_of(j):
        return pl.ds(pl.multiple_of(j * tile, tile), tile)

    def steps_tile(values, target, j):
        for row in range(rows):
            for c in range(tile // LANES):
                target[pl.ds(row * each * parts + j * (tile // LANES) + c, each, stride=parts), :] = values[row * each:(row + 1) * each, c * LANES:(c + 1) * LANES]

    loads[0].wait()
    def key_tile(j, _):
        steps_tile(dot(key_in[...], wk[:, cols_of(j)]), ks, j)
        return 0
    lax.fori_loop(0, width // tile, key_tile, 0)
    loads[1].wait()
    def value_tile(j, _):
        steps_tile(dot(value_in[...], wv[:, cols_of(j)]), vs, j)
        return 0
    lax.fori_loop(0, width // tile, value_tile, 0)
    save(ks)
    save(vs)
    loads[2].wait()
    def accept_tile(j, _):
        gate[:, cols_of(j)] = jax.nn.sigmoid(dot(recept_in[...], wr[:, cols_of(j)]))
        return 0
    lax.fori_loop(0, width // tile, accept_tile, 0)
    save(gate)

    decay = jnp.exp(-jnp.exp(slabs(fade, slab)))
    extra = slabs(bonus, slab)
    def step(t, carry):
        following = []
        for row in range(rows):
            here = pl.ds(pl.multiple_of((row * each + t) * parts, parts), parts)
            m = same_s[row, t]
            top, bottom = carry[2 * row] * m, carry[2 * row + 1] * m
            tops[here, :] = top
            bottoms[here, :] = bottom
            k, v = ks[here, :], vs[here, :]
            ek, now = jnp.exp(k), jnp.exp(extra + k)
            ys[here, :] = (top + now * v) / (bottom + now)
            following += [decay * top + ek * v, decay * bottom + ek]
        return tuple(following)
    zero = jnp.zeros(decay.shape, F32)
    lax.fori_loop(0, each, step, (zero,) * (2 * rows), unroll=4)
    save(tops)
    save(bottoms)

    for row in range(rows):
        def mixed_step(c, _, row=row):
            y = ys[pl.ds(row * each * parts + c, each, stride=parts), :]
            mixed[row * each:(row + 1) * each, lanes(c)] = (gate[row * each:(row + 1) * each, lanes(c)] * y).astype(BF)
            return 0
        lax.fori_loop(0, parts, mixed_step, 0)
    save(mixed)
    loads[3].wait()
    def middle_tile(j, _):
        middle[:, cols_of(j)] = h[:, cols_of(j)].astype(F32) + dot(mixed[...], wo[:, cols_of(j)])
        return 0
    lax.fori_loop(0, width // tile, middle_tile, 0)
    save(middle)

    statistics(middle, mean2, scale2, tokens, width)
    mix_into(middle, mean2, scale2, same, g2, b2, (ck, cr), (hidden_in, gate_in), width)
    save(hidden_in)
    save(gate_in)
    loads[4].wait()
    def hidden_tile(j, _):
        cols = pl.ds(pl.multiple_of(j * large, large), large)
        r = jnp.maximum(dot(hidden_in[...], fk[:, cols]), 0.0)
        act[:, cols] = (r * r).astype(BF)
        return 0
    lax.fori_loop(0, ff // large, hidden_tile, 0)
    save(act)
    piece_waits = []
    if orders:
        share = ff // 16
        for d in range(16):
            first, one, two = orders[d >> 3][:3]
            source = act.at[:, d * share:(d + 1) * share]
            column = (((d >> one) & 1) * 2 + ((d >> two) & 1)) * share
            relative = ((d >> first) & 1) ^ bits[first]
            for r, target in ((1, pieces[2 * (d >> 3)]), (0, pieces[2 * (d >> 3) + 1])):
                copy = pltpu.make_async_copy(source, target.at[:, column:column + share], piece_sems.at[d])
                @pl.when(relative == r)
                def _(copy=copy):
                    copy.start()
            piece_waits.append(copy)
    for i in (0, 1, 2, 5):
        saves[i].wait()
    result, delta_out, delta_gate = key_in, value_in, recept_in
    loads[5].wait()
    def gate_tile(j, _):
        gate[:, cols_of(j)] = jax.nn.sigmoid(dot(gate_in[...], fr[:, cols_of(j)]))
        return 0
    lax.fori_loop(0, width // tile, gate_tile, 0)
    loads[6].wait()
    def out_tile(j, _):
        cols = cols_of(j)
        o = dot(act[...], fv[:, cols])
        s = gate[:, cols]
        result[:, cols] = (middle[:, cols] + s * o).astype(BF)
        g = cot[:, cols].astype(F32)
        if with_delta:
            delta_out[:, cols] = (g * s).astype(BF)
            delta_gate[:, cols] = (g * o * s * (1.0 - s)).astype(BF)
        else:
            delta_out[:, cols] = s.astype(BF)
            delta_gate[:, cols] = (o * s * (1.0 - s)).astype(BF)
        return 0
    lax.fori_loop(0, width // tile, out_tile, 0)
    save(result)
    save(delta_out)
    save(delta_gate)
    for z in (mean, scale, mean2, scale2):
        save(z)
    if orders and with_delta:
        for i in (0, 1):
            piece_waits.append(pltpu.make_async_copy(delta_out, pieces[2 * i].at[:, width:2 * width], piece_sems.at[16 + i]))
            piece_waits[-1].start()
    for copy in piece_waits:
        copy.wait()
    for i, c in enumerate(saves):
        if i not in (0, 1, 2, 5):
            c.wait()

def forward(rows, with_delta, same_s, same, h, p, cot, bits=None, orders=None):
    (g1, b1, fade, bonus, mk, mv, mr, wk, wv, wr, wo, g2, b2, ck, cr, fk, fr, fv) = p
    tokens, width = h.shape
    ff = fk.shape[1]
    vm = pl.BlockSpec(memory_space=pltpu.VMEM)
    hbm = pl.BlockSpec(memory_space=pl.ANY)
    slabs = tokens * width // LANES
    outs = [((tokens, width), BF)] * 3 + [((slabs, LANES), F32)] * 2 + [((tokens, width), F32)] + [((slabs, LANES), F32)] * 2
    outs += [((tokens, width), BF), ((tokens, width), F32)]
    outs += [((tokens, width), BF)] * 2 + [((tokens, ff), BF)] + [((tokens, width), BF)] * 3
    outs = outs[:14] if False else outs
    outs += [((tokens, LANES), F32)] * 4
    wide, wide32, step32 = pltpu.VMEM((tokens, width), BF), pltpu.VMEM((tokens, width), F32), pltpu.VMEM((slabs, LANES), F32)
    stat = pltpu.VMEM((tokens, LANES), F32)
    square = pltpu.VMEM((width, width), BF)
    big = pltpu.VMEM((tokens, ff), BF)
    scratch = [square] * 4 + [pltpu.VMEM((width, ff), BF), square, pltpu.VMEM((ff, width), BF), stat, stat, stat, stat] + [wide] * 3
    scratch += [step32] * 5 + [wide32, wide, wide32, wide, wide, big]
    scratch += [pltpu.VMEM((width // LANES, LANES), F32), pltpu.SemaphoreType.DMA((7,)), pltpu.SemaphoreType.DMA((len(outs),))]
    if orders:
        sent = (tokens, width * (1 + with_delta))
        outs += [(sent, BF), ((tokens, width), BF)] * 2
        scratch.append(pltpu.SemaphoreType.DMA((18,)))
    smem = pl.BlockSpec(memory_space=pltpu.SMEM)
    return pl.pallas_call(
        functools.partial(forward_kernel, rows, with_delta, orders),
        out_shape=tuple(jax.ShapeDtypeStruct(*o) for o in outs),
        in_specs=[smem] * (orders is not None) + [smem] + [vm] * 14 + [hbm] * 7,
        out_specs=(hbm,) * len(outs),
        scratch_shapes=scratch,
        compiler_params=pltpu.CompilerParams(vmem_limit_bytes=60 << 20),
        cost_estimate=pl.CostEstimate(flops=90000000000, bytes_accessed=261000000, transcendentals=0),
        name="forward",
    )(*([bits] if orders else []), same_s, same, h, g1, b1, fade, bonus, mk, mv, mr, g2, b2, ck, cr, cot, wk, wv, wr, wo, fk, fr, fv)

def norm_backward(source, mean, scale, same, gain, bias, factors, grads, residual, targets, sums, hats, first, second, rows, leave):
    tokens, width = source.shape
    each = tokens // rows
    spans = [slice(row * each, (row + 1) * each) for row in range(rows)]

    def gather(c, carry):
        cols = lanes(c)
        g, b = gain[:, cols].astype(F32), bias[:, cols].astype(F32)
        following = []
        totals = [0.0] * (2 + len(grads))
        for row, at in enumerate(spans):
            hat = (source[at, cols].astype(F32) - mean[at, :]) * scale[at, :]
            z = hat * g + b
            step_up = z - pltpu.roll(z, 1, 0) * same[at, :]
            straight = rest = None
            for i, (factor, grad) in enumerate(zip(factors, grads)):
                d = grad[at, cols]
                df = d * factor[:, cols].astype(F32)
                totals[2 + i] += jnp.sum(d * step_up, axis=0, keepdims=True)
                straight = df if i == 0 else straight + df
                rest = d - df if i == 0 else rest + (d - df)
            dz = straight + pltpu.roll(rest * same[at, :], each - 1, 0)
            totals[0] += jnp.sum(dz * hat, axis=0, keepdims=True)
            totals[1] += jnp.sum(dz, axis=0, keepdims=True)
            dhat = dz * g
            hats[at, cols] = dhat
            following += [carry[2 * row] + dhat, carry[2 * row + 1] + dhat * hat]
        for i, total in enumerate(totals):
            sums[i:i + 1, cols] = total
        return tuple(following)

    zero = jnp.zeros((each, LANES), F32)
    done = lax.fori_loop(0, width // LANES, gather, (zero,) * (2 * rows))
    for row, at in enumerate(spans):
        for ref, value in ((first, done[2 * row]), (second, done[2 * row + 1])):
            ref[at, :] = jnp.broadcast_to(jnp.sum(value, axis=1, keepdims=True) * (1.0 / width), (each, LANES))

    for at in spans:
        def finish(c, _, at=at):
            cols = lanes(c)
            hat = (source[at, cols].astype(F32) - mean[at, :]) * scale[at, :]
            out = residual[at, cols].astype(F32) + scale[at, :] * (hats[at, cols] - first[at, :] - hat * second[at, :])
            for t in targets:
                t[at, cols] = out.astype(t.dtype)
            return 0

        lax.fori_loop(0, width // LANES, finish, 0)
        leave(at)


def channel_kernel(rows, times, *refs):
    (same, factor_out, factor_gate, g, g2, b2, ck, cr, rect_in, middle_in, mean_in, scale_in, fv_in, fk_in, fr_in) = refs[:15]
    n_out = 6
    outs = refs[15:15 + n_out]
    (fv, fk, fr, rect, middle, delta_out, delta_gate, delta_pre, dh, dg, mean, scale, first, second, hats, delta, branch, sums, in_sems, out_sems, row_sems) = refs[15 + n_out:]
    tokens, width = g.shape
    ff = rect.shape[1]
    tile = 512
    chunks = ff // tile
    first_loads = []
    for j in range(chunks):
        span = slice(j * tile, (j + 1) * tile)
        first_loads += [(fv_in.at[span, :], fv.at[span, :]), (rect_in.at[:, span], rect.at[:, span])]
    sums[...] = jnp.zeros_like(sums)
    loads = fetch(first_loads + [(fr_in, fr), (fk_in, fk), (middle_in, middle), (mean_in, mean), (scale_in, scale)], in_sems)
    saves = []
    def save(source, i):
        saves.append(pltpu.make_async_copy(source, outs[i], out_sems.at[i]))
        saves[-1].start()
    def cols_of(j):
        return pl.ds(pl.multiple_of(j * tile, tile), tile)
    if times:
        def scale_tile(j, _):
            cols = lanes(j)
            x = g[:, cols].astype(F32)
            delta_out[:, cols] = (x * factor_out[:, cols].astype(F32)).astype(BF)
            delta_gate[:, cols] = (x * factor_gate[:, cols].astype(F32)).astype(BF)
            return 0
        lax.fori_loop(0, width // LANES, scale_tile, 0)
        left_out, left_gate = delta_out, delta_gate
    else:
        left_out, left_gate = factor_out, factor_gate
    def pre_tile(j, _):
        cols = cols_of(j)
        pltpu.make_async_copy(fv_in.at[cols, :], fv.at[cols, :], in_sems.at[2 * j]).wait()
        pltpu.make_async_copy(rect_in.at[:, cols], rect.at[:, cols], in_sems.at[2 * j + 1]).wait()
        d = dot_nt(left_out[...], fv[cols, :])
        delta_pre[:, cols] = (d * (2.0 * jnp.sqrt(rect[:, cols].astype(F32)))).astype(BF)
        return 0
    lax.fori_loop(0, ff // tile, pre_tile, 0)
    save(delta_pre, 0)
    if times:
        save(delta_out, 4)
        save(delta_gate, 5)
    for c in loads[-5:]:
        c.wait()
    def hidden_tile(j, _):
        cols = cols_of(j)
        dh[:, cols] = dot_nt(delta_pre[...], fk[cols, :])
        dg[:, cols] = dot_nt(left_gate[...], fr[cols, :])
        return 0
    lax.fori_loop(0, width // tile, hidden_tile, 0)
    def leave(at):
        for i, z in ((1, delta), (2, branch)):
            saves.append(pltpu.make_async_copy(z.at[at, :], outs[i].at[at, :], row_sems.at[i - 1, at.start // (tokens // rows)]))
            saves[-1].start()
    norm_backward(middle, mean, scale, same, g2, b2, (ck, cr), (dh, dg), g, (delta, branch), sums, hats, first, second, rows, leave)
    save(sums, 3)
    for c in saves:
        c.wait()

def channel(rows, times, same, factor_out, factor_gate, g, p, rect, middle, mean, scale):
    (g1, b1, fade, bonus, mk, mv, mr, wk, wv, wr, wo, g2, b2, ck, cr, fk, fr, fv) = p
    tokens, width = g.shape
    ff = fk.shape[1]
    vm = pl.BlockSpec(memory_space=pltpu.VMEM)
    hbm = pl.BlockSpec(memory_space=pl.ANY)
    outs = [((tokens, ff), BF), ((tokens, width), F32), ((tokens, width), BF), ((8, width), F32)]
    outs += [((tokens, width), BF)] * 2 if times else [((16, LANES), BF)] * 2
    wide, wide32 = pltpu.VMEM((tokens, width), BF), pltpu.VMEM((tokens, width), F32)
    stat = pltpu.VMEM((tokens, LANES), F32)
    big = pltpu.VMEM((tokens, ff), BF)
    scratch = [pltpu.VMEM((ff, width), BF), pltpu.VMEM((width, ff), BF), pltpu.VMEM((width, width), BF), big, wide32, wide, wide, big, wide32, wide32]
    scratch += [stat] * 4 + [wide32, wide32, wide, pltpu.VMEM((8, width), F32), pltpu.SemaphoreType.DMA((2 * ff // 512 + 5,)), pltpu.SemaphoreType.DMA((6,)), pltpu.SemaphoreType.DMA((2, rows))]
    return pl.pallas_call(
        functools.partial(channel_kernel, rows, times),
        out_shape=tuple(jax.ShapeDtypeStruct(*o) for o in outs),
        in_specs=[vm] * 8 + [hbm] * 7,
        out_specs=(hbm,) * 6,
        scratch_shapes=scratch,
        compiler_params=pltpu.CompilerParams(vmem_limit_bytes=60 << 20),
        cost_estimate=pl.CostEstimate(flops=75000000000, bytes_accessed=217500000, transcendentals=0),
        name="channel",
    )(same, factor_out, factor_gate, g, g2, b2, ck, cr, rect, middle, mean, scale, fv, fk, fr)

def time_kernel(rows, *refs):
    (same_s, same, branch, h, g1, b1, fade, bonus, mk, mv, mr, wo_in, gate_in, ks_in, vs_in, tops_in, bottoms_in, wk_in, wv_in, wr_in, delta_in, mean_in, scale_in) = refs[:23]
    n_out = 5
    outs = refs[23:23 + n_out]
    (wo, gate, ks, vs, wk, wv, wr, delta, dm, gs, ys, tops, bottoms, dks, dvs, dk, dv, dr, ik, iv, ir, mean, scale, first, second, hats, state, sums, slab, in_sems, out_sems, row_sems) = refs[23 + n_out:]
    tokens, width = h.shape
    each = tokens // rows
    parts = width // LANES
    tile = 512
    sums[...] = jnp.zeros_like(sums)
    loads = fetch([(wo_in, wo), (gate_in, gate), (ks_in, ks), (vs_in, vs), (tops_in, tops), (bottoms_in, bottoms), (wk_in, wk), (wv_in, wv), (wr_in, wr), (delta_in, delta), (mean_in, mean), (scale_in, scale)], in_sems)
    saves = []
    def save(source, i):
        saves.append(pltpu.make_async_copy(source, outs[i], out_sems.at[i]))
        saves[-1].start()
    def cols_of(j):
        return pl.ds(pl.multiple_of(j * tile, tile), tile)
    loads[0].wait()
    loads[1].wait()
    def mixed_tile(j, _):
        cols = cols_of(j)
        d = dot_nt(branch[...], wo[cols, :])
        dm[:, cols] = d
        e = d * gate[:, cols]
        for row in range(rows):
            for c in range(tile // LANES):
                gs[pl.ds(row * each * parts + j * (tile // LANES) + c, each, stride=parts), :] = e[row * each:(row + 1) * each, c * LANES:(c + 1) * LANES]
        return 0
    lax.fori_loop(0, width // tile, mixed_tile, 0)
    for i in (2, 3, 4, 5):
        loads[i].wait()
    rate = jnp.exp(slabs(fade, slab))
    decay = jnp.exp(-rate)
    extra = slabs(bonus, slab)
    zero = jnp.zeros(decay.shape, F32)
    def back(i, carry):
        t = each - 1 - i
        dw, du = carry[:2]
        following = []
        for row in range(rows):
            here = pl.ds(pl.multiple_of((row * each + t) * parts, parts), parts)
            a, b = carry[2 + 2 * row], carry[3 + 2 * row]
            k, v = ks[here, :], vs[here, :]
            ek, now = jnp.exp(k), jnp.exp(extra + k)
            inverse = 1.0 / (bottoms[here, :] + now)
            y = (tops[here, :] + now * v) * inverse
            ys[here, :] = y
            ga = gs[here, :] * inverse
            gb = -ga * y
            q = now * (v * ga + gb)
            dks[here, :] = ek * (v * a + b) + q
            dvs[here, :] = ek * a + now * ga
            du = du + q
            dw = dw + (a * tops[here, :] + b * bottoms[here, :])
            m = same_s[row, t]
            following += [(ga + decay * a) * m, (gb + decay * b) * m]
        return (dw, du, *following)
    done = lax.fori_loop(0, each, back, (zero,) * (2 + 2 * rows), unroll=4)
    dfade = -done[0] * decay * rate
    for c in range(parts):
        sums[5:6, c * LANES:(c + 1) * LANES] = dfade[c:c + 1, :]
        sums[6:7, c * LANES:(c + 1) * LANES] = done[1][c:c + 1, :]
    for row in range(rows):
        def out_step(c, _, row=row):
            span = slice(row * each, (row + 1) * each)
            cols = lanes(c)
            at = pl.ds(row * each * parts + c, each, stride=parts)
            dk[span, cols] = dks[at, :].astype(BF)
            dv[span, cols] = dvs[at, :].astype(BF)
            s = gate[span, cols]
            dr[span, cols] = (dm[span, cols] * ys[at, :] * s * (1.0 - s)).astype(BF)
            return 0
        lax.fori_loop(0, parts, out_step, 0)
    for i, z in enumerate((dk, dv, dr)):
        save(z, i)
    for i in (6, 7, 8):
        loads[i].wait()
    def in_tile(j, _):
        cols = cols_of(j)
        ik[:, cols] = dot_nt(dk[...], wk[cols, :])
        iv[:, cols] = dot_nt(dv[...], wv[cols, :])
        ir[:, cols] = dot_nt(dr[...], wr[cols, :])
        return 0
    lax.fori_loop(0, width // tile, in_tile, 0)
    for c in loads[9:]:
        c.wait()
    def leave(at):
        saves.append(pltpu.make_async_copy(state.at[at, :], outs[3].at[at, :], row_sems.at[at.start // each]))
        saves[-1].start()
    norm_backward(h, mean, scale, same, g1, b1, (mk, mv, mr), (ik, iv, ir), delta, (state,), sums, hats, first, second, rows, leave)
    save(sums, 4)
    for c in saves:
        c.wait()

def time_mix(rows, dtype, same_s, same, branch, delta, h, p, gate, ks, vs, tops, bottoms, mean, scale):
    (g1, b1, fade, bonus, mk, mv, mr, wk, wv, wr, wo, g2, b2, ck, cr, fk, fr, fv) = p
    tokens, width = h.shape
    vm = pl.BlockSpec(memory_space=pltpu.VMEM)
    hbm = pl.BlockSpec(memory_space=pl.ANY)
    outs = [((tokens, width), BF)] * 3 + [((tokens, width), dtype), ((8, width), F32)]
    wide, wide32 = pltpu.VMEM((tokens, width), BF), pltpu.VMEM((tokens, width), F32)
    step32 = pltpu.VMEM(ks.shape, F32)
    stat = pltpu.VMEM((tokens, LANES), F32)
    square = pltpu.VMEM((width, width), BF)
    scratch = [square, wide32, step32, step32, square, square, square, wide32, wide32] + [step32] * 6 + [wide] * 3 + [wide32] * 3 + [stat] * 4 + [wide32]
    scratch += [pltpu.VMEM((tokens, width), dtype), pltpu.VMEM((8, width), F32), pltpu.VMEM((width // LANES, LANES), F32), pltpu.SemaphoreType.DMA((12,)), pltpu.SemaphoreType.DMA((5,)), pltpu.SemaphoreType.DMA((rows,))]
    return pl.pallas_call(
        functools.partial(time_kernel, rows),
        out_shape=tuple(jax.ShapeDtypeStruct(*o) for o in outs),
        in_specs=[pl.BlockSpec(memory_space=pltpu.SMEM)] + [vm] * 10 + [hbm] * 12,
        out_specs=(hbm,) * 5,
        scratch_shapes=scratch,
        compiler_params=pltpu.CompilerParams(vmem_limit_bytes=60 << 20),
        cost_estimate=pl.CostEstimate(flops=87000000000, bytes_accessed=252300000, transcendentals=0),
        name="time_mix",
    )(same_s, same, branch, h, g1, b1, fade, bonus, mk, mv, mr, wo, gate, ks, vs, tops, bottoms, wk, wv, wr, delta, mean, scale)


UNIT = 1024


def starts(parts):
    return [sum(c for c, _ in parts[:i]) for i in range(len(parts))]


def terms_kernel(count, parts, shapes, with_sums, with_factor, *refs):
    bits, refs = refs[0], refs[1:]
    if with_factor:
        factor, refs = refs[0], refs[1:]
    n, np_ = len(shapes), len(parts)
    left_in, right_in, refs = refs[:n], refs[n:2 * n], refs[2 * n:]
    if with_sums:
        early, late, *refs = refs
    outs, refs = refs[:2 * np_], refs[2 * np_:]
    lefts, rights, refs = refs[:n], refs[n:2 * n], refs[2 * n:]
    bufs, (in_sems, out_sems) = refs[:np_], refs[np_:]
    sends, keeps = outs[::2], outs[1::2]
    tile = 512
    columns = starts(parts)

    def place(order, d):
        bit = [(d >> b) & 1 if isinstance(d, int) else lax.rem(lax.div(d, 1 << b), 2) for b in order]
        return bit[0] ^ bits[order[0]], bit[1] * 4 + bit[2] * 2 + bit[3]

    chunk_base = [sum(kin // tile for kin, _ in shapes[:m]) for m in range(n)]

    def load(m, j):
        cols = pl.ds(pl.multiple_of(j * tile, tile), tile)
        return pltpu.make_async_copy(left_in[m].at[:, cols], lefts[m].at[:, cols], in_sems.at[chunk_base[m] + j])

    right_base = [chunk_base[-1] + shapes[-1][0] // tile + sum(width // UNIT for _, width in shapes[:m]) for m in range(n)]

    def load_right(m, q):
        cols = slice(q * UNIT, (q + 1) * UNIT)
        return pltpu.make_async_copy(right_in[m].at[:, cols], rights[m].at[:, cols], in_sems.at[right_base[m] + q])

    for m, (kin, width) in enumerate(shapes):
        load_right(m, 0).start()
        for j in range(kin // tile):
            load(m, j).start()
        for q in range(1, width // UNIT):
            load_right(m, q).start()
    waits = []
    base = 0
    blocks = 0
    for m, ((kin, width), left, right) in enumerate(zip(shapes, lefts, rights)):
        rows = kin // count
        per = tile // rows
        for q in range(width // UNIT):
            load_right(m, q).wait()
            if with_factor:
                right[...] = (right[...].astype(F32) * factor[...].astype(F32)).astype(BF)

            def step(j, _, m=m, q=q, left=left, right=right, rows=rows, per=per, base=base):
                if q == 0:
                    load(m, j).wait()
                lhs = left[:, pl.ds(pl.multiple_of(j * tile, tile), tile)]
                for i, (cols, order) in enumerate(parts):
                    at = q * UNIT + columns[i]
                    res = lax.dot_general(lhs, right[:, at:at + cols], (((0,), (0,)), ((), ())), preferred_element_type=F32).astype(BF)
                    for s in range(per):
                        relative, index = place(order, j * per + s)
                        bufs[i][relative, index, base:base + rows, :] = res[s * rows:(s + 1) * rows]
                        if rows >= 256:
                            source = bufs[i].at[relative, index]
                            for r, target in ((1, sends[i]), (0, keeps[i])):
                                @pl.when(relative == r)
                                def _(source=source, target=target, index=index, i=i):
                                    pltpu.make_async_copy(source, target.at[index], out_sems.at[i, j * per + s]).start()
                return 0

            lax.fori_loop(0, kin // tile, step, 0)
            for i in range(np_):
                if rows >= 256:
                    for j in range(count):
                        waits.append(pltpu.make_async_copy(bufs[i].at[0, 0], keeps[i].at[0], out_sems.at[i, j]))
                else:
                    for r, target in ((1, sends[i]), (0, keeps[i])):
                        c = pltpu.make_async_copy(bufs[i].at[r, :, base:base + rows, :], target.at[:, base:base + rows, :], out_sems.at[i, 2 * blocks + r])
                        c.start()
                        waits.append(c)
            base += rows
            blocks += 1
    if with_sums:
        share = early.shape[1] // count
        both = jnp.concatenate([early[...], late[...]], axis=0)
        for buf in bufs:
            buf[:, :, base:base + 16, :] = jnp.zeros(buf.shape[:2] + (16, buf.shape[3]), BF)
        for d in range(count):
            column = d * share // LANES * LANES
            piece = both[:, column:column + LANES]
            if d * share - column:
                piece = pltpu.roll(piece, LANES - (d * share - column), 1)
            relative, index = place(parts[0][1], d)
            bufs[0][relative, index, base:base + 16, 0:LANES] = piece.astype(BF)
        for i in range(np_):
            for r, target in ((1, sends[i]), (0, keeps[i])):
                c = pltpu.make_async_copy(bufs[i].at[r, :, base:base + 16, :], target.at[:, base:base + 16, :], out_sems.at[i, 2 * blocks + r])
                c.start()
                waits.append(c)
    for c in waits:
        c.wait()


def terms(bits, parts, pairs, sums=(), factor=None):
    count = 16
    lefts, rights = zip(*pairs)
    shapes = tuple((a.shape[1], b.shape[1]) for a, b in pairs)
    tokens = lefts[0].shape[0]
    rows = sum(kin // count * (width // UNIT) for kin, width in shapes) + (16 if sums else 0)
    outs, bufs = [], []
    for cols, _ in parts:
        outs += [jax.ShapeDtypeStruct((count // 2, rows, cols), BF)] * 2
        bufs.append(pltpu.VMEM((2, count // 2, rows, cols), BF))
    flops = sum(2 * tokens * kin * width for kin, width in shapes)
    result = pl.pallas_call(
        functools.partial(terms_kernel, count, parts, shapes, bool(sums), factor is not None),
        out_shape=tuple(outs),
        in_specs=[SM] + [VM] * (factor is not None) + [HBM] * (2 * len(shapes)) + [VM] * len(sums),
        out_specs=(HBM,) * len(outs),
        scratch_shapes=[pltpu.VMEM(x.shape, BF) for x in (*lefts, *rights)]
        + bufs + [pltpu.SemaphoreType.DMA((sum(kin // 512 + width // UNIT for kin, width in shapes),)), pltpu.SemaphoreType.DMA((len(parts), 16))],
        compiler_params=pltpu.CompilerParams(vmem_limit_bytes=56 << 20),
        cost_estimate=pl.CostEstimate(flops=39000000000, bytes_accessed=113100000, transcendentals=0),
        name="terms",
    )(bits, *(() if factor is None else (factor,)), *lefts, *rights, *sums)
    return list(zip(result[::2], result[1::2]))


def swap(block, bit):
    count = lax.axis_size("dp")
    return lax.ppermute(block, "dp", [(i, i ^ (1 << bit)) for i in range(count)])


def summed(kept, came, dtype=BF):
    return (kept.astype(F32) + came.astype(F32)).astype(dtype)


def advance_kernel(bits, kept_go, came_go, kept_stay, came_stay, send, keep):
    send[...] = summed(kept_go[...], came_go[...])
    keep[...] = summed(kept_stay[...], came_stay[...])


def advance(bits, kept, came, bit):
    lead, rows, cols = kept.shape
    half = lead // 2
    block = rows
    go = pl.BlockSpec((1, block, cols), lambda g, i, b: ((1 - b[bit]) * half + g, i, 0))
    stay = pl.BlockSpec((1, block, cols), lambda g, i, b: (b[bit] * half + g, i, 0))
    out = pl.BlockSpec((1, block, cols), lambda g, i, b: (g, i, 0))
    return pl.pallas_call(
        advance_kernel,
        out_shape=(jax.ShapeDtypeStruct((half, rows, cols), BF),) * 2,
        grid_spec=pltpu.PrefetchScalarGridSpec(
            num_scalar_prefetch=1, grid=(half, rows // block), in_specs=[go, go, stay, stay], out_specs=(out, out)
        ),
        compiler_params=pltpu.CompilerParams(vmem_limit_bytes=30 << 20),
        cost_estimate=pl.CostEstimate(flops=9000000000, bytes_accessed=26100000, transcendentals=0),
        name="advance",
    )(bits, kept, came, kept, came)


def final_kernel(pieces, parts, *refs):
    n = len(parts)
    ins, outs = refs[:2 * n], refs[2 * n:]
    for (row, rows, blocks, columns), out in zip(pieces, outs):
        for q in range(blocks):
            span = slice(row + q * rows, row + (q + 1) * rows)
            if columns < UNIT:
                out[...] = summed(ins[0][0, span, 0:LANES], ins[1][0, span, 0:LANES], F32)[:, :columns]
                continue
            for i, at in enumerate(starts(parts)):
                out[:, q * UNIT + at:q * UNIT + at + parts[i][0]] = summed(ins[2 * i][0, span, :], ins[2 * i + 1][0, span, :], F32)


def final(parts, pieces, arrays):
    size = sum(a.size for a in arrays)
    return pl.pallas_call(
        functools.partial(final_kernel, pieces, parts),
        out_shape=tuple(jax.ShapeDtypeStruct((rows, blocks * columns), F32) for row, rows, blocks, columns in pieces),
        in_specs=[VM] * len(arrays),
        out_specs=(VM,) * len(pieces),
        compiler_params=pltpu.CompilerParams(vmem_limit_bytes=40 << 20),
        cost_estimate=pl.CostEstimate(flops=4500000000, bytes_accessed=13050000, transcendentals=0),
        name="final",
    )(*arrays)


def after(value, *earlier):
    return lax.optimization_barrier((value, earlier))[0]


def values_kernel(orders, offset, bits, own, *refs):
    ins, refs = refs[:6], refs[6:]
    outs, refs = refs[:4], refs[4:]
    held, mine_d, (bufs, in_sems, out_sems) = refs[:6], refs[6], refs[7:]
    width = mine_d.shape[1]
    loads = [pltpu.make_async_copy(own, mine_d, in_sems.at[0])]
    for i in (0, 1):
        kept, came, delta = ins[3 * i:3 * i + 3]
        loads += [
            pltpu.make_async_copy(kept, held[3 * i], in_sems.at[3 * i + 1]),
            pltpu.make_async_copy(came.at[:, 0:width], held[3 * i + 1], in_sems.at[3 * i + 2]),
            pltpu.make_async_copy(delta.at[:, offset:offset + width], held[3 * i + 2], in_sems.at[3 * i + 3]),
        ]
    for c in loads:
        c.start()
    loads[0].wait()
    tile = 512
    waits = []

    def dot_tn(left, right):
        return lax.dot_general(left, right, (((0,), (0,)), ((), ())), preferred_element_type=F32)

    for i in (0, 1):
        for c in loads[3 * i + 1:3 * i + 4]:
            c.wait()
        kept, came, delta = held[3 * i:3 * i + 3]

        def step(n, _, i=i, kept=kept, came=came, delta=delta):
            j, q = n // 2, n % 2
            rows = pl.ds(pl.multiple_of(j * tile, tile), tile)
            cols = pl.ds(pl.multiple_of(q * tile, tile), tile)
            res = (dot_tn(kept[:, rows], mine_d[:, cols]) + dot_tn(came[:, rows], delta[:, cols])).astype(BF)
            for s in (0, 1):
                bufs[i, j, s, :, cols] = res[s * 256:(s + 1) * 256]
            return 0

        lax.fori_loop(0, 4, step, 0)
        for j in (0, 1):
            for r, target in ((1, outs[2 * i]), (0, outs[2 * i + 1])):
                copy = pltpu.make_async_copy(bufs.at[i, j], target, out_sems.at[i, j])
                @pl.when((j ^ bits[orders[i][1]]) == r)
                def _(copy=copy):
                    copy.start()
            waits.append(copy)
    for c in waits:
        c.wait()


def values(bits, orders, offset, own, parts):
    tokens, width = own.shape
    out = jax.ShapeDtypeStruct((2, 256, width), BF)
    wide = pltpu.VMEM((tokens, width), BF)
    result = pl.pallas_call(
        functools.partial(values_kernel, orders, offset),
        out_shape=(out,) * 4,
        in_specs=[SM] + [HBM] * 7,
        out_specs=(HBM,) * 4,
        scratch_shapes=[wide] * 7 + [pltpu.VMEM((2, 2, 2, 256, width), BF), pltpu.SemaphoreType.DMA((7,)), pltpu.SemaphoreType.DMA((2, 2))],
        compiler_params=pltpu.CompilerParams(vmem_limit_bytes=56 << 20),
        cost_estimate=pl.CostEstimate(flops=30000000000, bytes_accessed=87000000, transcendentals=0),
        name="values",
    )(bits, own, *parts[0], *parts[1])
    return list(zip(result[::2], result[1::2]))


def cross_kernel(bits, kept_a, came_a, kept_b, came_b, send, keep):
    low, high = summed(kept_a[...], came_a[...]), summed(kept_b[...], came_b[...])

    @pl.when(bits[3] == 0)
    def _():
        send[...] = high
        keep[...] = low

    @pl.when(bits[3] == 1)
    def _():
        send[...] = low
        keep[...] = high


def cross(bits, arrays):
    out = jax.ShapeDtypeStruct(arrays[0].shape, BF)
    return pl.pallas_call(
        cross_kernel,
        out_shape=(out, out),
        in_specs=[SM] + [VM] * 4,
        out_specs=(VM, VM),
        compiler_params=pltpu.CompilerParams(vmem_limit_bytes=30 << 20),
        cost_estimate=pl.CostEstimate(flops=4500000000, bytes_accessed=13050000, transcendentals=0),
        name="cross",
    )(bits, *arrays)


class Line:
    def __init__(self, bits, plan, pieces):
        self.bits, self.plan, self.pieces, self.token, self.flight, self.sums = bits, plan, pieces, None, {}, {}

    def tie(self, value):
        return value if self.token is None else after(value, self.token)

    def open(self, group, pairs, sums=(), factor=None):
        pairs = ((self.tie(pairs[0][0]), pairs[0][1]),) + tuple(pairs[1:])
        found = terms(self.bits, self.plan[group], pairs, sums, factor)
        self.token = found
        for i, (send, keep) in enumerate(found):
            self.flight[group, i] = keep, swap(send, self.plan[group][i][1][0])

    def join(self, offset, own, parts):
        orders = tuple(order for _, order in self.plan["a"])
        found = values(self.bits, orders, offset, self.tie(own), parts)
        self.token = found
        for i, (send, keep) in enumerate(found):
            self.flight["a", i] = keep, swap(send, orders[i][1])

    def serve(self, steps):
        for group, i, stage in steps:
            parts = self.plan[group]
            if group == "a" and stage == 3:
                send, keep = cross(self.bits, self.tie(self.flight.pop(("a", 0)) + self.flight.pop(("a", 1))))
                self.token = send, keep
                self.flight["a", 0] = keep, swap(send, 3)
            elif group == "a" and stage == 4:
                self.sums["a"] = final(((UNIT, None),), self.pieces["a"], self.tie(list(self.flight.pop(("a", 0)))))
                self.token = self.sums["a"][0]
            elif stage < 4:
                kept, came = self.tie(self.flight[group, i])
                send, keep = advance(self.bits, kept, came, parts[i][1][stage])
                self.token = send, keep
                self.flight[group, i] = keep, swap(send, parts[i][1][stage])
            else:
                self.sums[group, i] = self.flight.pop((group, i))
                if all((group, k) in self.sums for k in range(len(parts))):
                    arrays = [a for k in range(len(parts)) for a in self.sums[group, k]]
                    arrays[0] = self.tie(arrays[0])
                    self.sums[group] = final(parts, self.pieces[group], arrays)
                    self.token = self.sums[group][0]


def halving(left, right=None):
    count = lax.axis_size("dp")
    bits = count.bit_length() - 1
    me = lax.axis_index("dp")
    if right is not None:
        left = lax.dot_general(left, right, (((0,), (0,)), ((), ())), preferred_element_type=F32).astype(BF)
    current = left.reshape((2,) * bits + (left.shape[0] // count, left.shape[1]))
    for bit in range(bits):
        axis = bits - 1 - bit
        mine = (me >> bit) & 1
        send = lax.dynamic_index_in_dim(current, 1 - mine, axis, keepdims=False)
        keep = lax.dynamic_index_in_dim(current, mine, axis, keepdims=False)
        current = summed(keep, swap(send, bit), BF if bit + 1 < bits else F32)
    return current


def unwritten(function, *args):
    shapes, tree = jax.tree.flatten(jax.eval_shape(function, *args))
    outs = pl.pallas_call(
        lambda *refs: None, out_shape=tuple(shapes), out_specs=(HBM,) * len(shapes), name="unwritten"
    )()
    return jax.tree.unflatten(tree, outs)


VECTORS = (0, 1, 5, 6, 2, 3, 4, 8, 9, 10, 11)
PARTS_0 = dict(
    a=((512, (0, 1, 2, 3)), (512, (2, 1, 0, 3))),
    b=((512, (2, 1, 0, 3)), (512, (0, 1, 2, 3))),
    e=((512, (1, 0, 2, 3)), (512, (0, 2, 1, 3))),
)
PARTS_1 = dict(
    a=((512, (1, 0, 2, 3)), (512, (2, 0, 1, 3))),
    b=((512, (1, 0, 2, 3)), (512, (2, 0, 1, 3))),
    e=((512, (1, 0, 2, 3)), (512, (2, 0, 1, 3))),
)
ORDER_1 = ('b', 'a', 'e')
STEPS_0 = (('a', 0, 2), ('a', 1, 2), ('b', 1, 1), ('b', 0, 1), ('e', 0, 1), ('b', 1, 2), ('e', 1, 1), ('a', 0, 3), ('b', 1, 3), ('b', 0, 2), ('e', 1, 2), ('e', 0, 2), ('a', 0, 4), ('b', 0, 3), ('b', 1, 4), ('e', 0, 3), ('e', 1, 3), ('b', 0, 4), ('e', 0, 4), ('e', 1, 4))
STEPS_1 = (('a', 0, 2), ('a', 1, 2), ('b', 0, 1), ('b', 1, 1), ('e', 0, 1), ('b', 0, 2), ('e', 1, 1), ('a', 0, 3), ('b', 0, 3), ('b', 1, 2), ('a', 0, 4), ('b', 0, 4), ('e', 0, 2), ('b', 1, 3), ('e', 0, 3), ('e', 1, 2), ('b', 1, 4), ('e', 1, 3), ('e', 0, 4), ('e', 1, 4))


def local(entry_pair, labels, *params):
    count = lax.axis_size("dp")
    section = lax.axis_index("section")
    rows, each, width = entry_pair.shape[1:]
    own = entry_pair.reshape(rows * each, width)
    share = width // count
    p = [e if e.ndim == 2 else e[0] for e in params]
    ff = p[15].shape[1]
    first = jnp.zeros((rows, 1), F32)
    same_s = jnp.concatenate([first, (labels[:, 1:] == labels[:, :-1]).astype(F32)], axis=1)
    same = jnp.broadcast_to(same_s.reshape(rows * each, 1), (rows * each, LANES))
    fast = count == 16 and width == UNIT
    me = lax.axis_index("dp")
    bits = jnp.stack([(me >> i) & 1 for i in range(4)])
    wide = ff // width
    pieces = dict(
        a=((0, ff // count, 1, width),),
        b=((0, share, wide, width), (share * wide, share, 1, width), (share * (wide + 1), share, 1, width)),
        e=tuple((i * share, share, 1, width) for i in range(3)) + tuple((3 * share + i, 1, 1, share) for i in VECTORS),
    )

    def plain_rest(pairs, sums):
        together = jnp.concatenate(sums).astype(BF).reshape(16, count, share).transpose(1, 0, 2).reshape(count * 16, share)
        vectors = halving(together)
        return tuple(halving(*pair) for pair in pairs) + tuple(vectors[i:i + 1] for i in VECTORS)

    def orders(plan):
        return tuple(order for _, order in plan["a"]) if fast else None

    def start():
        return forward(rows, False, same_s, same, own, p, own, bits, orders(PARTS_0))

    def middle_part(received):
        kept = forward(rows, True, same_s, same, received, p, own, bits, orders(PARTS_1))
        (key_in, value_in, recept_in, ks, vs, gate, tops, bottoms, mixed, middle, hidden_in, gate_in, act, result, delta_out, delta_gate, mean, scale, mean2, scale2, *acts) = kept
        begun = act, delta_out
        if fast:
            came = [swap(acts[2 * i], PARTS_1["a"][i][1][0]) for i in (0, 1)]
            begun = delta_out, [(acts[2 * i + 1], came[i]) for i in (0, 1)]
        g = after(own, acts[0]) if fast else own
        delta_pre, delta, branch, late, _, _ = channel(rows, False, same, delta_out, delta_gate, g, p, act, middle, mean2, scale2)
        dk, dv, dr, state, early = time_mix(rows, BF, same_s, same, branch, delta, received, p, gate, ks, vs, tops, bottoms, mean, scale)
        key_pairs = ((hidden_in, delta_pre), (gate_in, delta_gate), (mixed, branch))
        return state, result, begun, (early, late), key_pairs, ((key_in, dk), (value_in, dv), (recept_in, dr))

    def end_first(received, kept, acts_came):
        (key_in, value_in, recept_in, ks, vs, gate, tops, bottoms, mixed, middle, hidden_in, gate_in, act, result, factor_out, factor_gate, mean, scale, mean2, scale2, *acts) = kept
        line = Line(bits, PARTS_0, pieces)
        if fast:
            own_delta = (received.astype(F32) * factor_out.astype(F32)).astype(BF)
            came = [swap(own_delta, PARTS_0["a"][i][1][0]) for i in (0, 1)]
            line.token = own_delta
        g = line.tie(received)
        delta_pre, delta, branch, late, delta_out, delta_gate = channel(rows, True, same, factor_out, factor_gate, g, p, act, middle, mean2, scale2)
        key_pairs = ((hidden_in, delta_pre), (gate_in, delta_gate), (mixed, branch))
        line.token = branch
        if fast:
            line.open("b", key_pairs)
            line.join(0, own_delta, [(acts[2 * i + 1], acts_came[i], came[i]) for i in (0, 1)])
        dk, dv, dr, state, early = time_mix(rows, F32, same_s, same, line.tie(branch), delta, own, p, gate, ks, vs, tops, bottoms, mean, scale)
        rest_pairs = ((key_in, dk), (value_in, dv), (recept_in, dr))
        if not fast:
            return state, (halving(act, delta_out),), tuple(halving(*pair) for pair in key_pairs), plain_rest(rest_pairs, (early, late))
        line.token = state
        line.open("e", rest_pairs, (early, late))
        line.serve(STEPS_0)
        return state, line.sums["a"], line.sums["b"], line.sums["e"]

    def end_second(result, begun, sums, key_pairs, rest_pairs):
        if not fast:
            return result.astype(F32), (halving(*begun),), tuple(halving(*pair) for pair in key_pairs), plain_rest(rest_pairs, sums)
        line = Line(bits, PARTS_1, pieces)
        for name in ORDER_1:
            if name == "a":
                line.join(width, begun[0], [(kept, came, came) for kept, came in begun[1]])
            elif name == "b":
                line.open("b", key_pairs)
            else:
                line.open("e", rest_pairs, sums)
        line.serve(STEPS_1)
        return result.astype(F32), line.sums["a"], line.sums["b"], line.sums["e"]

    def swap_first(block, bit):
        return lax.ppermute(block, ("section", "dp"), [(i, i ^ (1 << bit)) for i in range(count)])

    kept = lax.cond(section == 0, start, lambda: unwritten(start))
    received = lax.ppermute(kept[13], "section", [(0, 1)])
    acts_came = [swap_first(kept[20 + 2 * i], PARTS_0["a"][i][1][0]) for i in (0, 1)] if fast else []
    delta, *pending = lax.cond(section == 1, middle_part, lambda r: unwritten(middle_part, r), received)
    received = lax.ppermute(delta, "section", [(1, 0)])
    ends, (value_sum,), (key_sum, gate_sum, exit_sum), rest = lax.cond(
        section == 0, lambda r, k, a, q: end_first(r, k, a), lambda r, k, a, q: end_second(*q), received, kept, acts_came, pending
    )
    ends = ends.reshape(rows, each, width)
    everything = (ends, *(z[0] for z in rest[3:10]), *rest[:3], exit_sum, *(z[0] for z in rest[10:14]), key_sum, gate_sum, value_sum)
    return tuple(e[None] for e in everything)


def solution(mesh):
    vec, mat = P("section", None), P("section", None, None)
    in_specs = (P("section", "dp", None, None), P("dp", None)) + (vec,) * 7 + (mat,) * 4 + (vec,) * 4 + (mat,) * 3
    vec, mat = P("section", "dp"), P("section", "dp", None)
    out_specs = (P("section", "dp", None, None),) + (vec,) * 7 + (mat,) * 4 + (vec,) * 4 + (mat,) * 3
    return jax.shard_map(local, mesh=mesh, in_specs=in_specs, out_specs=out_specs, check_vma=False)
```
